128 devices in a mesh: seq: 16 (over y, x_hi, core), grp: 8 (over z, x_lo).
Axes of the slice: x: 4 (x_hi: 2, x_lo: 2; x = x_hi * 2 + x_lo), y: 4, z: 4, core: 2. Of those that a mesh axis runs over, the one named last changes fastest.
Arguments:
- byte_ids: int32 [3072, 8], P('seq'), may hold values from 0 to 255
- patch_order: int32 [3072], P('seq'), may hold values from 0 to 3071, as said below
- query_rows: bfloat16 [3072, 8192], P('seq', 'grp'), may hold values from -25 to 25
- key_rows: bfloat16 [3072, 8192], P('seq', 'grp'), may hold values from -25 to 25
- value_rows: bfloat16 [3072, 8192], P('seq', 'grp'), may hold values from -6 to 6
- byte_embed: bfloat16 [256, 1024], replicated, may hold values from -6.5 to 6.5
- norm_gain: float32 [1024], replicated, may hold values from 0.25 to 1.75
- w_up: bfloat16 [1024, 4096], replicated, may hold values from -0.1875 to 0.1875
- w_down: bfloat16 [4096, 1024], replicated, may hold values from -0.09375 to 0.09375
- vocab_head: bfloat16 [1024, 256], replicated, may hold values from -12 to 12
Outputs:
- byte_loss: float32 [3072, 8], P(('seq', 'grp'))
- query_grad: bfloat16 [3072, 8192], P('seq', 'grp')
- key_grad: bfloat16 [3072, 8192], P('seq', 'grp')
- value_grad: bfloat16 [3072, 8192], P('seq', 'grp')
The draws below stay inside these ranges and needn't reach their ends.
Inputs may be any that keep to these rules, and one draw needn't show every extreme that they name: `patch_order`: each aligned block of 192 entries is a permutation of that block's own indices.
All inputs are finite; a program needn't handle non-finite values.
Results may differ from the reference program's by a relative error of at most 0.028.
Values may be sent and summed in bfloat16 or wider, within the bound.
No kernel may reach another device: no remote copies, remote signals or barrier semaphores. Data moves between devices by JAX's collectives and lax.ppermute only.
A program may use at most 192 MiB of HBM per device.

```python
import math
import jax
import jax.numpy as jnp
from jax import lax

DG = 8192
DL = 1024
FFL = 4096
VOCAB = 256
HEAD = 128
PATCH = 8
P_DEV = 192
PATCHES = 3072


def drawn_rows(key, which):
    base = jnp.clip(jax.random.normal(jax.random.fold_in(key, 101 + which), (PATCHES, DG), jnp.float32), -4.0, 4.0)
    return (1.7 * base).astype(jnp.bfloat16)


def draw_query_rows(key, part):
    return drawn_rows(key, 0)


def draw_key_rows(key, part):
    return drawn_rows(key, 1)


def draw_patch_order(key, part):
    block_count = PATCHES // P_DEV
    keys = jax.random.split(jax.random.fold_in(key, 31), block_count)
    orders = jax.vmap(lambda single: jax.random.permutation(single, P_DEV))(keys)
    offsets = (jnp.arange(block_count, dtype=jnp.int32) * P_DEV)[:, None]
    return (orders.astype(jnp.int32) + offsets).reshape(PATCHES).astype(jnp.int32)


def draw_byte_embed(key, part):
    entries = jnp.clip(jax.random.normal(jax.random.fold_in(key, 301), (VOCAB, DL), jnp.float32), -4.0, 4.0)
    factor = jnp.exp(jax.random.uniform(jax.random.fold_in(key, 303), (VOCAB, 1), jnp.float32, 0.0, math.log(10.0)))
    return (0.1 * factor * entries).astype(jnp.bfloat16)


def draw_vocab_head(key, part):
    entries = jnp.clip(jax.random.normal(jax.random.fold_in(key, 401), (DL, VOCAB), jnp.float32), -4.0, 4.0) * (3.0 / math.sqrt(DL))
    return jnp.clip(entries, -11.5, 11.5).astype(jnp.bfloat16)


def place_ends(array, key, smallest, top_value):
    longest = array.shape.index(max(array.shape))
    spots = []
    for shift in (0, 1):
        where = [jax.random.randint(jax.random.fold_in(key, axis), (), 0, length) for axis, length in enumerate(array.shape)]
        where[longest] = (where[longest] + shift) % array.shape[longest]
        spots.append(tuple(where))
    return array.at[spots[0]].set(smallest).at[spots[1]].set(top_value)


def level_of(key, extent, shards, smallest, top_value):
    level = 1.0
    for axis_at, blocks in shards:
        draws = jax.random.uniform(jax.random.fold_in(jax.random.fold_in(key, 6), axis_at), (blocks,), jnp.float32, smallest / len(shards), top_value / len(shards))
        level = level * jnp.repeat(jnp.exp(draws), extent[axis_at] // blocks).reshape((-1,) + (1,) * (len(extent) - 1 - axis_at))
    return level


def centred(own_key, dims, scale, reach, pieces=(), kind=jnp.bfloat16):
    values = jax.random.normal(own_key, dims, jnp.float32) * scale
    if len(pieces) > 0:
        values = level_of(own_key, dims, pieces, -0.22, 0.18) * values
    return jnp.clip(values, min=-reach, max=reach).astype(kind)


def setup_inputs(seed: int = 0) -> dict:
    splits = jax.random.split(jax.random.key(seed), 11)
    byte_ids = place_ends(jax.random.randint(splits[0], (PATCHES, PATCH), 0, VOCAB), jax.random.fold_in(splits[0], 1), 0, VOCAB - 1).astype(jnp.int32)
    patch_order = draw_patch_order(jax.random.fold_in(splits[10], 71), 0)
    query_rows = draw_query_rows(jax.random.fold_in(splits[10], 71), 0)
    key_rows = draw_key_rows(jax.random.fold_in(splits[10], 71), 0)
    value_rows = centred(splits[4], (PATCHES, DG), 1.0, 6.0, ((0, 16), (1, 8)))
    byte_embed = draw_byte_embed(jax.random.fold_in(splits[10], 71), 0)
    norm_gain = jnp.clip(1.0 + 0.15 * jax.random.normal(splits[6], (DL,), jnp.float32), 0.25, 1.75)
    w_up = centred(splits[7], (DL, FFL), DL ** -0.5, 0.1875)
    w_down = centred(splits[8], (FFL, DL), FFL ** -0.5, 0.09375)
    vocab_head = draw_vocab_head(jax.random.fold_in(splits[10], 71), 0)
    return dict(byte_ids=byte_ids, patch_order=patch_order, query_rows=query_rows, key_rows=key_rows, value_rows=value_rows, byte_embed=byte_embed, norm_gain=norm_gain, w_up=w_up, w_down=w_down, vocab_head=vocab_head)


EPSILON = 1e-05

def local_model(context, byte_ids, byte_embed, norm_gain, w_up, w_down, vocab_head):
    patch_count = context.shape[0]
    model_width = byte_embed.shape[1]
    vocab_size = vocab_head.shape[1]
    hidden_in = context.astype(jnp.float32).reshape(patch_count * PATCH, model_width)
    previous = jnp.concatenate([byte_ids[:, :1], byte_ids[:, :-1]], axis=1).reshape(-1)
    live_rows = jnp.tile(jnp.arange(PATCH) > 0, patch_count)
    letters = jnp.arange(vocab_size)
    one_hot = ((previous[:, None] == letters[None, :]) & live_rows[:, None]).astype(jnp.bfloat16)
    hidden_in = hidden_in + jnp.dot(one_hot, byte_embed, preferred_element_type=jnp.float32)
    inverse_rms = lax.rsqrt(lax.optimization_barrier(jnp.mean(hidden_in * hidden_in, axis=1, keepdims=True)) + EPSILON)
    normed = (hidden_in * inverse_rms * norm_gain).astype(jnp.bfloat16)
    raised = jnp.dot(normed, w_up, preferred_element_type=jnp.float32)
    active = jax.nn.gelu(raised, approximate=True).astype(jnp.bfloat16)
    after_mlp = hidden_in + jnp.dot(active, w_down, preferred_element_type=jnp.float32)
    final_scale = lax.rsqrt(lax.optimization_barrier(jnp.mean(after_mlp * after_mlp, axis=1, keepdims=True)) + EPSILON)
    final_rows = (after_mlp * final_scale).astype(jnp.bfloat16)
    logits = jnp.dot(final_rows, vocab_head, preferred_element_type=jnp.float32)
    row_top = lax.stop_gradient(lax.optimization_barrier(jnp.max(logits, axis=1, keepdims=True)))
    log_total = jnp.log(lax.optimization_barrier(jnp.sum(jnp.exp(logits - row_top), axis=1))) + row_top[:, 0]
    target = byte_ids.reshape(-1)
    chosen = lax.optimization_barrier(jnp.sum(jnp.where(target[:, None] == letters[None, :], logits, 0.0), axis=1))
    return (log_total - chosen).reshape(patch_count, PATCH)

def visible(size):
    order = jnp.arange(size)
    return order[None, :] <= order[:, None]

def head_scores(queries, key_side):
    return jnp.dot(queries, key_side.T, preferred_element_type=jnp.float32) * HEAD ** (-0.5)

def head_forward(operands):
    queries, key_side, value_side = operands
    scores = head_scores(queries, key_side)
    allowed = visible(scores.shape[0])
    row_top = lax.optimization_barrier(jnp.max(jnp.where(allowed, scores, -1e+30), axis=1, keepdims=True))
    spread = jnp.where(allowed, jnp.exp(jnp.where(allowed, scores - row_top, -1e+30)), 0.0)
    log_mass = row_top[:, 0] + jnp.log(lax.optimization_barrier(jnp.sum(spread, axis=1)))
    shifted = jnp.where(allowed, scores - log_mass[:, None], -1e+30)
    weights = jnp.where(allowed, jnp.exp(shifted), 0.0)
    attended = jnp.dot(weights, value_side.astype(jnp.float32), precision=lax.Precision.HIGHEST).astype(jnp.bfloat16)
    return (attended, log_mass)

def head_backward(operands):
    queries, key_side, value_side, attended, log_mass, out_grad = operands
    scores = head_scores(queries, key_side)
    allowed = visible(scores.shape[0])
    shifted = jnp.where(allowed, scores - log_mass[:, None], -1e+30)
    chances = jnp.where(allowed, jnp.exp(shifted), 0.0)
    row_dot = lax.optimization_barrier(jnp.sum(out_grad.astype(jnp.float32) * attended.astype(jnp.float32), axis=1))
    chance_grad = jnp.dot(out_grad, value_side.T, preferred_element_type=jnp.float32)
    score_grad = (chances * (chance_grad - row_dot[:, None])).astype(jnp.bfloat16)
    query_grad = (jnp.dot(score_grad, key_side, preferred_element_type=jnp.float32) * HEAD ** (-0.5)).astype(jnp.bfloat16)
    key_grad = (jnp.dot(score_grad.T, queries, preferred_element_type=jnp.float32) * HEAD ** (-0.5)).astype(jnp.bfloat16)
    value_grad = jnp.dot(chances.astype(jnp.bfloat16).T, out_grad, preferred_element_type=jnp.float32).astype(jnp.bfloat16)
    return (query_grad, key_grad, value_grad)

def by_heads(matrix):
    return matrix.reshape(matrix.shape[0], -1, HEAD).transpose(1, 0, 2)

def from_heads(stack):
    return stack.transpose(1, 0, 2).reshape(stack.shape[1], -1)

def reference(byte_ids, patch_order, query_rows, key_rows, value_rows, byte_embed, norm_gain, w_up, w_down, vocab_head):
    split_query = by_heads(query_rows)
    split_key = by_heads(key_rows)
    split_value = by_heads(value_rows)
    attended_stack, log_mass = lax.map(head_forward, (split_query, split_key, split_value))
    attended = from_heads(attended_stack)

    def scored(context):
        return local_model(context, byte_ids, byte_embed, norm_gain, w_up, w_down, vocab_head)
    byte_loss, pull_back = jax.vjp(scored, attended)
    context_grad, = pull_back(jnp.ones_like(byte_loss))
    grads = lax.map(head_backward, (split_query, split_key, split_value, attended_stack, log_mass, by_heads(context_grad)))
    return (byte_loss[patch_order], from_heads(grads[0]), from_heads(grads[1]), from_heads(grads[2]))
```

```python
import functools

import jax
import jax.numpy as jnp
from jax import lax
from jax.experimental import pallas as pl
from jax.experimental.pallas import tpu as pltpu
from jax.sharding import Mesh
from jax.sharding import PartitionSpec as P

HEAD = 128
PATCH = 8
SEQ = ("seq_0", "seq_1", "seq_2")
SEQ_GRP = ("seq_0", "seq_1", "seq_2", "grp")
CHIPS = ("seq_0", "seq_1")

EPSILON = 1e-05
FLOOR = -1e30
SCALE = HEAD ** (-0.5)
LOG2E = 1.4426950408889634
MIB = 2**20

BF16 = jnp.bfloat16
F32 = jnp.float32

NT = (((1,), (1,)), ((), ()))
NN = (((1,), (0,)), ((), ()))


def dot(a, b, dims=NN):
    return lax.dot_general(a, b, dims, preferred_element_type=F32)


WIDE = 256


def chunk_plan(rows, block):
    plan = []
    base = 0
    for first in range(0, rows, WIDE):
        lowest, highest = first // block, (first + WIDE - 1) // block
        own_keys = first + WIDE
        other_keys = min(rows, 2 * block * ((highest + 2) // 2))
        pieces = []
        for at in range(0, own_keys, WIDE):
            pieces.append((0, at, WIDE, "causal" if at == first else "all"))
        at = 0
        while at < other_keys:
            part = at // block
            if part < lowest:
                pieces.append((1, at, block, "all"))
            elif part <= highest:
                pieces.append((1, at, block, "block"))
            else:
                pieces.append((1, at, block, "none"))
            at += block
        plan.append((first, base, own_keys, other_keys, pieces))
        base += own_keys + other_keys
    return plan, base


def forward_kernel(
    plan, block, core_ref, own_ref, other_ref, out_ref, inverse_ref, kept_ref, key_s, turned_s, score_s
):
    parts = own_ref.shape[0]
    for j in range(parts):
        rows = pl.ds(j * block, block)
        key_s[0, rows] = own_ref[j, 1]
        key_s[1, rows] = other_ref[j, 0]
    for j in range(0, parts, 2):
        columns = pl.ds(j * block, 2 * block)
        for side in range(2):
            ref = own_ref if side == 0 else other_ref
            at = 2 if side == 0 else 1
            two = jnp.concatenate([ref[j, at], ref[j + 1, at]], 0)
            turned_s[side, :, columns] = two.T
    core = core_ref[0]
    factor = SCALE * LOG2E
    for first, base, own_keys, other_keys, pieces in plan:
        q_parts = []
        at = first
        while at < first + WIDE:
            stop = min(first + WIDE, (at // block + 1) * block)
            q_parts.append(own_ref[at // block, 0, pl.ds(at % block, stop - at)])
            at = stop
        queries = jnp.concatenate(q_parts, 0)
        top = None
        for side, at, size, kind in pieces:
            if kind == "none":
                continue
            score = dot(key_s[side, pl.ds(at, size)], queries, NT)
            if kind == "causal":
                key_at = lax.broadcasted_iota(jnp.int32, score.shape, 0)
                query_at = lax.broadcasted_iota(jnp.int32, score.shape, 1)
                score = jnp.where(key_at <= query_at, score, FLOOR)
            elif kind == "block":
                row = first + lax.broadcasted_iota(jnp.int32, (1, WIDE), 1)
                part = at // block
                shown = row >= block * (part + 1 - core)
                score = jnp.where(shown, score, FLOOR)
            score_s[pl.ds(side * own_keys + at, size)] = score
            piece_top = jnp.max(score, axis=0, keepdims=True)
            top = piece_top if top is None else jnp.maximum(top, piece_top)
        shift = top * factor
        total = jnp.zeros((1, WIDE), F32)
        for side, at, size, kind in pieces:
            spot = side * own_keys + at
            if kind == "none":
                kept_ref[pl.ds(base + spot, size)] = jnp.zeros((size, WIDE), BF16)
                continue
            chance = jnp.exp2(score_s[pl.ds(spot, size)] * factor - shift)
            total = total + jnp.sum(chance, axis=0, keepdims=True)
            kept_ref[pl.ds(base + spot, size)] = chance.astype(BF16)
        mixed = dot(turned_s[0, :, :own_keys], kept_ref[pl.ds(base, own_keys)])
        mixed += dot(turned_s[1, :, :other_keys], kept_ref[pl.ds(base + own_keys, other_keys)])
        inverse = jnp.broadcast_to(1.0 / total, (HEAD, WIDE))
        out_ref[pl.ds(first, WIDE)] = (mixed * inverse).T.astype(BF16)
        inverse_ref[pl.ds(first, WIDE)] = inverse.T


def backward_kernel(
    plan,
    block,
    own_ref,
    other_ref,
    mixed_ref,
    inverse_ref,
    kept_ref,
    grad_ref,
    query_ref,
    own_out_ref,
    other_out_ref,
    value_s,
    turned_s,
    key_sum,
    value_sum,
    slope_s,
):
    parts = own_ref.shape[0]
    for j in range(parts):
        rows = pl.ds(j * block, block)
        value_s[0, rows] = own_ref[j, 2]
        value_s[1, rows] = other_ref[j, 1]
    for j in range(0, parts, 2):
        columns = pl.ds(j * block, 2 * block)
        for side in range(2):
            ref = own_ref if side == 0 else other_ref
            at = 1 if side == 0 else 0
            two = jnp.concatenate([ref[j, at], ref[j + 1, at]], 0)
            turned_s[side, :, columns] = two.T
    reached = [0, 0]
    for first, base, own_keys, other_keys, pieces in plan:
        q_parts = []
        at = first
        while at < first + WIDE:
            stop = min(first + WIDE, (at // block + 1) * block)
            q_parts.append(own_ref[at // block, 0, pl.ds(at % block, stop - at)])
            at = stop
        queries = jnp.concatenate(q_parts, 0)
        rows = pl.ds(first, WIDE)
        grads = (grad_ref[rows].astype(F32) * inverse_ref[rows]).astype(BF16)
        product = grads.astype(F32) * mixed_ref[rows].astype(F32)
        row_dot = jnp.sum(product.T, axis=0, keepdims=True)
        for side, at, size, kind in pieces:
            spot = side * own_keys + at
            if kind == "none":
                slope_s[pl.ds(spot, size)] = jnp.zeros((size, WIDE), BF16)
                continue
            kept = kept_ref[pl.ds(base + spot, size)]
            chance_grad = dot(value_s[side, pl.ds(at, size)], grads, NT)
            slope = (kept.astype(F32) * (chance_grad - row_dot)).astype(BF16)
            slope_s[pl.ds(spot, size)] = slope
            value_part = dot(kept, grads)
            key_part = dot(slope, queries)
            keys = pl.ds(at, size)
            if at >= reached[side]:
                reached[side] = at + size
                value_sum[side, keys] = value_part
                key_sum[side, keys] = key_part
            else:
                value_sum[side, keys] += value_part
                key_sum[side, keys] += key_part
        turned = dot(turned_s[0, :, :own_keys], slope_s[pl.ds(0, own_keys)])
        turned += dot(turned_s[1, :, :other_keys], slope_s[pl.ds(own_keys, other_keys)])
        query_ref[rows] = (turned * SCALE).T.astype(BF16)
    for j in range(parts):
        rows = pl.ds(j * block, block)
        own_out_ref[j, 0] = key_sum[0, rows] * SCALE
        own_out_ref[j, 1] = value_sum[0, rows]
        other_out_ref[j, 0] = (key_sum[1, rows] * SCALE).astype(BF16)
        other_out_ref[j, 1] = value_sum[1, rows].astype(BF16)


GELU_A = 0.7978845608028654
GELU_B = 0.044715


def byte_kernel(
    pieces,
    place_ref,
    rows_ref,
    ids_ref,
    order_ref,
    embed_ref,
    gain_ref,
    up_hbm,
    down_hbm,
    vocab_ref,
    grad_ref,
    loss_ref,
    up_s,
    down_s,
    bend_s,
    up_sem,
    down_sem,
):
    heads, count, _ = rows_ref.shape
    width = embed_ref.shape[1]
    hidden = up_s.shape[1]
    size = hidden // pieces
    up_copies = []
    down_copies = []
    for i in range(pieces):
        part = pl.ds(i * size, size)
        up_copies.append(pltpu.make_async_copy(up_hbm.at[:, part], up_s.at[:, part], up_sem.at[i]))
        down_copies.append(pltpu.make_async_copy(down_hbm.at[part], down_s.at[part], down_sem.at[i]))
        up_copies[-1].start()
        down_copies[-1].start()
    place = place_ref[0]
    ids = ids_ref[...]
    lane = lax.broadcasted_iota(jnp.int32, ids.shape, 1)
    target = jnp.sum(jnp.where(lane == place, ids, 0), axis=1, keepdims=True)
    previous = jnp.sum(jnp.where(lane == place - 1, ids, 0), axis=1, keepdims=True)
    letters = lax.broadcasted_iota(jnp.int32, (count, vocab_ref.shape[1]), 1)
    live = jnp.where(place > 0, 1.0, 0.0)
    one_hot = jnp.where(previous == letters, live, 0.0).astype(BF16)
    hidden_in = jnp.concatenate([rows_ref[h].astype(F32) for h in range(heads)], 1)
    hidden_in = hidden_in + dot(one_hot, embed_ref[...])
    inverse_rms = lax.rsqrt(jnp.mean(hidden_in * hidden_in, axis=1, keepdims=True) + EPSILON)
    gain = gain_ref[...]
    normed = (hidden_in * inverse_rms * gain).astype(BF16)
    after = hidden_in
    for i in range(pieces):
        part = pl.ds(i * size, size)
        up_copies[i].wait()
        raised = dot(normed, up_s[:, part])
        square = raised * raised
        bent = jnp.tanh(GELU_A * raised * (1.0 + GELU_B * square))
        half = 0.5 * (1.0 + bent)
        active = (raised * half).astype(BF16)
        bend_s[:, part] = half + 0.5 * raised * (1.0 - bent * bent) * (
            GELU_A + (3.0 * GELU_A * GELU_B) * square
        )
        down_copies[i].wait()
        after = after + dot(active, down_s[part])
    final_scale = lax.rsqrt(jnp.mean(after * after, axis=1, keepdims=True) + EPSILON)
    final_rows = (after * final_scale).astype(BF16)
    logits = dot(final_rows, vocab_ref[...])
    row_top = jnp.max(logits, axis=1, keepdims=True)
    raised_mass = jnp.exp(logits - row_top)
    mass = jnp.sum(raised_mass, axis=1, keepdims=True)
    is_target = target == letters
    chosen = jnp.sum(jnp.where(is_target, logits, 0.0), axis=1, keepdims=True)
    loss = jnp.log(mass) + row_top - chosen
    row_at = lax.broadcasted_iota(jnp.int32, (count, count), 0)
    loss_ref[...] = jnp.sum(jnp.where(row_at == order_ref[...], loss, 0.0), axis=0, keepdims=True)
    logit_grad = raised_mass / mass - jnp.where(is_target, 1.0, 0.0)
    final_grad = dot(logit_grad.astype(BF16), vocab_ref[...], NT).astype(BF16).astype(F32)
    mean_dot = jnp.mean(final_grad * after, axis=1, keepdims=True)
    after_grad = final_scale * final_grad - after * (final_scale * final_scale * final_scale * mean_dot)
    narrow = after_grad.astype(BF16)
    normed_grad = None
    for i in range(pieces):
        part = pl.ds(i * size, size)
        active_grad = dot(narrow, down_s[part], NT).astype(BF16).astype(F32)
        raised_grad = (active_grad * bend_s[:, part]).astype(BF16)
        term = dot(raised_grad, up_s[:, part], NT)
        normed_grad = term if normed_grad is None else normed_grad + term
    scaled = normed_grad.astype(BF16).astype(F32) * gain
    mean_dot = jnp.mean(scaled * hidden_in, axis=1, keepdims=True)
    total = (
        after_grad
        + inverse_rms * scaled
        - hidden_in * (inverse_rms * inverse_rms * inverse_rms * mean_dot)
    ).astype(BF16)
    for h in range(heads):
        grad_ref[h] = total[:, h * HEAD : (h + 1) * HEAD]


def vmem():
    return pl.BlockSpec(memory_space=pltpu.VMEM)


def smem():
    return pl.BlockSpec(memory_space=pltpu.SMEM)


def shape(dims, kind=BF16):
    return jax.ShapeDtypeStruct(dims, kind)


def exchange(value):
    return lax.all_to_all(value, CHIPS, split_axis=0, concat_axis=0, tiled=True)


def swap_cores(value):
    return lax.ppermute(value, "seq_2", [(0, 1), (1, 0)])


def shards(
    byte_ids,
    patch_order,
    query_rows,
    key_rows,
    value_rows,
    byte_embed,
    norm_gain,
    w_up,
    w_down,
    vocab_head,
):
    count, columns = query_rows.shape
    heads = columns // HEAD
    rows = heads * count
    seq_here = lax.axis_index(SEQ)
    place = lax.axis_index("grp").astype(jnp.int32)
    core = lax.axis_index("seq_2").astype(jnp.int32)
    plan, kept_rows = chunk_plan(rows, count)

    stacked = jnp.stack([query_rows, key_rows, value_rows])
    stacked = stacked.reshape(3, count, heads, HEAD).transpose(2, 0, 1, 3)
    own = exchange(stacked)
    other = swap_cores(own[:, 1:])

    attended, inverse, kept = pl.pallas_call(
        functools.partial(forward_kernel, plan, count),
        out_shape=(shape((rows, HEAD)), shape((rows, HEAD), F32), shape((kept_rows, WIDE))),
        in_specs=[smem(), vmem(), vmem()],
        out_specs=(vmem(), vmem(), vmem()),
        scratch_shapes=[
            pltpu.VMEM((2, rows, HEAD), BF16),
            pltpu.VMEM((2, HEAD, rows), BF16),
            pltpu.VMEM((2 * rows, WIDE), F32),
        ],
        compiler_params=pltpu.CompilerParams(vmem_limit_bytes=30 * MIB),
        cost_estimate=pl.CostEstimate(
            flops=4 * kept_rows * WIDE * HEAD, bytes_accessed=8 * MIB, transcendentals=kept_rows * WIDE
        ),
        name="attention_forward",
    )(core[None], own, other)

    owned_rows = exchange(attended.reshape(heads, count, HEAD))
    local_order = (patch_order - seq_here * count)[None]
    hidden = w_up.shape[1]
    pieces = 8
    context_grad, loss = pl.pallas_call(
        functools.partial(byte_kernel, pieces),
        out_shape=(shape((heads, count, HEAD)), shape((1, count), F32)),
        in_specs=[
            smem(),
            vmem(),
            vmem(),
            vmem(),
            vmem(),
            vmem(),
            pl.BlockSpec(memory_space=pl.ANY),
            pl.BlockSpec(memory_space=pl.ANY),
            vmem(),
        ],
        out_specs=(vmem(), vmem()),
        scratch_shapes=[
            pltpu.VMEM(w_up.shape, BF16),
            pltpu.VMEM(w_down.shape, BF16),
            pltpu.VMEM((count, hidden), F32),
            pltpu.SemaphoreType.DMA((pieces,)),
            pltpu.SemaphoreType.DMA((pieces,)),
        ],
        compiler_params=pltpu.CompilerParams(vmem_limit_bytes=44 * MIB),
        cost_estimate=pl.CostEstimate(
            flops=8 * count * columns * hidden,
            bytes_accessed=4 * columns * hidden,
            transcendentals=count * hidden,
        ),
        name="byte_layer",
    )(
        place[None],
        owned_rows,
        byte_ids,
        local_order,
        byte_embed,
        norm_gain[None],
        w_up,
        w_down,
        vocab_head,
    )

    grad_rows = exchange(context_grad).reshape(rows, HEAD)
    query_grad, own_grad, other_grad = pl.pallas_call(
        functools.partial(backward_kernel, plan, count),
        out_shape=(
            shape((rows, HEAD)),
            shape((heads, 2, count, HEAD), F32),
            shape((heads, 2, count, HEAD)),
        ),
        in_specs=[vmem()] * 6,
        out_specs=(vmem(), vmem(), vmem()),
        scratch_shapes=[
            pltpu.VMEM((2, rows, HEAD), BF16),
            pltpu.VMEM((2, HEAD, rows), BF16),
            pltpu.VMEM((2, rows, HEAD), F32),
            pltpu.VMEM((2, rows, HEAD), F32),
            pltpu.VMEM((2 * rows, WIDE), BF16),
        ],
        compiler_params=pltpu.CompilerParams(vmem_limit_bytes=30 * MIB),
        cost_estimate=pl.CostEstimate(
            flops=8 * kept_rows * WIDE * HEAD, bytes_accessed=12 * MIB, transcendentals=0
        ),
        name="attention_backward",
    )(own, other, attended, inverse, kept, grad_rows)

    pair_grad = (own_grad + swap_cores(other_grad).astype(F32)).astype(BF16)
    all_grads = jnp.concatenate([query_grad.reshape(heads, 1, count, HEAD), pair_grad], 1)
    back = exchange(all_grads).transpose(1, 2, 0, 3).reshape(3, count, columns)

    losses = lax.all_gather(loss[0], "grp")
    own_slots = count // PATCH
    byte_loss = lax.dynamic_slice_in_dim(losses, place * own_slots, own_slots, 1).T
    return byte_loss, back[0], back[1], back[2]


def solution(mesh):
    torus = Mesh(
        mesh.devices.reshape(4, 2, 2, mesh.shape["grp"]), ("seq_0", "seq_1", "seq_2", "grp")
    )
    placed = (
        P(SEQ, None),
        P(SEQ),
        P(SEQ, "grp"),
        P(SEQ, "grp"),
        P(SEQ, "grp"),
        P(),
        P(),
        P(),
        P(),
        P(),
    )
    return jax.shard_map(
        shards,
        mesh=torus,
        in_specs=placed,
        out_specs=(P(SEQ_GRP, None), P(SEQ, "grp"), P(SEQ, "grp"), P(SEQ, "grp")),
        check_vma=False,
    )
```

```python
import functools

import jax
import jax.numpy as jnp
from jax import lax
from jax.experimental import pallas as pl
from jax.experimental.pallas import tpu as pltpu
from jax.sharding import Mesh
from jax.sharding import PartitionSpec as P

HEAD = 128
PATCH = 8
SEQ = ("seq_0", "seq_1", "seq_2")
SEQ_GRP = ("seq_0", "seq_1", "seq_2", "grp")
CHIPS = ("seq_0", "seq_1")

EPSILON = 1e-05
FLOOR = -1e30
SCALE = HEAD ** (-0.5)
LOG2E = 1.4426950408889634
MIB = 2**20

BF16 = jnp.bfloat16
F32 = jnp.float32

NT = (((1,), (1,)), ((), ()))
NN = (((1,), (0,)), ((), ()))


def dot(a, b, dims=NN):
    return lax.dot_general(a, b, dims, preferred_element_type=F32)


WIDE = 256


def own_plan(rows):
    plan = []
    base = 0
    for first in range(0, rows, WIDE):
        pieces = [(at, WIDE, "causal" if at == first else "all") for at in range(0, first + WIDE, WIDE)]
        plan.append((first, base, first + WIDE, pieces))
        base += first + WIDE
    return plan, base


def other_plan(rows, block):
    plan = []
    base = 0
    for first in range(0, rows, WIDE):
        lowest, highest = first // block, (first + WIDE - 1) // block
        keys = min(rows, 2 * block * ((highest + 2) // 2))
        pieces = []
        for at in range(0, keys, block):
            part = at // block
            kind = "all" if part < lowest else "block" if part <= highest else "none"
            pieces.append((at, block, kind))
        plan.append((first, base, keys, pieces))
        base += keys
    return plan, base


def flat_rows(ref, at, target):
    block = ref.shape[2]
    for j in range(ref.shape[0]):
        target[pl.ds(j * block, block)] = ref[j, at]


def turned_rows(ref, at, target):
    block = ref.shape[2]
    for j in range(0, ref.shape[0], 2):
        two = jnp.concatenate([ref[j, at], ref[j + 1, at]], 0)
        target[:, pl.ds(j * block, 2 * block)] = two.T


def query_chunk(ref, first):
    block = ref.shape[2]
    found = []
    at = first
    while at < first + WIDE:
        stop = min(first + WIDE, (at // block + 1) * block)
        found.append(ref[at // block, 0, pl.ds(at % block, stop - at)])
        at = stop
    return jnp.concatenate(found, 0)


def piece_scores(queries, first, pieces, key_s, score_s, core):
    top = None
    for at, size, kind in pieces:
        if kind == "none":
            continue
        score = dot(key_s[pl.ds(at, size)], queries, NT)
        if kind == "causal":
            key_at = lax.broadcasted_iota(jnp.int32, score.shape, 0)
            query_at = lax.broadcasted_iota(jnp.int32, score.shape, 1)
            score = jnp.where(key_at <= query_at, score, FLOOR)
        elif kind == "block":
            row = first + lax.broadcasted_iota(jnp.int32, (1, WIDE), 1)
            shown = row >= size * (at // size + 1 - core)
            score = jnp.where(shown, score, FLOOR)
        score_s[pl.ds(at, size)] = score
        piece_top = jnp.max(score, axis=0, keepdims=True)
        top = piece_top if top is None else jnp.maximum(top, piece_top)
    return top


def piece_chances(shift, base, pieces, score_s, kept_ref):
    total = jnp.zeros((1, WIDE), F32)
    for at, size, kind in pieces:
        kept = pl.ds(base + at, size)
        if kind == "none":
            kept_ref[kept] = jnp.zeros((size, WIDE), BF16)
            continue
        chance = jnp.exp2(score_s[pl.ds(at, size)] * (SCALE * LOG2E) - shift)
        total = total + jnp.sum(chance, axis=0, keepdims=True)
        kept_ref[kept] = chance.astype(BF16)
    return total


def forward_own(plan, own_ref, load_ref, kept_ref, mixed_ref, stats_ref, loaded_ref, key_s, turned_s, score_s, sem):
    load = pltpu.make_async_copy(load_ref, loaded_ref, sem)
    load.start()
    flat_rows(own_ref, 1, key_s)
    turned_rows(own_ref, 2, turned_s)
    for i, (first, base, keys, pieces) in enumerate(plan):
        top = piece_scores(query_chunk(own_ref, first), first, pieces, key_s, score_s, None)
        shift = top * (SCALE * LOG2E)
        total = piece_chances(shift, base, pieces, score_s, kept_ref)
        mixed_ref[i] = dot(turned_s[:, :keys], kept_ref[pl.ds(base, keys)])
        stats_ref[i, 0:1] = shift
        stats_ref[i, 1:2] = total
    load.wait()


def forward_other(
    plan,
    facts_ref,
    own_ref,
    other_ref,
    mixed_ref,
    stats_ref,
    load_ref,
    kept_ref,
    out_ref,
    own_inverse_ref,
    inverse_ref,
    loaded_ref,
    key_s,
    turned_s,
    score_s,
    sem,
):
    load = pltpu.make_async_copy(load_ref, loaded_ref, sem)
    load.start()
    flat_rows(other_ref, 0, key_s)
    turned_rows(other_ref, 1, turned_s)
    core = facts_ref[2]
    for i, (first, base, keys, pieces) in enumerate(plan):
        top = piece_scores(query_chunk(own_ref, first), first, pieces, key_s, score_s, core)
        own_shift = stats_ref[i, 0:1]
        shift = jnp.maximum(top * (SCALE * LOG2E), own_shift)
        total = piece_chances(shift, base, pieces, score_s, kept_ref)
        own_part = jnp.exp2(own_shift - shift)
        total = total + own_part * stats_ref[i, 1:2]
        mixed = mixed_ref[i] * own_part + dot(turned_s[:, :keys], kept_ref[pl.ds(base, keys)])
        inverse = 1.0 / total
        rows = pl.ds(first, WIDE)
        out_ref[rows] = (mixed * inverse).T.astype(BF16)
        inverse_ref[rows] = jnp.broadcast_to(inverse, (HEAD, WIDE)).T
        own_inverse_ref[rows] = jnp.broadcast_to(own_part * inverse, (HEAD, WIDE)).T
    load.wait()


def backward_side(
    plan, key_at, own_ref, side_ref, mixed_ref, inverse_ref, kept_ref, grad_ref, key_sum, value_sum, value_s, turned_s,
    slope_s,
):
    flat_rows(side_ref, key_at + 1, value_s)
    turned_rows(side_ref, key_at, turned_s)
    reached = 0
    for i, (first, base, keys, pieces) in enumerate(plan):
        queries = query_chunk(own_ref, first)
        rows = pl.ds(first, WIDE)
        grads = (grad_ref[rows].astype(F32) * inverse_ref[rows]).astype(BF16)
        product = grads.astype(F32) * mixed_ref[rows].astype(F32)
        row_dot = jnp.sum(product.T, axis=0, keepdims=True)
        for at, size, kind in pieces:
            spot = pl.ds(at, size)
            if kind == "none":
                slope_s[spot] = jnp.zeros((size, WIDE), BF16)
                continue
            kept = kept_ref[pl.ds(base + at, size)]
            chance_grad = dot(value_s[spot], grads, NT)
            slope = (kept.astype(F32) * (chance_grad - row_dot)).astype(BF16)
            slope_s[spot] = slope
            value_part = dot(kept, grads)
            key_part = dot(slope, queries)
            if at >= reached:
                reached = at + size
                value_sum[spot] = value_part
                key_sum[spot] = key_part
            else:
                value_sum[spot] += value_part
                key_sum[spot] += key_part
        yield i, dot(turned_s[:, :keys], slope_s[pl.ds(0, keys)])


def backward_other(
    plan, own_ref, other_ref, mixed_ref, inverse_ref, kept_ref, grad_ref, pair_ref, query_ref, key_sum, value_sum,
    value_s, turned_s, slope_s,
):
    for i, turned in backward_side(
        plan, 0, own_ref, other_ref, mixed_ref, inverse_ref, kept_ref, grad_ref, key_sum, value_sum, value_s, turned_s,
        slope_s,
    ):
        query_ref[i] = turned
    parts, _, block, _ = other_ref.shape
    for j in range(parts):
        rows = pl.ds(j * block, block)
        pair_ref[j, 0] = (key_sum[rows] * SCALE).astype(BF16)
        pair_ref[j, 1] = value_sum[rows].astype(BF16)


def backward_own(
    plan, own_ref, mixed_ref, inverse_ref, kept_ref, grad_ref, turned_ref, query_ref, key_ref, value_ref, value_s,
    turned_s, slope_s,
):
    for i, turned in backward_side(
        plan, 1, own_ref, own_ref, mixed_ref, inverse_ref, kept_ref, grad_ref, key_ref, value_ref, value_s, turned_s,
        slope_s,
    ):
        first = plan[i][0]
        query_ref[pl.ds(first, WIDE)] = ((turned + turned_ref[i]) * SCALE).T.astype(BF16)


def join_kernel(query_ref, key_ref, value_ref, pair_ref, out_ref):
    parts, _, block, _ = out_ref.shape
    for j in range(parts):
        rows = pl.ds(j * block, block)
        out_ref[j, 0] = query_ref[rows]
        out_ref[j, 1] = (key_ref[rows] * SCALE + pair_ref[j, 0].astype(F32)).astype(BF16)
        out_ref[j, 2] = (value_ref[rows] + pair_ref[j, 1].astype(F32)).astype(BF16)


def pack_kernel(*refs):
    arrays, out_ref, sems = refs[:-2], refs[-2], refs[-1]
    copies = []
    for t, ref in enumerate(arrays):
        for h in range(out_ref.shape[0]):
            source = ref.at[:, pl.ds(h * HEAD, HEAD)]
            copies.append(pltpu.make_async_copy(source, out_ref.at[h, t], sems.at[len(copies)]))
            copies[-1].start()
    for copy in copies:
        copy.wait()


def unpack_kernel(stack_ref, *refs):
    arrays, sems = refs[:-1], refs[-1]
    copies = []
    for t, ref in enumerate(arrays):
        for h in range(stack_ref.shape[0]):
            target = ref.at[:, pl.ds(h * HEAD, HEAD)]
            copies.append(pltpu.make_async_copy(stack_ref.at[h, t], target, sems.at[len(copies)]))
            copies[-1].start()
    for copy in copies:
        copy.wait()


def turn_kernel(up_ref, down_ref, up_out, down_out):
    up_out[...] = up_ref[...].T
    down_out[...] = down_ref[...].T


GELU_A = 0.7978845608028654
GELU_B = 0.044715


def byte_kernel(
    pieces,
    facts_ref,
    rows_ref,
    ids_ref,
    order_ref,
    embed_ref,
    gain_ref,
    up_ref,
    down_ref,
    up_turned_ref,
    down_turned_ref,
    vocab_ref,
    grad_ref,
    loss_ref,
    bend_s,
):
    heads, count, _ = rows_ref.shape
    size = up_ref.shape[1] // pieces
    place = facts_ref[0]
    ids = ids_ref[...].T
    lane = lax.broadcasted_iota(jnp.int32, ids.shape, 1)
    target = jnp.sum(jnp.where(lane == place, ids, 0), axis=1, keepdims=True)
    previous = jnp.sum(jnp.where(lane == place - 1, ids, 0), axis=1, keepdims=True)
    letters = lax.broadcasted_iota(jnp.int32, (count, vocab_ref.shape[1]), 1)
    live = jnp.where(place > 0, 1.0, 0.0)
    one_hot = jnp.where(previous == letters, live, 0.0).astype(BF16)
    hidden_in = jnp.concatenate([rows_ref[h].astype(F32) for h in range(heads)], 1)
    hidden_in = hidden_in + dot(one_hot, embed_ref[...])
    inverse_rms = lax.rsqrt(jnp.mean(hidden_in * hidden_in, axis=1, keepdims=True) + EPSILON)
    gain = gain_ref[...]
    normed = (hidden_in * inverse_rms * gain).astype(BF16)
    after = hidden_in
    for i in range(pieces):
        part = pl.ds(i * size, size)
        raised = dot(normed, up_ref[:, part])
        square = raised * raised
        half = 0.5 + 0.5 * jnp.tanh(raised * (GELU_A + (GELU_A * GELU_B) * square))
        active = (raised * half).astype(BF16)
        bend_s[:, part] = half + half * (1.0 - half) * raised * (
            2.0 * GELU_A + (6.0 * GELU_A * GELU_B) * square
        )
        after = after + dot(active, down_ref[part])
    final_scale = lax.rsqrt(jnp.mean(after * after, axis=1, keepdims=True) + EPSILON)
    final_rows = (after * final_scale).astype(BF16)
    logits = dot(final_rows, vocab_ref[...])
    row_top = jnp.max(logits, axis=1, keepdims=True)
    raised_mass = jnp.exp(logits - row_top)
    mass = jnp.sum(raised_mass, axis=1, keepdims=True)
    is_target = target == letters
    chosen = jnp.sum(jnp.where(is_target, logits, 0.0), axis=1, keepdims=True)
    loss = jnp.log(mass) + row_top - chosen
    row_at = lax.broadcasted_iota(jnp.int32, (count, count), 0)
    ordered = jnp.sum(jnp.where(row_at == order_ref[...] - facts_ref[1], loss, 0.0), axis=0, keepdims=True)
    slot = lax.broadcasted_iota(jnp.int32, loss_ref.shape, 0)
    loss_ref[...] = jnp.where(slot == place, ordered, 0.0)
    logit_grad = raised_mass / mass - jnp.where(is_target, 1.0, 0.0)
    final_grad = dot(logit_grad.astype(BF16), vocab_ref[...], NT).astype(BF16).astype(F32)
    mean_dot = jnp.mean(final_grad * after, axis=1, keepdims=True)
    after_grad = final_scale * final_grad - after * (final_scale * final_scale * final_scale * mean_dot)
    narrow = after_grad.astype(BF16)
    normed_grad = None
    for i in range(pieces):
        part = pl.ds(i * size, size)
        active_grad = dot(narrow, down_turned_ref[:, part]).astype(BF16).astype(F32)
        raised_grad = (active_grad * bend_s[:, part]).astype(BF16)
        term = dot(raised_grad, up_turned_ref[part])
        normed_grad = term if normed_grad is None else normed_grad + term
    scaled = normed_grad.astype(BF16).astype(F32) * gain
    mean_dot = jnp.mean(scaled * hidden_in, axis=1, keepdims=True)
    total = (
        after_grad
        + inverse_rms * scaled
        - hidden_in * (inverse_rms * inverse_rms * inverse_rms * mean_dot)
    ).astype(BF16)
    for h in range(heads):
        grad_ref[h] = total[:, h * HEAD : (h + 1) * HEAD]


def vmem():
    return pl.BlockSpec(memory_space=pltpu.VMEM)


def far():
    return pl.BlockSpec(memory_space=pltpu.HBM)


def smem():
    return pl.BlockSpec(memory_space=pltpu.SMEM)


def held(dims, kind=BF16):
    return pltpu.VMEM(dims, kind)


def shape(dims, kind=BF16):
    return jax.ShapeDtypeStruct(dims, kind)


def exchange(value):
    return lax.all_to_all(value, CHIPS, split_axis=0, concat_axis=0, tiled=True)


def gather_losses(value, bit):
    return value + lax.ppermute(value, "grp", [(i, i ^ (1 << bit)) for i in range(PATCH)])


def swap_cores(value):
    return lax.ppermute(value, "seq_2", [(0, 1), (1, 0)])


def anywhere():
    return pl.BlockSpec(memory_space=pl.ANY)


def kernel_call(body, name, outs, ins, out_specs, scratch, grant, flops, transcendentals=0, moved=4 * MIB):
    return pl.pallas_call(
        body,
        out_shape=outs,
        in_specs=ins,
        out_specs=out_specs,
        scratch_shapes=scratch,
        compiler_params=pltpu.CompilerParams(vmem_limit_bytes=grant * MIB),
        cost_estimate=pl.CostEstimate(
            flops=flops, bytes_accessed=moved, transcendentals=transcendentals
        ),
        name=name,
    )


def shards(
    byte_ids,
    patch_order,
    query_rows,
    key_rows,
    value_rows,
    byte_embed,
    norm_gain,
    w_up,
    w_down,
    vocab_head,
):
    count, columns = query_rows.shape
    hidden = w_up.shape[1]
    heads = columns // HEAD
    rows = heads * count
    chunks = rows // WIDE
    seq_here = lax.axis_index(SEQ)
    place = lax.axis_index("grp").astype(jnp.int32)
    core = lax.axis_index("seq_2").astype(jnp.int32)
    facts = jnp.stack([place, seq_here * count, core])
    query_rows, facts = lax.optimization_barrier((query_rows, facts))
    near_plan, near_rows = own_plan(rows)
    far_plan, far_rows = other_plan(rows, count)

    query_rows, key_rows, value_rows = (
        pltpu.with_memory_space_constraint(a, pltpu.HBM) for a in (query_rows, key_rows, value_rows)
    )
    stacked = kernel_call(
        pack_kernel,
        "pack",
        shape((heads, 3, count, HEAD)),
        [far()] * 3,
        anywhere(),
        [pltpu.SemaphoreType.DMA((3 * heads,))],
        1,
        0,
    )(query_rows, key_rows, value_rows)
    own = exchange(stacked)

    size = 512
    w_up = pltpu.with_memory_space_constraint(w_up, pltpu.HBM)
    w_down = pltpu.with_memory_space_constraint(w_down, pltpu.HBM)
    wide_block = pl.BlockSpec((columns, size), lambda i: (0, i))
    tall_block = pl.BlockSpec((size, columns), lambda i: (i, 0))
    turned = pl.pallas_call(
        turn_kernel,
        out_shape=(pltpu.HBM((hidden, columns), BF16), pltpu.HBM((columns, hidden), BF16)),
        grid=(hidden // size,),
        in_specs=[wide_block, tall_block],
        out_specs=(tall_block, wide_block),
        compiler_params=pltpu.CompilerParams(vmem_limit_bytes=12 * MIB),
        cost_estimate=pl.CostEstimate(flops=0, bytes_accessed=32 * MIB, transcendentals=0),
        name="turn_weights",
    )(w_up, w_down)
    own, turned = lax.optimization_barrier((own, turned))
    other = swap_cores(own[:, 1:])

    kv_scratch = [pltpu.VMEM((rows, HEAD), BF16), pltpu.VMEM((HEAD, rows), BF16)]
    near_kept, near_mixed, stats, up_held = kernel_call(
        functools.partial(forward_own, near_plan),
        "forward_own",
        (
            held((near_rows, WIDE)),
            held((chunks, HEAD, WIDE), F32),
            held((chunks, 8, WIDE), F32),
            held(w_up.shape),
        ),
        [vmem(), far()],
        (vmem(),) * 4,
        kv_scratch + [pltpu.VMEM((rows, WIDE), F32), pltpu.SemaphoreType.DMA],
        8,
        4 * near_rows * WIDE * HEAD,
        near_rows * WIDE,
    )(own, w_up)
    far_kept, attended, near_inverse, far_inverse, down_held = kernel_call(
        functools.partial(forward_other, far_plan),
        "forward_other",
        (
            held((far_rows, WIDE)),
            held((rows, HEAD)),
            held((rows, HEAD), F32),
            held((rows, HEAD), F32),
            held(w_down.shape),
        ),
        [smem()] + [vmem()] * 4 + [far()],
        (vmem(),) * 5,
        kv_scratch + [pltpu.VMEM((rows, WIDE), F32), pltpu.SemaphoreType.DMA],
        8,
        4 * far_rows * WIDE * HEAD,
        far_rows * WIDE,
    )(facts, own, other, near_mixed, stats, w_down)

    byte_pieces = 4
    owned_rows = exchange(attended.reshape(heads, count, HEAD))
    context_grad, losses = kernel_call(
        functools.partial(byte_kernel, byte_pieces),
        "byte_layer",
        (shape((heads, count, HEAD)), shape((PATCH, count), F32)),
        [smem()] + [vmem()] * 10,
        (vmem(), vmem()),
        [pltpu.VMEM((count, hidden), F32)],
        14,
        8 * count * columns * hidden,
        count * hidden,
    )(
        facts,
        owned_rows,
        byte_ids.T,
        patch_order[None],
        byte_embed,
        norm_gain[None],
        up_held,
        down_held,
        *turned,
        vocab_head,
    )

    grad_rows, losses = lax.optimization_barrier((exchange(context_grad), losses))
    grad_rows = grad_rows.reshape(rows, HEAD)
    side_scratch = kv_scratch + [pltpu.VMEM((rows, WIDE), BF16)]
    sums = [pltpu.VMEM((rows, HEAD), F32)] * 2
    pair_grad, turned_grad = kernel_call(
        functools.partial(backward_other, far_plan),
        "backward_other",
        (shape((heads, 2, count, HEAD)), shape((chunks, HEAD, WIDE), F32)),
        [vmem()] * 6,
        (vmem(), vmem()),
        sums + side_scratch,
        8,
        8 * far_rows * WIDE * HEAD,
    )(own, other, attended, far_inverse, far_kept, grad_rows)
    pair_grad, turned_grad, losses = lax.optimization_barrier((pair_grad, turned_grad, gather_losses(losses, 0)))
    pair_sent = swap_cores(pair_grad)
    query_grad, key_grad, value_grad = kernel_call(
        functools.partial(backward_own, near_plan),
        "backward_own",
        (shape((rows, HEAD)), shape((rows, HEAD), F32), shape((rows, HEAD), F32)),
        [vmem()] * 6,
        (vmem(), vmem(), vmem()),
        side_scratch,
        8,
        8 * near_rows * WIDE * HEAD,
    )(own, attended, near_inverse, near_kept, grad_rows, turned_grad)
    query_grad, losses = lax.optimization_barrier((query_grad, gather_losses(losses, 1)))
    losses = gather_losses(losses, 2)
    joined = kernel_call(
        join_kernel,
        "join",
        shape((heads, 3, count, HEAD)),
        [vmem()] * 4,
        vmem(),
        [],
        4,
        0,
    )(query_grad, key_grad, value_grad, pair_sent)
    joined, losses = lax.optimization_barrier((joined, losses))
    back = exchange(joined)
    query_out, key_out, value_out = kernel_call(
        unpack_kernel,
        "unpack",
        (shape((count, columns)),) * 3,
        [anywhere()],
        (anywhere(),) * 3,
        [pltpu.SemaphoreType.DMA((3 * heads,))],
        1,
        0,
    )(back)

    own_slots = count // PATCH
    byte_loss = lax.dynamic_slice_in_dim(losses, place * own_slots, own_slots, 1).T
    return byte_loss, query_out, key_out, value_out


def solution(mesh):
    torus = Mesh(
        mesh.devices.reshape(4, 2, 2, mesh.shape["grp"]), ("seq_0", "seq_1", "seq_2", "grp")
    )
    placed = (
        P(SEQ, None),
        P(SEQ),
        P(SEQ, "grp"),
        P(SEQ, "grp"),
        P(SEQ, "grp"),
        P(),
        P(),
        P(),
        P(),
        P(),
    )
    return jax.shard_map(
        shards,
        mesh=torus,
        in_specs=placed,
        out_specs=(P(SEQ_GRP, None), P(SEQ, "grp"), P(SEQ, "grp"), P(SEQ, "grp")),
        check_vma=False,
    )
```

```python
import functools

import jax
import jax.numpy as jnp
from jax import lax
from jax.experimental import pallas as pl
from jax.experimental.pallas import tpu as pltpu
from jax.sharding import Mesh
from jax.sharding import PartitionSpec as P

HEAD = 128
PATCH = 8
SEQ = ("seq_0", "seq_1", "seq_2")
SEQ_GRP = ("seq_0", "seq_1", "seq_2", "grp")
CHIPS = ("seq_0", "seq_1")

EPSILON = 1e-05
FLOOR = -1e30
SCALE = HEAD ** (-0.5)
LOG2E = 1.4426950408889634
MIB = 2**20

BF16 = jnp.bfloat16
F32 = jnp.float32

NT = (((1,), (1,)), ((), ()))
NN = (((1,), (0,)), ((), ()))


def dot(a, b, dims=NN):
    return lax.dot_general(a, b, dims, preferred_element_type=F32)


WIDE = 256


def own_plan(rows):
    plan = []
    base = 0
    for first in range(0, rows, WIDE):
        pieces = [(at, WIDE, "causal" if at == first else "all") for at in range(0, first + WIDE, WIDE)]
        plan.append((first, base, first + WIDE, pieces))
        base += first + WIDE
    return plan, base


def other_plan(rows, block):
    plan = []
    base = 0
    for first in range(0, rows, WIDE):
        lowest, highest = first // block, (first + WIDE - 1) // block
        keys = min(rows, 2 * block * ((highest + 2) // 2))
        pieces = []
        for at in range(0, keys, block):
            part = at // block
            kind = "all" if part < lowest else "block" if part <= highest else "none"
            pieces.append((at, block, kind))
        plan.append((first, base, keys, pieces))
        base += keys
    return plan, base


def flat_rows(ref, at, target):
    block = ref.shape[2]
    for j in range(ref.shape[0]):
        target[pl.ds(j * block, block)] = ref[j, at]


def turned_rows(ref, at, target):
    block = ref.shape[2]
    for j in range(0, ref.shape[0], 2):
        two = jnp.concatenate([ref[j, at], ref[j + 1, at]], 0)
        target[:, pl.ds(j * block, 2 * block)] = two.T


def query_chunk(ref, first):
    block = ref.shape[2]
    found = []
    at = first
    while at < first + WIDE:
        stop = min(first + WIDE, (at // block + 1) * block)
        found.append(ref[at // block, 0, pl.ds(at % block, stop - at)])
        at = stop
    return jnp.concatenate(found, 0)


def piece_scores(queries, first, pieces, key_s, score_s, core):
    top = None
    for at, size, kind in pieces:
        if kind == "none":
            continue
        score = dot(key_s[pl.ds(at, size)], queries, NT)
        if kind == "causal":
            key_at = lax.broadcasted_iota(jnp.int32, score.shape, 0)
            query_at = lax.broadcasted_iota(jnp.int32, score.shape, 1)
            score = jnp.where(key_at <= query_at, score, FLOOR)
        elif kind == "block":
            row = first + lax.broadcasted_iota(jnp.int32, (1, WIDE), 1)
            shown = row >= size * (at // size + 1 - core)
            score = jnp.where(shown, score, FLOOR)
        score_s[pl.ds(at, size)] = score
        piece_top = jnp.max(score, axis=0, keepdims=True)
        top = piece_top if top is None else jnp.maximum(top, piece_top)
    return top


def piece_chances(shift, base, pieces, score_s, kept_ref):
    total = jnp.zeros((1, WIDE), F32)
    for at, size, kind in pieces:
        kept = pl.ds(base + at, size)
        if kind == "none":
            kept_ref[kept] = jnp.zeros((size, WIDE), BF16)
            continue
        chance = jnp.exp2(score_s[pl.ds(at, size)] * (SCALE * LOG2E) - shift)
        total = total + jnp.sum(chance, axis=0, keepdims=True)
        kept_ref[kept] = chance.astype(BF16)
    return total


def forward_own(plan, own_ref, load_ref, kept_ref, mixed_ref, stats_ref, loaded_ref, key_s, turned_s, score_s, sem):
    load = pltpu.make_async_copy(load_ref, loaded_ref, sem)
    load.start()
    flat_rows(own_ref, 1, key_s)
    turned_rows(own_ref, 2, turned_s)
    for i, (first, base, keys, pieces) in enumerate(plan):
        top = piece_scores(query_chunk(own_ref, first), first, pieces, key_s, score_s, None)
        shift = top * (SCALE * LOG2E)
        total = piece_chances(shift, base, pieces, score_s, kept_ref)
        mixed_ref[i] = dot(turned_s[:, :keys], kept_ref[pl.ds(base, keys)])
        stats_ref[i, 0:1] = shift
        stats_ref[i, 1:2] = total
    load.wait()


def forward_other(
    plan,
    facts_ref,
    own_ref,
    other_ref,
    mixed_ref,
    stats_ref,
    load_ref,
    kept_ref,
    out_ref,
    own_inverse_ref,
    inverse_ref,
    loaded_ref,
    key_s,
    turned_s,
    score_s,
    sem,
):
    load = pltpu.make_async_copy(load_ref, loaded_ref, sem)
    load.start()
    flat_rows(other_ref, 0, key_s)
    turned_rows(other_ref, 1, turned_s)
    core = facts_ref[2]
    for i, (first, base, keys, pieces) in enumerate(plan):
        top = piece_scores(query_chunk(own_ref, first), first, pieces, key_s, score_s, core)
        own_shift = stats_ref[i, 0:1]
        shift = jnp.maximum(top * (SCALE * LOG2E), own_shift)
        total = piece_chances(shift, base, pieces, score_s, kept_ref)
        own_part = jnp.exp2(own_shift - shift)
        total = total + own_part * stats_ref[i, 1:2]
        mixed = mixed_ref[i] * own_part + dot(turned_s[:, :keys], kept_ref[pl.ds(base, keys)])
        inverse = 1.0 / total
        rows = pl.ds(first, WIDE)
        out_ref[rows] = (mixed * inverse).T.astype(BF16)
        inverse_ref[rows] = jnp.broadcast_to(inverse, (HEAD, WIDE)).T
        own_inverse_ref[rows] = jnp.broadcast_to(own_part * inverse, (HEAD, WIDE)).T
    load.wait()


def backward_side(
    plan, key_at, own_ref, side_ref, mixed_ref, inverse_ref, kept_ref, grad_ref, key_sum, value_sum, value_s, turned_s,
    slope_s,
):
    flat_rows(side_ref, key_at + 1, value_s)
    turned_rows(side_ref, key_at, turned_s)
    reached = 0
    for i, (first, base, keys, pieces) in enumerate(plan):
        queries = query_chunk(own_ref, first)
        rows = pl.ds(first, WIDE)
        grads = (grad_ref[rows].astype(F32) * inverse_ref[rows]).astype(BF16)
        product = grads.astype(F32) * mixed_ref[rows].astype(F32)
        row_dot = jnp.sum(product.T, axis=0, keepdims=True)
        for at, size, kind in pieces:
            spot = pl.ds(at, size)
            if kind == "none":
                slope_s[spot] = jnp.zeros((size, WIDE), BF16)
                continue
            kept = kept_ref[pl.ds(base + at, size)]
            chance_grad = dot(value_s[spot], grads, NT)
            slope = (kept.astype(F32) * (chance_grad - row_dot)).astype(BF16)
            slope_s[spot] = slope
            value_part = dot(kept, grads)
            key_part = dot(slope, queries)
            if at >= reached:
                reached = at + size
                value_sum[spot] = value_part
                key_sum[spot] = key_part
            else:
                value_sum[spot] += value_part
                key_sum[spot] += key_part
        yield i, dot(turned_s[:, :keys], slope_s[pl.ds(0, keys)])


def backward_other(
    plan, own_ref, other_ref, mixed_ref, inverse_ref, kept_ref, grad_ref, pair_ref, query_ref, key_sum, value_sum,
    value_s, turned_s, slope_s,
):
    for i, turned in backward_side(
        plan, 0, own_ref, other_ref, mixed_ref, inverse_ref, kept_ref, grad_ref, key_sum, value_sum, value_s, turned_s,
        slope_s,
    ):
        query_ref[i] = turned
    parts, _, block, _ = other_ref.shape
    for j in range(parts):
        rows = pl.ds(j * block, block)
        pair_ref[j, 0] = (key_sum[rows] * SCALE).astype(BF16)
        pair_ref[j, 1] = value_sum[rows].astype(BF16)


def backward_own(
    plan, own_ref, mixed_ref, inverse_ref, kept_ref, grad_ref, turned_ref, query_ref, key_ref, value_ref, value_s,
    turned_s, slope_s,
):
    for i, turned in backward_side(
        plan, 1, own_ref, own_ref, mixed_ref, inverse_ref, kept_ref, grad_ref, key_ref, value_ref, value_s, turned_s,
        slope_s,
    ):
        first = plan[i][0]
        query_ref[pl.ds(first, WIDE)] = ((turned + turned_ref[i]) * SCALE).T.astype(BF16)


def join_kernel(query_ref, key_ref, value_ref, pair_ref, out_ref):
    parts, _, block, _ = out_ref.shape
    for j in range(parts):
        rows = pl.ds(j * block, block)
        out_ref[j, 0] = query_ref[rows]
        out_ref[j, 1] = (key_ref[rows] * SCALE + pair_ref[j, 0].astype(F32)).astype(BF16)
        out_ref[j, 2] = (value_ref[rows] + pair_ref[j, 1].astype(F32)).astype(BF16)


def pack_kernel(*refs):
    arrays, out_ref, held_ref, in_sems, out_sems = refs[:-4], refs[-4], refs[-3], refs[-2], refs[-1]
    heads = out_ref.shape[0]
    loads = [pltpu.make_async_copy(ref, held_ref.at[t], in_sems.at[t]) for t, ref in enumerate(arrays)]
    for load in loads:
        load.start()
    stores = []
    for t, load in enumerate(loads):
        load.wait()
        for h in range(heads):
            source = held_ref.at[t, :, pl.ds(h * HEAD, HEAD)]
            stores.append(pltpu.make_async_copy(source, out_ref.at[h, t], out_sems.at[len(stores)]))
            stores[-1].start()
    for store in stores:
        store.wait()


def unpack_kernel(facts_ref, stack_ref, losses_ref, *refs):
    arrays, loss_ref, turned_s, sems = refs[:-3], refs[-3], refs[-2], refs[-1]
    copies = []
    for t, ref in enumerate(arrays):
        for h in range(stack_ref.shape[0]):
            target = ref.at[:, pl.ds(h * HEAD, HEAD)]
            copies.append(pltpu.make_async_copy(stack_ref.at[h, t], target, sems.at[len(copies)]))
            copies[-1].start()
    slots = loss_ref.shape[1]
    turned_s[...] = losses_ref[...].T
    loss_ref[...] = turned_s[pl.ds(pl.multiple_of(facts_ref[0] * slots, 8), slots)].T
    for copy in copies:
        copy.wait()


def turn_kernel(up_ref, down_ref, up_out, down_out):
    up_out[...] = up_ref[...].T
    down_out[...] = down_ref[...].T


GELU_A = 0.7978845608028654
GELU_B = 0.044715


def byte_kernel(
    pieces,
    facts_ref,
    rows_ref,
    ids_ref,
    order_ref,
    embed_ref,
    gain_ref,
    up_ref,
    down_ref,
    up_turned_ref,
    down_turned_ref,
    vocab_ref,
    grad_ref,
    loss_ref,
    bend_s,
):
    heads, count, _ = rows_ref.shape
    size = up_ref.shape[1] // pieces
    place = facts_ref[0]
    ids = ids_ref[...].T
    lane = lax.broadcasted_iota(jnp.int32, ids.shape, 1)
    target = jnp.sum(jnp.where(lane == place, ids, 0), axis=1, keepdims=True)
    previous = jnp.sum(jnp.where(lane == place - 1, ids, 0), axis=1, keepdims=True)
    letters = lax.broadcasted_iota(jnp.int32, (count, vocab_ref.shape[1]), 1)
    live = jnp.where(place > 0, 1.0, 0.0)
    one_hot = jnp.where(previous == letters, live, 0.0).astype(BF16)
    hidden_in = jnp.concatenate([rows_ref[h].astype(F32) for h in range(heads)], 1)
    hidden_in = hidden_in + dot(one_hot, embed_ref[...])
    inverse_rms = lax.rsqrt(jnp.mean(hidden_in * hidden_in, axis=1, keepdims=True) + EPSILON)
    gain = gain_ref[...]
    normed = (hidden_in * inverse_rms * gain).astype(BF16)
    after = hidden_in
    for i in range(pieces):
        part = pl.ds(i * size, size)
        raised = dot(normed, up_ref[:, part])
        square = raised * raised
        half = 0.5 + 0.5 * jnp.tanh(raised * (GELU_A + (GELU_A * GELU_B) * square))
        active = (raised * half).astype(BF16)
        bend_s[:, part] = half + half * (1.0 - half) * raised * (
            2.0 * GELU_A + (6.0 * GELU_A * GELU_B) * square
        )
        after = after + dot(active, down_ref[part])
    final_scale = lax.rsqrt(jnp.mean(after * after, axis=1, keepdims=True) + EPSILON)
    final_rows = (after * final_scale).astype(BF16)
    logits = dot(final_rows, vocab_ref[...])
    row_top = jnp.max(logits, axis=1, keepdims=True)
    raised_mass = jnp.exp(logits - row_top)
    mass = jnp.sum(raised_mass, axis=1, keepdims=True)
    is_target = target == letters
    chosen = jnp.sum(jnp.where(is_target, logits, 0.0), axis=1, keepdims=True)
    loss = jnp.log(mass) + row_top - chosen
    row_at = lax.broadcasted_iota(jnp.int32, (count, count), 0)
    ordered = jnp.sum(jnp.where(row_at == order_ref[...] - facts_ref[1], loss, 0.0), axis=0, keepdims=True)
    slot = lax.broadcasted_iota(jnp.int32, loss_ref.shape, 0)
    loss_ref[...] = jnp.where(slot == place, ordered, 0.0)
    logit_grad = raised_mass / mass - jnp.where(is_target, 1.0, 0.0)
    final_grad = dot(logit_grad.astype(BF16), vocab_ref[...], NT).astype(BF16).astype(F32)
    mean_dot = jnp.mean(final_grad * after, axis=1, keepdims=True)
    after_grad = final_scale * final_grad - after * (final_scale * final_scale * final_scale * mean_dot)
    narrow = after_grad.astype(BF16)
    normed_grad = None
    for i in range(pieces):
        part = pl.ds(i * size, size)
        active_grad = dot(narrow, down_turned_ref[:, part]).astype(BF16).astype(F32)
        raised_grad = (active_grad * bend_s[:, part]).astype(BF16)
        term = dot(raised_grad, up_turned_ref[part])
        normed_grad = term if normed_grad is None else normed_grad + term
    scaled = normed_grad.astype(BF16).astype(F32) * gain
    mean_dot = jnp.mean(scaled * hidden_in, axis=1, keepdims=True)
    total = (
        after_grad
        + inverse_rms * scaled
        - hidden_in * (inverse_rms * inverse_rms * inverse_rms * mean_dot)
    ).astype(BF16)
    for h in range(heads):
        grad_ref[h] = total[:, h * HEAD : (h + 1) * HEAD]


def vmem():
    return pl.BlockSpec(memory_space=pltpu.VMEM)


def far():
    return pl.BlockSpec(memory_space=pltpu.HBM)


def smem():
    return pl.BlockSpec(memory_space=pltpu.SMEM)


def held(dims, kind=BF16):
    return pltpu.VMEM(dims, kind)


def shape(dims, kind=BF16):
    return jax.ShapeDtypeStruct(dims, kind)


def exchange(value):
    return lax.all_to_all(value, CHIPS, split_axis=0, concat_axis=0, tiled=True)


def gather_losses(value, bit):
    return value + lax.ppermute(value, "grp", [(i, i ^ (1 << bit)) for i in range(PATCH)])


def swap_cores(value):
    return lax.ppermute(value, "seq_2", [(0, 1), (1, 0)])


def anywhere():
    return pl.BlockSpec(memory_space=pl.ANY)


def kernel_call(body, name, outs, ins, out_specs, scratch, grant, flops, transcendentals=0, moved=4 * MIB):
    return pl.pallas_call(
        body,
        out_shape=outs,
        in_specs=ins,
        out_specs=out_specs,
        scratch_shapes=scratch,
        compiler_params=pltpu.CompilerParams(vmem_limit_bytes=grant * MIB),
        cost_estimate=pl.CostEstimate(
            flops=flops, bytes_accessed=moved, transcendentals=transcendentals
        ),
        name=name,
    )


def shards(
    byte_ids,
    patch_order,
    query_rows,
    key_rows,
    value_rows,
    byte_embed,
    norm_gain,
    w_up,
    w_down,
    vocab_head,
):
    count, columns = query_rows.shape
    hidden = w_up.shape[1]
    heads = columns // HEAD
    rows = heads * count
    chunks = rows // WIDE
    seq_here = lax.axis_index(SEQ)
    place = lax.axis_index("grp").astype(jnp.int32)
    core = lax.axis_index("seq_2").astype(jnp.int32)
    facts = jnp.stack([place, seq_here * count, core])
    query_rows, facts = lax.optimization_barrier((query_rows, facts))
    near_plan, near_rows = own_plan(rows)
    far_plan, far_rows = other_plan(rows, count)

    query_rows, key_rows, value_rows = (
        pltpu.with_memory_space_constraint(a, pltpu.HBM) for a in (query_rows, key_rows, value_rows)
    )
    stacked = kernel_call(
        pack_kernel,
        "pack",
        shape((heads, 3, count, HEAD)),
        [far()] * 3,
        anywhere(),
        [
            pltpu.VMEM((3, count, columns), BF16),
            pltpu.SemaphoreType.DMA((3,)),
            pltpu.SemaphoreType.DMA((3 * heads,)),
        ],
        4,
        0,
    )(query_rows, key_rows, value_rows)
    own = exchange(stacked)

    size = 512
    w_up = pltpu.with_memory_space_constraint(w_up, pltpu.HBM)
    w_down = pltpu.with_memory_space_constraint(w_down, pltpu.HBM)
    wide_block = pl.BlockSpec((columns, size), lambda i: (0, i))
    tall_block = pl.BlockSpec((size, columns), lambda i: (i, 0))
    turned = pl.pallas_call(
        turn_kernel,
        out_shape=(pltpu.HBM((hidden, columns), BF16), pltpu.HBM((columns, hidden), BF16)),
        grid=(hidden // size,),
        in_specs=[wide_block, tall_block],
        out_specs=(tall_block, wide_block),
        compiler_params=pltpu.CompilerParams(vmem_limit_bytes=12 * MIB),
        cost_estimate=pl.CostEstimate(flops=0, bytes_accessed=32 * MIB, transcendentals=0),
        name="turn_weights",
    )(w_up, w_down)
    own, turned = lax.optimization_barrier((own, turned))
    other = swap_cores(own[:, 1:])

    kv_scratch = [pltpu.VMEM((rows, HEAD), BF16), pltpu.VMEM((HEAD, rows), BF16)]
    near_kept, near_mixed, stats, up_held = kernel_call(
        functools.partial(forward_own, near_plan),
        "forward_own",
        (
            held((near_rows, WIDE)),
            held((chunks, HEAD, WIDE), F32),
            held((chunks, 8, WIDE), F32),
            held(w_up.shape),
        ),
        [vmem(), far()],
        (vmem(),) * 4,
        kv_scratch + [pltpu.VMEM((rows, WIDE), F32), pltpu.SemaphoreType.DMA],
        8,
        4 * near_rows * WIDE * HEAD,
        near_rows * WIDE,
    )(own, w_up)
    far_kept, attended, near_inverse, far_inverse, down_held = kernel_call(
        functools.partial(forward_other, far_plan),
        "forward_other",
        (
            held((far_rows, WIDE)),
            held((rows, HEAD)),
            held((rows, HEAD), F32),
            held((rows, HEAD), F32),
            held(w_down.shape),
        ),
        [smem()] + [vmem()] * 4 + [far()],
        (vmem(),) * 5,
        kv_scratch + [pltpu.VMEM((rows, WIDE), F32), pltpu.SemaphoreType.DMA],
        8,
        4 * far_rows * WIDE * HEAD,
        far_rows * WIDE,
    )(facts, own, other, near_mixed, stats, w_down)

    byte_pieces = 4
    owned_rows = exchange(attended.reshape(heads, count, HEAD))
    context_grad, losses = kernel_call(
        functools.partial(byte_kernel, byte_pieces),
        "byte_layer",
        (shape((heads, count, HEAD)), shape((PATCH, count), F32)),
        [smem()] + [vmem()] * 10,
        (vmem(), vmem()),
        [pltpu.VMEM((count, hidden), F32)],
        14,
        8 * count * columns * hidden,
        count * hidden,
    )(
        facts,
        owned_rows,
        byte_ids.T,
        patch_order[None],
        byte_embed,
        norm_gain[None],
        up_held,
        down_held,
        *turned,
        vocab_head,
    )

    grad_rows, losses = lax.optimization_barrier((exchange(context_grad), losses))
    grad_rows = grad_rows.reshape(rows, HEAD)
    side_scratch = kv_scratch + [pltpu.VMEM((rows, WIDE), BF16)]
    sums = [pltpu.VMEM((rows, HEAD), F32)] * 2
    pair_grad, turned_grad = kernel_call(
        functools.partial(backward_other, far_plan),
        "backward_other",
        (shape((heads, 2, count, HEAD)), shape((chunks, HEAD, WIDE), F32)),
        [vmem()] * 6,
        (vmem(), vmem()),
        sums + side_scratch,
        8,
        8 * far_rows * WIDE * HEAD,
    )(own, other, attended, far_inverse, far_kept, grad_rows)
    pair_grad, turned_grad, losses = lax.optimization_barrier((pair_grad, turned_grad, gather_losses(losses, 0)))
    pair_sent = swap_cores(pair_grad)
    query_grad, key_grad, value_grad = kernel_call(
        functools.partial(backward_own, near_plan),
        "backward_own",
        (shape((rows, HEAD)), shape((rows, HEAD), F32), shape((rows, HEAD), F32)),
        [vmem()] * 6,
        (vmem(), vmem(), vmem()),
        side_scratch,
        8,
        8 * near_rows * WIDE * HEAD,
    )(own, attended, near_inverse, near_kept, grad_rows, turned_grad)
    query_grad, losses = lax.optimization_barrier((query_grad, gather_losses(losses, 1)))
    joined = kernel_call(
        join_kernel,
        "join",
        shape((heads, 3, count, HEAD)),
        [vmem()] * 4,
        vmem(),
        [],
        4,
        0,
    )(query_grad, key_grad, value_grad, pair_sent)
    back = exchange(joined)
    losses = gather_losses(losses, 2)
    query_out, key_out, value_out, byte_loss = kernel_call(
        unpack_kernel,
        "unpack",
        (shape((count, columns)),) * 3 + (shape((PATCH, count // PATCH), F32),),
        [smem(), anywhere(), vmem()],
        (anywhere(),) * 3 + (vmem(),),
        [pltpu.VMEM((count, PATCH), F32), pltpu.SemaphoreType.DMA((3 * heads,))],
        2,
        0,
    )(facts, back, losses)
    return byte_loss.T, query_out, key_out, value_out


def solution(mesh):
    torus = Mesh(
        mesh.devices.reshape(4, 2, 2, mesh.shape["grp"]), ("seq_0", "seq_1", "seq_2", "grp")
    )
    placed = (
        P(SEQ, None),
        P(SEQ),
        P(SEQ, "grp"),
        P(SEQ, "grp"),
        P(SEQ, "grp"),
        P(),
        P(),
        P(),
        P(),
        P(),
    )
    return jax.shard_map(
        shards,
        mesh=torus,
        in_specs=placed,
        out_specs=(P(SEQ_GRP, None), P(SEQ, "grp"), P(SEQ, "grp"), P(SEQ, "grp")),
        check_vma=False,
    )
```

```python
import functools

import jax
import jax.numpy as jnp
from jax import lax
from jax.experimental import pallas as pl
from jax.experimental.pallas import tpu as pltpu
from jax.sharding import Mesh
from jax.sharding import PartitionSpec as P

HEAD = 128
PATCH = 8
SEQ = ("seq_0", "seq_1", "seq_2")
SEQ_GRP = ("seq_0", "seq_1", "seq_2", "grp")
CHIPS = ("seq_0", "seq_1")

EPSILON = 1e-05
FLOOR = -1e30
SCALE = HEAD ** (-0.5)
LOG2E = 1.4426950408889634
MIB = 2**20

BF16 = jnp.bfloat16
F32 = jnp.float32

NT = (((1,), (1,)), ((), ()))
NN = (((1,), (0,)), ((), ()))


def dot(a, b, dims=NN):
    return lax.dot_general(a, b, dims, preferred_element_type=F32)


WIDE = 256


def own_plan(rows):
    plan = []
    base = 0
    for first in range(0, rows, WIDE):
        pieces = [(at, WIDE, "causal" if at == first else "all") for at in range(0, first + WIDE, WIDE)]
        plan.append((first, base, first + WIDE, pieces))
        base += first + WIDE
    return plan, base


def other_plan(rows, block):
    plan = []
    base = 0
    for first in range(0, rows, WIDE):
        lowest, highest = first // block, (first + WIDE - 1) // block
        keys = min(rows, 2 * block * ((highest + 2) // 2))
        pieces = []
        for at in range(0, keys, block):
            part = at // block
            kind = "all" if part < lowest else "block" if part <= highest else "none"
            pieces.append((at, block, kind))
        plan.append((first, base, keys, pieces))
        base += keys
    return plan, base


def flat_rows(ref, at, target):
    block = ref.shape[2]
    for j in range(ref.shape[0]):
        target[pl.ds(j * block, block)] = ref[j, at]


def turned_rows(ref, at, target):
    block = ref.shape[2]
    for j in range(0, ref.shape[0], 2):
        two = jnp.concatenate([ref[j, at], ref[j + 1, at]], 0)
        target[:, pl.ds(j * block, 2 * block)] = two.T


def query_chunk(ref, first):
    block = ref.shape[2]
    found = []
    at = first
    while at < first + WIDE:
        stop = min(first + WIDE, (at // block + 1) * block)
        found.append(ref[at // block, 0, pl.ds(at % block, stop - at)])
        at = stop
    return jnp.concatenate(found, 0)


def piece_scores(queries, first, pieces, key_s, score_s, core):
    top = None
    for at, size, kind in pieces:
        if kind == "none":
            continue
        score = dot(key_s[pl.ds(at, size)], queries, NT)
        if kind == "causal":
            key_at = lax.broadcasted_iota(jnp.int32, score.shape, 0)
            query_at = lax.broadcasted_iota(jnp.int32, score.shape, 1)
            score = jnp.where(key_at <= query_at, score, FLOOR)
        elif kind == "block":
            row = first + lax.broadcasted_iota(jnp.int32, (1, WIDE), 1)
            shown = row >= size * (at // size + 1 - core)
            score = jnp.where(shown, score, FLOOR)
        score_s[pl.ds(at, size)] = score
        piece_top = jnp.max(score, axis=0, keepdims=True)
        top = piece_top if top is None else jnp.maximum(top, piece_top)
    return top


def piece_chances(shift, base, pieces, score_s, kept_ref):
    total = jnp.zeros((1, WIDE), F32)
    for at, size, kind in pieces:
        kept = pl.ds(base + at, size)
        if kind == "none":
            kept_ref[kept] = jnp.zeros((size, WIDE), BF16)
            continue
        chance = jnp.exp2(score_s[pl.ds(at, size)] * (SCALE * LOG2E) - shift)
        total = total + jnp.sum(chance, axis=0, keepdims=True)
        kept_ref[kept] = chance.astype(BF16)
    return total


def forward_own(plan, own_ref, load_ref, kept_ref, mixed_ref, stats_ref, loaded_ref, key_s, turned_s, score_s, sem):
    load = pltpu.make_async_copy(load_ref, loaded_ref, sem)
    load.start()
    flat_rows(own_ref, 1, key_s)
    turned_rows(own_ref, 2, turned_s)
    for i, (first, base, keys, pieces) in enumerate(plan):
        top = piece_scores(query_chunk(own_ref, first), first, pieces, key_s, score_s, None)
        shift = top * (SCALE * LOG2E)
        total = piece_chances(shift, base, pieces, score_s, kept_ref)
        mixed_ref[i] = dot(turned_s[:, :keys], kept_ref[pl.ds(base, keys)])
        stats_ref[i, 0:1] = shift
        stats_ref[i, 1:2] = total
    load.wait()


def forward_other(
    plan,
    facts_ref,
    own_ref,
    other_ref,
    mixed_ref,
    stats_ref,
    kept_ref,
    out_ref,
    own_inverse_ref,
    inverse_ref,
    key_s,
    turned_s,
    score_s,
):
    flat_rows(other_ref, 0, key_s)
    turned_rows(other_ref, 1, turned_s)
    core = facts_ref[2]
    for i, (first, base, keys, pieces) in enumerate(plan):
        top = piece_scores(query_chunk(own_ref, first), first, pieces, key_s, score_s, core)
        own_shift = stats_ref[i, 0:1]
        shift = jnp.maximum(top * (SCALE * LOG2E), own_shift)
        total = piece_chances(shift, base, pieces, score_s, kept_ref)
        own_part = jnp.exp2(own_shift - shift)
        total = total + own_part * stats_ref[i, 1:2]
        mixed = mixed_ref[i] * own_part + dot(turned_s[:, :keys], kept_ref[pl.ds(base, keys)])
        inverse = 1.0 / total
        rows = pl.ds(first, WIDE)
        out_ref[rows] = (mixed * inverse).T.astype(BF16)
        inverse_ref[rows] = jnp.broadcast_to(inverse, (HEAD, WIDE)).T
        own_inverse_ref[rows] = jnp.broadcast_to(own_part * inverse, (HEAD, WIDE)).T


def backward_side(
    plan, key_at, own_ref, side_ref, mixed_ref, inverse_ref, kept_ref, grad_ref, key_sum, value_sum, value_s, turned_s,
    slope_s,
):
    flat_rows(side_ref, key_at + 1, value_s)
    turned_rows(side_ref, key_at, turned_s)
    reached = 0
    for i, (first, base, keys, pieces) in enumerate(plan):
        queries = query_chunk(own_ref, first)
        rows = pl.ds(first, WIDE)
        grads = (grad_ref[rows].astype(F32) * inverse_ref[rows]).astype(BF16)
        product = grads.astype(F32) * mixed_ref[rows].astype(F32)
        row_dot = jnp.sum(product.T, axis=0, keepdims=True)
        for at, size, kind in pieces:
            spot = pl.ds(at, size)
            if kind == "none":
                slope_s[spot] = jnp.zeros((size, WIDE), BF16)
                continue
            kept = kept_ref[pl.ds(base + at, size)]
            chance_grad = dot(value_s[spot], grads, NT)
            slope = (kept.astype(F32) * (chance_grad - row_dot)).astype(BF16)
            slope_s[spot] = slope
            value_part = dot(kept, grads)
            key_part = dot(slope, queries)
            if at >= reached:
                reached = at + size
                value_sum[spot] = value_part
                key_sum[spot] = key_part
            else:
                value_sum[spot] += value_part
                key_sum[spot] += key_part
        yield i, dot(turned_s[:, :keys], slope_s[pl.ds(0, keys)])


def backward_other(
    plan, own_ref, other_ref, mixed_ref, inverse_ref, kept_ref, grad_ref, pair_ref, query_ref, key_sum, value_sum,
    value_s, turned_s, slope_s,
):
    for i, turned in backward_side(
        plan, 0, own_ref, other_ref, mixed_ref, inverse_ref, kept_ref, grad_ref, key_sum, value_sum, value_s, turned_s,
        slope_s,
    ):
        query_ref[i] = turned
    parts, _, block, _ = other_ref.shape
    for j in range(parts):
        rows = pl.ds(j * block, block)
        pair_ref[j, 0] = (key_sum[rows] * SCALE).astype(BF16)
        pair_ref[j, 1] = value_sum[rows].astype(BF16)


def backward_own(
    plan, own_ref, mixed_ref, inverse_ref, kept_ref, grad_ref, turned_ref, query_ref, key_ref, value_ref, value_s,
    turned_s, slope_s,
):
    for i, turned in backward_side(
        plan, 1, own_ref, own_ref, mixed_ref, inverse_ref, kept_ref, grad_ref, key_ref, value_ref, value_s, turned_s,
        slope_s,
    ):
        first = plan[i][0]
        query_ref[pl.ds(first, WIDE)] = ((turned + turned_ref[i]) * SCALE).T.astype(BF16)


def join_kernel(query_ref, key_ref, value_ref, pair_ref, out_ref):
    parts, _, block, _ = out_ref.shape
    for j in range(parts):
        rows = pl.ds(j * block, block)
        out_ref[j, 0] = query_ref[rows]
        out_ref[j, 1] = (key_ref[rows] * SCALE + pair_ref[j, 0].astype(F32)).astype(BF16)
        out_ref[j, 2] = (value_ref[rows] + pair_ref[j, 1].astype(F32)).astype(BF16)


def pack_kernel(*refs):
    arrays, out_ref, held_ref, in_sems, out_sems = refs[:-4], refs[-4], refs[-3], refs[-2], refs[-1]
    heads = out_ref.shape[0]
    loads = [pltpu.make_async_copy(ref, held_ref.at[t], in_sems.at[t]) for t, ref in enumerate(arrays)]
    for load in loads:
        load.start()
    stores = []
    for t, load in enumerate(loads):
        load.wait()
        for h in range(heads):
            source = held_ref.at[t, :, pl.ds(h * HEAD, HEAD)]
            stores.append(pltpu.make_async_copy(source, out_ref.at[h, t], out_sems.at[len(stores)]))
            stores[-1].start()
    for store in stores:
        store.wait()


def unpack_kernel(facts_ref, stack_ref, losses_ref, *refs):
    arrays, loss_ref, turned_s, loss_s, sems = refs[:-4], refs[-4], refs[-3], refs[-2], refs[-1]
    copies = []
    for t, ref in enumerate(arrays):
        for h in range(stack_ref.shape[0]):
            target = ref.at[:, pl.ds(h * HEAD, HEAD)]
            copies.append(pltpu.make_async_copy(stack_ref.at[h, t], target, sems.at[len(copies)]))
            copies[-1].start()
    slots = loss_ref.shape[1]
    turned_s[...] = losses_ref[...].T
    loss_s[...] = turned_s[pl.ds(pl.multiple_of(facts_ref[0] * slots, 8), slots)].T
    copies.append(pltpu.make_async_copy(loss_s, loss_ref, sems.at[len(copies)]))
    copies[-1].start()
    for copy in copies:
        copy.wait()


GELU_A = 0.7978845608028654
GELU_B = 0.044715


def byte_forward(
    pieces,
    facts_ref,
    rows_ref,
    ids_ref,
    order_ref,
    embed_ref,
    gain_ref,
    up_ref,
    down_ref,
    vocab_ref,
    loss_ref,
    bend_ref,
    hidden_ref,
    scale_ref,
    grad_ref,
):
    heads, count, _ = rows_ref.shape
    size = up_ref.shape[1] // pieces
    place = facts_ref[0]
    ids = ids_ref[...].T
    lane = lax.broadcasted_iota(jnp.int32, ids.shape, 1)
    target = jnp.sum(jnp.where(lane == place, ids, 0), axis=1, keepdims=True)
    previous = jnp.sum(jnp.where(lane == place - 1, ids, 0), axis=1, keepdims=True)
    letters = lax.broadcasted_iota(jnp.int32, (count, vocab_ref.shape[1]), 1)
    live = jnp.where(place > 0, 1.0, 0.0)
    one_hot = jnp.where(previous == letters, live, 0.0).astype(BF16)
    hidden_in = jnp.concatenate([rows_ref[h].astype(F32) for h in range(heads)], 1)
    hidden_in = hidden_in + dot(one_hot, embed_ref[...])
    inverse_rms = lax.rsqrt(jnp.mean(hidden_in * hidden_in, axis=1, keepdims=True) + EPSILON)
    normed = (hidden_in * inverse_rms * gain_ref[...]).astype(BF16)
    hidden_ref[...] = hidden_in
    scale_ref[...] = jnp.broadcast_to(inverse_rms, scale_ref.shape)
    after = hidden_in
    for i in range(pieces):
        part = pl.ds(i * size, size)
        raised = dot(normed, up_ref[:, part])
        square = raised * raised
        half = 0.5 + 0.5 * jnp.tanh(raised * (GELU_A + (GELU_A * GELU_B) * square))
        active = (raised * half).astype(BF16)
        bend_ref[:, part] = half + half * (1.0 - half) * raised * (
            2.0 * GELU_A + (6.0 * GELU_A * GELU_B) * square
        )
        after = after + dot(active, down_ref[part])
    final_scale = lax.rsqrt(jnp.mean(after * after, axis=1, keepdims=True) + EPSILON)
    final_rows = (after * final_scale).astype(BF16)
    logits = dot(final_rows, vocab_ref[...])
    row_top = jnp.max(logits, axis=1, keepdims=True)
    raised_mass = jnp.exp(logits - row_top)
    mass = jnp.sum(raised_mass, axis=1, keepdims=True)
    is_target = target == letters
    chosen = jnp.sum(jnp.where(is_target, logits, 0.0), axis=1, keepdims=True)
    loss = jnp.log(mass) + row_top - chosen
    row_at = lax.broadcasted_iota(jnp.int32, (count, count), 0)
    ordered = jnp.sum(
        jnp.where(row_at == order_ref[...] - facts_ref[1], loss, 0.0), axis=0, keepdims=True
    )
    slot = lax.broadcasted_iota(jnp.int32, loss_ref.shape, 0)
    loss_ref[...] = jnp.where(slot == place, ordered, 0.0)
    logit_grad = raised_mass / mass - jnp.where(is_target, 1.0, 0.0)
    final_grad = dot(logit_grad.astype(BF16), vocab_ref[...], NT).astype(BF16).astype(F32)
    mean_dot = jnp.mean(final_grad * after, axis=1, keepdims=True)
    grad_ref[...] = final_scale * final_grad - after * (
        final_scale * final_scale * final_scale * mean_dot
    )


def byte_backward(pieces, gain_ref, up_ref, down_ref, bend_ref, hidden_ref, scale_ref, after_ref, grad_ref):
    heads, count, _ = grad_ref.shape
    size = up_ref.shape[1] // pieces
    after_grad = after_ref[...]
    narrow = after_grad.astype(BF16)
    normed_grad = None
    for i in range(pieces):
        part = pl.ds(i * size, size)
        active_grad = dot(narrow, down_ref[part], NT).astype(BF16).astype(F32)
        raised_grad = (active_grad * bend_ref[:, part]).astype(BF16)
        term = dot(raised_grad, up_ref[:, part], NT)
        normed_grad = term if normed_grad is None else normed_grad + term
    hidden_in = hidden_ref[...]
    inverse_rms = scale_ref[:, 0:1]
    scaled = normed_grad.astype(BF16).astype(F32) * gain_ref[...]
    mean_dot = jnp.mean(scaled * hidden_in, axis=1, keepdims=True)
    total = (
        after_grad
        + inverse_rms * scaled
        - hidden_in * (inverse_rms * inverse_rms * inverse_rms * mean_dot)
    ).astype(BF16)
    for h in range(heads):
        grad_ref[h] = total[:, h * HEAD : (h + 1) * HEAD]


def vmem():
    return pl.BlockSpec(memory_space=pltpu.VMEM)


def far():
    return pl.BlockSpec(memory_space=pltpu.HBM)


def smem():
    return pl.BlockSpec(memory_space=pltpu.SMEM)


def held(dims, kind=BF16):
    return pltpu.VMEM(dims, kind)


def shape(dims, kind=BF16):
    return jax.ShapeDtypeStruct(dims, kind)


def exchange(value):
    return lax.all_to_all(value, CHIPS, split_axis=0, concat_axis=0, tiled=True)


def gather_losses(value, bit):
    return value + lax.ppermute(value, "grp", [(i, i ^ (1 << bit)) for i in range(PATCH)])


def swap_cores(value):
    return lax.ppermute(value, "seq_2", [(0, 1), (1, 0)])


def anywhere():
    return pl.BlockSpec(memory_space=pl.ANY)


def kernel_call(body, name, outs, ins, out_specs, scratch, grant, flops, transcendentals=0, moved=4 * MIB):
    return pl.pallas_call(
        body,
        out_shape=outs,
        in_specs=ins,
        out_specs=out_specs,
        scratch_shapes=scratch,
        compiler_params=pltpu.CompilerParams(vmem_limit_bytes=grant * MIB),
        cost_estimate=pl.CostEstimate(
            flops=flops, bytes_accessed=moved, transcendentals=transcendentals
        ),
        name=name,
    )


def shards(
    byte_ids,
    patch_order,
    query_rows,
    key_rows,
    value_rows,
    byte_embed,
    norm_gain,
    w_up,
    w_down,
    vocab_head,
):
    count, columns = query_rows.shape
    hidden = w_up.shape[1]
    heads = columns // HEAD
    rows = heads * count
    chunks = rows // WIDE
    seq_here = lax.axis_index(SEQ)
    place = lax.axis_index("grp").astype(jnp.int32)
    core = lax.axis_index("seq_2").astype(jnp.int32)
    facts = jnp.stack([place, seq_here * count, core])
    query_rows, facts = lax.optimization_barrier((query_rows, facts))
    near_plan, near_rows = own_plan(rows)
    far_plan, far_rows = other_plan(rows, count)

    query_rows, key_rows, value_rows = (
        pltpu.with_memory_space_constraint(a, pltpu.HBM) for a in (query_rows, key_rows, value_rows)
    )
    stacked = kernel_call(
        pack_kernel,
        "pack",
        shape((heads, 3, count, HEAD)),
        [far()] * 3,
        anywhere(),
        [
            pltpu.VMEM((3, count, columns), BF16),
            pltpu.SemaphoreType.DMA((3,)),
            pltpu.SemaphoreType.DMA((3 * heads,)),
        ],
        4,
        0,
    )(query_rows, key_rows, value_rows)
    own = exchange(stacked)

    other = swap_cores(own[:, 1:])

    kv_scratch = [pltpu.VMEM((rows, HEAD), BF16), pltpu.VMEM((HEAD, rows), BF16)]
    near_kept, near_mixed, stats, down_held = kernel_call(
        functools.partial(forward_own, near_plan),
        "forward_own",
        (
            held((near_rows, WIDE)),
            held((chunks, HEAD, WIDE), F32),
            held((chunks, 8, WIDE), F32),
            held(w_down.shape),
        ),
        [vmem(), far()],
        (vmem(),) * 4,
        kv_scratch + [pltpu.VMEM((rows, WIDE), F32), pltpu.SemaphoreType.DMA],
        8,
        4 * near_rows * WIDE * HEAD,
        near_rows * WIDE,
    )(own, pltpu.with_memory_space_constraint(w_down, pltpu.HBM))
    far_kept, attended, near_inverse, far_inverse = kernel_call(
        functools.partial(forward_other, far_plan),
        "forward_other",
        (
            held((far_rows, WIDE)),
            held((rows, HEAD)),
            held((rows, HEAD), F32),
            held((rows, HEAD), F32),
        ),
        [smem()] + [vmem()] * 4,
        (vmem(),) * 4,
        kv_scratch + [pltpu.VMEM((rows, WIDE), F32)],
        8,
        4 * far_rows * WIDE * HEAD,
        far_rows * WIDE,
    )(facts, own, other, near_mixed, stats)

    byte_pieces = 4
    owned_rows = exchange(attended.reshape(heads, count, HEAD))
    gain = norm_gain[None]
    losses, bend, hidden_in, scale, after_grad = kernel_call(
        functools.partial(byte_forward, byte_pieces),
        "byte_forward",
        (
            shape((PATCH, count), F32),
            held((count, hidden), F32),
            held((count, columns), F32),
            held((count, HEAD), F32),
            held((count, columns), F32),
        ),
        [smem()] + [vmem()] * 8,
        (vmem(),) * 5,
        [],
        12,
        4 * count * columns * hidden,
        count * hidden,
    )(
        facts,
        owned_rows,
        byte_ids.T,
        patch_order[None],
        byte_embed,
        gain,
        w_up,
        down_held,
        vocab_head,
    )
    sent_losses = gather_losses(losses, 0)
    context_grad = kernel_call(
        functools.partial(byte_backward, byte_pieces),
        "byte_backward",
        held((heads, count, HEAD)),
        [vmem()] * 7,
        vmem(),
        [],
        12,
        4 * count * columns * hidden,
    )(gain, w_up, down_held, bend, hidden_in, scale, after_grad)
    context_grad, losses = lax.optimization_barrier((context_grad, sent_losses))
    grad_rows, losses = lax.optimization_barrier((exchange(context_grad), losses))
    grad_rows = grad_rows.reshape(rows, HEAD)
    side_scratch = kv_scratch + [pltpu.VMEM((rows, WIDE), BF16)]
    sums = [pltpu.VMEM((rows, HEAD), F32)] * 2
    pair_grad, turned_grad = kernel_call(
        functools.partial(backward_other, far_plan),
        "backward_other",
        (shape((heads, 2, count, HEAD)), shape((chunks, HEAD, WIDE), F32)),
        [vmem()] * 6,
        (vmem(), vmem()),
        sums + side_scratch,
        8,
        8 * far_rows * WIDE * HEAD,
    )(own, other, attended, far_inverse, far_kept, grad_rows)
    pair_grad, turned_grad, losses = lax.optimization_barrier((pair_grad, turned_grad, gather_losses(losses, 1)))
    pair_sent = swap_cores(pair_grad)
    query_grad, key_grad, value_grad = kernel_call(
        functools.partial(backward_own, near_plan),
        "backward_own",
        (shape((rows, HEAD)), shape((rows, HEAD), F32), shape((rows, HEAD), F32)),
        [vmem()] * 6,
        (vmem(), vmem(), vmem()),
        side_scratch,
        8,
        8 * near_rows * WIDE * HEAD,
    )(own, attended, near_inverse, near_kept, grad_rows, turned_grad)
    query_grad, losses = lax.optimization_barrier((query_grad, gather_losses(losses, 2)))
    joined = kernel_call(
        join_kernel,
        "join",
        shape((heads, 3, count, HEAD)),
        [vmem()] * 4,
        vmem(),
        [],
        4,
        0,
    )(query_grad, key_grad, value_grad, pair_sent)
    back = exchange(joined)
    query_out, key_out, value_out, byte_loss = kernel_call(
        unpack_kernel,
        "unpack",
        (shape((count, columns)),) * 3 + (shape((PATCH, count // PATCH), F32),),
        [smem(), anywhere(), vmem()],
        (anywhere(),) * 4,
        [
            pltpu.VMEM((count, PATCH), F32),
            pltpu.VMEM((PATCH, count // PATCH), F32),
            pltpu.SemaphoreType.DMA((3 * heads + 1,)),
        ],
        2,
        0,
    )(facts, back, losses)
    return byte_loss.T, query_out, key_out, value_out


def solution(mesh):
    torus = Mesh(
        mesh.devices.reshape(4, 2, 2, mesh.shape["grp"]), ("seq_0", "seq_1", "seq_2", "grp")
    )
    placed = (
        P(SEQ, None),
        P(SEQ),
        P(SEQ, "grp"),
        P(SEQ, "grp"),
        P(SEQ, "grp"),
        P(),
        P(),
        P(),
        P(),
        P(),
    )
    return jax.shard_map(
        shards,
        mesh=torus,
        in_specs=placed,
        out_specs=(P(SEQ_GRP, None), P(SEQ, "grp"), P(SEQ, "grp"), P(SEQ, "grp")),
        check_vma=False,
    )
```

```python
import functools

import jax
import jax.numpy as jnp
from jax import lax
from jax.experimental import pallas as pl
from jax.experimental.pallas import tpu as pltpu
from jax.sharding import Mesh
from jax.sharding import PartitionSpec as P

HEAD = 128
PATCH = 8
SEQ = ("seq_0", "seq_1", "seq_2")
SEQ_GRP = ("seq_0", "seq_1", "seq_2", "grp")
CHIPS = ("seq_0", "seq_1")

EPSILON = 1e-05
FLOOR = -1e30
SCALE = HEAD ** (-0.5)
LOG2E = 1.4426950408889634
MIB = 2**20

BF16 = jnp.bfloat16
F32 = jnp.float32

NT = (((1,), (1,)), ((), ()))
NN = (((1,), (0,)), ((), ()))


def dot(a, b, dims=NN):
    return lax.dot_general(a, b, dims, preferred_element_type=F32)


WIDE = 256


def own_plan(rows):
    plan = []
    base = 0
    for first in range(0, rows, WIDE):
        pieces = [(at, WIDE, "causal" if at == first else "all") for at in range(0, first + WIDE, WIDE)]
        plan.append((first, base, first + WIDE, pieces))
        base += first + WIDE
    return plan, base


def other_plan(rows, block):
    plan = []
    base = 0
    for first in range(0, rows, WIDE):
        lowest, highest = first // block, (first + WIDE - 1) // block
        keys = min(rows, 2 * block * ((highest + 2) // 2))
        pieces = []
        for at in range(0, keys, block):
            part = at // block
            kind = "all" if part < lowest else "block" if part <= highest else "none"
            pieces.append((at, block, kind))
        plan.append((first, base, keys, pieces))
        base += keys
    return plan, base


def flat_rows(ref, at, target):
    block = ref.shape[2]
    for j in range(ref.shape[0]):
        target[pl.ds(j * block, block)] = ref[j, at]


def turned_rows(ref, at, target):
    block = ref.shape[2]
    for j in range(0, ref.shape[0], 2):
        two = jnp.concatenate([ref[j, at], ref[j + 1, at]], 0)
        target[:, pl.ds(j * block, 2 * block)] = two.T


def query_chunk(ref, first):
    block = ref.shape[2]
    found = []
    at = first
    while at < first + WIDE:
        stop = min(first + WIDE, (at // block + 1) * block)
        found.append(ref[at // block, 0, pl.ds(at % block, stop - at)])
        at = stop
    return jnp.concatenate(found, 0)


def piece_scores(queries, first, pieces, key_s, score_s, core):
    top = None
    for at, size, kind in pieces:
        if kind == "none":
            continue
        score = dot(key_s[pl.ds(at, size)], queries, NT)
        if kind == "causal":
            key_at = lax.broadcasted_iota(jnp.int32, score.shape, 0)
            query_at = lax.broadcasted_iota(jnp.int32, score.shape, 1)
            score = jnp.where(key_at <= query_at, score, FLOOR)
        elif kind == "block":
            row = first + lax.broadcasted_iota(jnp.int32, (1, WIDE), 1)
            shown = row >= size * (at // size + 1 - core)
            score = jnp.where(shown, score, FLOOR)
        score_s[pl.ds(at, size)] = score
        piece_top = jnp.max(score, axis=0, keepdims=True)
        top = piece_top if top is None else jnp.maximum(top, piece_top)
    return top


def piece_chances(shift, base, pieces, score_s, kept_ref):
    total = jnp.zeros((1, WIDE), F32)
    for at, size, kind in pieces:
        kept = pl.ds(base + at, size)
        if kind == "none":
            kept_ref[kept] = jnp.zeros((size, WIDE), BF16)
            continue
        chance = jnp.exp2(score_s[pl.ds(at, size)] * (SCALE * LOG2E) - shift)
        total = total + jnp.sum(chance, axis=0, keepdims=True)
        kept_ref[kept] = chance.astype(BF16)
    return total


def forward_own(plan, own_ref, load_ref, kept_ref, mixed_ref, stats_ref, loaded_ref, key_s, turned_s, score_s, sem):
    load = pltpu.make_async_copy(load_ref, loaded_ref, sem)
    load.start()
    flat_rows(own_ref, 1, key_s)
    turned_rows(own_ref, 2, turned_s)
    for i, (first, base, keys, pieces) in enumerate(plan):
        top = piece_scores(query_chunk(own_ref, first), first, pieces, key_s, score_s, None)
        shift = top * (SCALE * LOG2E)
        total = piece_chances(shift, base, pieces, score_s, kept_ref)
        mixed_ref[i] = dot(turned_s[:, :keys], kept_ref[pl.ds(base, keys)])
        stats_ref[i, 0:1] = shift
        stats_ref[i, 1:2] = total
    load.wait()


def forward_other(
    plan,
    facts_ref,
    own_ref,
    other_ref,
    mixed_ref,
    stats_ref,
    load_ref,
    kept_ref,
    out_ref,
    own_inverse_ref,
    inverse_ref,
    loaded_ref,
    key_s,
    turned_s,
    score_s,
    sem,
):
    load = pltpu.make_async_copy(load_ref, loaded_ref, sem)
    load.start()
    flat_rows(other_ref, 0, key_s)
    turned_rows(other_ref, 1, turned_s)
    core = facts_ref[2]
    for i, (first, base, keys, pieces) in enumerate(plan):
        top = piece_scores(query_chunk(own_ref, first), first, pieces, key_s, score_s, core)
        own_shift = stats_ref[i, 0:1]
        shift = jnp.maximum(top * (SCALE * LOG2E), own_shift)
        total = piece_chances(shift, base, pieces, score_s, kept_ref)
        own_part = jnp.exp2(own_shift - shift)
        total = total + own_part * stats_ref[i, 1:2]
        mixed = mixed_ref[i] * own_part + dot(turned_s[:, :keys], kept_ref[pl.ds(base, keys)])
        inverse = 1.0 / total
        rows = pl.ds(first, WIDE)
        out_ref[rows] = (mixed * inverse).T.astype(BF16)
        inverse_ref[rows] = jnp.broadcast_to(inverse, (HEAD, WIDE)).T
        own_inverse_ref[rows] = jnp.broadcast_to(own_part * inverse, (HEAD, WIDE)).T
    load.wait()


def backward_side(
    plan, key_at, own_ref, side_ref, mixed_ref, inverse_ref, kept_ref, grad_ref, key_sum, value_sum, value_s, turned_s,
    slope_s,
):
    flat_rows(side_ref, key_at + 1, value_s)
    turned_rows(side_ref, key_at, turned_s)
    reached = 0
    for i, (first, base, keys, pieces) in enumerate(plan):
        queries = query_chunk(own_ref, first)
        rows = pl.ds(first, WIDE)
        grads = (grad_ref[rows].astype(F32) * inverse_ref[rows]).astype(BF16)
        product = grads.astype(F32) * mixed_ref[rows].astype(F32)
        row_dot = jnp.sum(product.T, axis=0, keepdims=True)
        for at, size, kind in pieces:
            spot = pl.ds(at, size)
            if kind == "none":
                slope_s[spot] = jnp.zeros((size, WIDE), BF16)
                continue
            kept = kept_ref[pl.ds(base + at, size)]
            chance_grad = dot(value_s[spot], grads, NT)
            slope = (kept.astype(F32) * (chance_grad - row_dot)).astype(BF16)
            slope_s[spot] = slope
            value_part = dot(kept, grads)
            key_part = dot(slope, queries)
            if at >= reached:
                reached = at + size
                value_sum[spot] = value_part
                key_sum[spot] = key_part
            else:
                value_sum[spot] += value_part
                key_sum[spot] += key_part
        yield i, dot(turned_s[:, :keys], slope_s[pl.ds(0, keys)])


def backward_other(
    plan, own_ref, other_ref, mixed_ref, inverse_ref, kept_ref, grad_ref, pair_ref, query_ref, key_sum, value_sum,
    value_s, turned_s, slope_s,
):
    for i, turned in backward_side(
        plan, 0, own_ref, other_ref, mixed_ref, inverse_ref, kept_ref, grad_ref, key_sum, value_sum, value_s, turned_s,
        slope_s,
    ):
        query_ref[i] = turned
    parts, _, block, _ = other_ref.shape
    for j in range(parts):
        rows = pl.ds(j * block, block)
        pair_ref[j, 0] = (key_sum[rows] * SCALE).astype(BF16)
        pair_ref[j, 1] = value_sum[rows].astype(BF16)


def backward_own(
    plan, own_ref, mixed_ref, inverse_ref, kept_ref, grad_ref, turned_ref, query_ref, key_ref, value_ref, value_s,
    turned_s, slope_s,
):
    for i, turned in backward_side(
        plan, 1, own_ref, own_ref, mixed_ref, inverse_ref, kept_ref, grad_ref, key_ref, value_ref, value_s, turned_s,
        slope_s,
    ):
        first = plan[i][0]
        query_ref[pl.ds(first, WIDE)] = ((turned + turned_ref[i]) * SCALE).T.astype(BF16)


def join_kernel(query_ref, key_ref, value_ref, pair_ref, out_ref):
    parts, _, block, _ = out_ref.shape
    for j in range(parts):
        rows = pl.ds(j * block, block)
        out_ref[j, 0] = query_ref[rows]
        out_ref[j, 1] = (key_ref[rows] * SCALE + pair_ref[j, 0].astype(F32)).astype(BF16)
        out_ref[j, 2] = (value_ref[rows] + pair_ref[j, 1].astype(F32)).astype(BF16)


def pack_kernel(*refs):
    arrays, out_ref, held_ref, in_sems, out_sems = refs[:-4], refs[-4], refs[-3], refs[-2], refs[-1]
    heads = out_ref.shape[0]
    loads = [pltpu.make_async_copy(ref, held_ref.at[t], in_sems.at[t]) for t, ref in enumerate(arrays)]
    for load in loads:
        load.start()
    stores = []
    for t, load in enumerate(loads):
        load.wait()
        for h in range(heads):
            source = held_ref.at[t, :, pl.ds(h * HEAD, HEAD)]
            stores.append(pltpu.make_async_copy(source, out_ref.at[h, t], out_sems.at[len(stores)]))
            stores[-1].start()
    for store in stores:
        store.wait()


def unpack_kernel(facts_ref, stack_ref, losses_ref, *refs):
    arrays, loss_ref, row_s, turned_s, loss_s, sems = refs[:-5], refs[-5], refs[-4], refs[-3], refs[-2], refs[-1]
    copies = []
    for t, ref in enumerate(arrays):
        for h in range(stack_ref.shape[0]):
            target = ref.at[:, pl.ds(h * HEAD, HEAD)]
            copies.append(pltpu.make_async_copy(stack_ref.at[h, t], target, sems.at[len(copies)]))
    fetch = pltpu.make_async_copy(losses_ref.at[:, pl.ds(0, 8)], row_s, sems.at[len(copies)])
    fetch.start()
    for copy in copies:
        copy.start()
    fetch.wait()
    slots = loss_s.shape[1]
    turned_s[...] = row_s[:, 0].T
    loss_s[...] = turned_s[pl.ds(pl.multiple_of(facts_ref[0] * slots, 8), slots)].T
    copies.append(pltpu.make_async_copy(loss_s, loss_ref, sems.at[len(copies) + 1]))
    copies[-1].start()
    for copy in copies:
        copy.wait()


def turn_kernel(up_ref, down_ref, up_out, down_out):
    up_out[...] = up_ref[...].T
    down_out[...] = down_ref[...].T


LOSS_ROWS = 128

GELU_A = 0.7978845608028654
GELU_B = 0.044715


def byte_kernel(
    pieces,
    facts_ref,
    rows_ref,
    ids_ref,
    order_ref,
    embed_ref,
    gain_ref,
    up_ref,
    down_ref,
    up_turned_ref,
    down_turned_ref,
    vocab_ref,
    grad_ref,
    loss_ref,
    bend_s,
):
    heads, count, _ = rows_ref.shape
    size = up_ref.shape[1] // pieces
    place = facts_ref[0]
    ids = ids_ref[...].T
    lane = lax.broadcasted_iota(jnp.int32, ids.shape, 1)
    target = jnp.sum(jnp.where(lane == place, ids, 0), axis=1, keepdims=True)
    previous = jnp.sum(jnp.where(lane == place - 1, ids, 0), axis=1, keepdims=True)
    letters = lax.broadcasted_iota(jnp.int32, (count, vocab_ref.shape[1]), 1)
    live = jnp.where(place > 0, 1.0, 0.0)
    one_hot = jnp.where(previous == letters, live, 0.0).astype(BF16)
    hidden_in = jnp.concatenate([rows_ref[h].astype(F32) for h in range(heads)], 1)
    hidden_in = hidden_in + dot(one_hot, embed_ref[...])
    inverse_rms = lax.rsqrt(jnp.mean(hidden_in * hidden_in, axis=1, keepdims=True) + EPSILON)
    gain = gain_ref[...]
    normed = (hidden_in * inverse_rms * gain).astype(BF16)
    after = hidden_in
    for i in range(pieces):
        part = pl.ds(i * size, size)
        raised = dot(normed, up_ref[:, part])
        square = raised * raised
        half = 0.5 + 0.5 * jnp.tanh(raised * (GELU_A + (GELU_A * GELU_B) * square))
        active = (raised * half).astype(BF16)
        bend_s[:, part] = half + half * (1.0 - half) * raised * (
            2.0 * GELU_A + (6.0 * GELU_A * GELU_B) * square
        )
        after = after + dot(active, down_ref[part])
    final_scale = lax.rsqrt(jnp.mean(after * after, axis=1, keepdims=True) + EPSILON)
    final_rows = (after * final_scale).astype(BF16)
    logits = dot(final_rows, vocab_ref[...])
    row_top = jnp.max(logits, axis=1, keepdims=True)
    raised_mass = jnp.exp(logits - row_top)
    mass = jnp.sum(raised_mass, axis=1, keepdims=True)
    is_target = target == letters
    chosen = jnp.sum(jnp.where(is_target, logits, 0.0), axis=1, keepdims=True)
    loss = jnp.log(mass) + row_top - chosen
    row_at = lax.broadcasted_iota(jnp.int32, (count, count), 0)
    ordered = jnp.sum(jnp.where(row_at == order_ref[...] - facts_ref[1], loss, 0.0), axis=0, keepdims=True)
    loss_ref[...] = jnp.zeros(loss_ref.shape, F32)
    loss_ref[0:1, 0:count] = ordered
    logit_grad = raised_mass / mass - jnp.where(is_target, 1.0, 0.0)
    final_grad = dot(logit_grad.astype(BF16), vocab_ref[...], NT).astype(BF16).astype(F32)
    mean_dot = jnp.mean(final_grad * after, axis=1, keepdims=True)
    after_grad = final_scale * final_grad - after * (final_scale * final_scale * final_scale * mean_dot)
    narrow = after_grad.astype(BF16)
    normed_grad = None
    for i in range(pieces):
        part = pl.ds(i * size, size)
        active_grad = dot(narrow, down_turned_ref[:, part]).astype(BF16).astype(F32)
        raised_grad = (active_grad * bend_s[:, part]).astype(BF16)
        term = dot(raised_grad, up_turned_ref[part])
        normed_grad = term if normed_grad is None else normed_grad + term
    scaled = normed_grad.astype(BF16).astype(F32) * gain
    mean_dot = jnp.mean(scaled * hidden_in, axis=1, keepdims=True)
    total = (
        after_grad
        + inverse_rms * scaled
        - hidden_in * (inverse_rms * inverse_rms * inverse_rms * mean_dot)
    ).astype(BF16)
    for h in range(heads):
        grad_ref[h] = total[:, h * HEAD : (h + 1) * HEAD]


def vmem():
    return pl.BlockSpec(memory_space=pltpu.VMEM)


def far():
    return pl.BlockSpec(memory_space=pltpu.HBM)


def smem():
    return pl.BlockSpec(memory_space=pltpu.SMEM)


def held(dims, kind=BF16):
    return pltpu.VMEM(dims, kind)


def shape(dims, kind=BF16):
    return jax.ShapeDtypeStruct(dims, kind)


def exchange(value):
    return lax.all_to_all(value, CHIPS, split_axis=0, concat_axis=0, tiled=True)


def swap_cores(value):
    return lax.ppermute(value, "seq_2", [(0, 1), (1, 0)])


def anywhere():
    return pl.BlockSpec(memory_space=pl.ANY)


def kernel_call(body, name, outs, ins, out_specs, scratch, grant, flops, transcendentals=0, moved=4 * MIB):
    return pl.pallas_call(
        body,
        out_shape=outs,
        in_specs=ins,
        out_specs=out_specs,
        scratch_shapes=scratch,
        compiler_params=pltpu.CompilerParams(vmem_limit_bytes=grant * MIB),
        cost_estimate=pl.CostEstimate(
            flops=flops, bytes_accessed=moved, transcendentals=transcendentals
        ),
        name=name,
    )


def shards(
    byte_ids,
    patch_order,
    query_rows,
    key_rows,
    value_rows,
    byte_embed,
    norm_gain,
    w_up,
    w_down,
    vocab_head,
):
    count, columns = query_rows.shape
    hidden = w_up.shape[1]
    heads = columns // HEAD
    rows = heads * count
    chunks = rows // WIDE
    seq_here = lax.axis_index(SEQ)
    place = lax.axis_index("grp").astype(jnp.int32)
    core = lax.axis_index("seq_2").astype(jnp.int32)
    facts = jnp.stack([place, seq_here * count, core])
    query_rows, facts = lax.optimization_barrier((query_rows, facts))
    near_plan, near_rows = own_plan(rows)
    far_plan, far_rows = other_plan(rows, count)

    query_rows, key_rows, value_rows = (
        pltpu.with_memory_space_constraint(a, pltpu.HBM) for a in (query_rows, key_rows, value_rows)
    )
    stacked = kernel_call(
        pack_kernel,
        "pack",
        shape((heads, 3, count, HEAD)),
        [far()] * 3,
        anywhere(),
        [
            pltpu.VMEM((3, count, columns), BF16),
            pltpu.SemaphoreType.DMA((3,)),
            pltpu.SemaphoreType.DMA((3 * heads,)),
        ],
        4,
        0,
    )(query_rows, key_rows, value_rows)
    own = exchange(stacked)

    size = 512
    w_up = pltpu.with_memory_space_constraint(w_up, pltpu.HBM)
    w_down = pltpu.with_memory_space_constraint(w_down, pltpu.HBM)
    wide_block = pl.BlockSpec((columns, size), lambda i: (0, i))
    tall_block = pl.BlockSpec((size, columns), lambda i: (i, 0))
    turned = pl.pallas_call(
        turn_kernel,
        out_shape=(pltpu.HBM((hidden, columns), BF16), pltpu.HBM((columns, hidden), BF16)),
        grid=(hidden // size,),
        in_specs=[wide_block, tall_block],
        out_specs=(tall_block, wide_block),
        compiler_params=pltpu.CompilerParams(vmem_limit_bytes=12 * MIB),
        cost_estimate=pl.CostEstimate(flops=0, bytes_accessed=32 * MIB, transcendentals=0),
        name="turn_weights",
    )(w_up, w_down)
    own, turned = lax.optimization_barrier((own, turned))
    other = swap_cores(own[:, 1:])

    kv_scratch = [pltpu.VMEM((rows, HEAD), BF16), pltpu.VMEM((HEAD, rows), BF16)]
    near_kept, near_mixed, stats, up_held = kernel_call(
        functools.partial(forward_own, near_plan),
        "forward_own",
        (
            held((near_rows, WIDE)),
            held((chunks, HEAD, WIDE), F32),
            held((chunks, 8, WIDE), F32),
            held(w_up.shape),
        ),
        [vmem(), far()],
        (vmem(),) * 4,
        kv_scratch + [pltpu.VMEM((rows, WIDE), F32), pltpu.SemaphoreType.DMA],
        8,
        4 * near_rows * WIDE * HEAD,
        near_rows * WIDE,
    )(own, w_up)
    far_kept, attended, near_inverse, far_inverse, down_held = kernel_call(
        functools.partial(forward_other, far_plan),
        "forward_other",
        (
            held((far_rows, WIDE)),
            held((rows, HEAD)),
            held((rows, HEAD), F32),
            held((rows, HEAD), F32),
            held(w_down.shape),
        ),
        [smem()] + [vmem()] * 4 + [far()],
        (vmem(),) * 5,
        kv_scratch + [pltpu.VMEM((rows, WIDE), F32), pltpu.SemaphoreType.DMA],
        8,
        4 * far_rows * WIDE * HEAD,
        far_rows * WIDE,
    )(facts, own, other, near_mixed, stats, w_down)

    byte_pieces = 4
    owned_rows = exchange(attended.reshape(heads, count, HEAD))
    context_grad, losses = kernel_call(
        functools.partial(byte_kernel, byte_pieces),
        "byte_layer",
        (shape((heads, count, HEAD)), shape((LOSS_ROWS, 2 * HEAD), F32)),
        [smem()] + [vmem()] * 10,
        (vmem(), vmem()),
        [pltpu.VMEM((count, hidden), F32)],
        14,
        8 * count * columns * hidden,
        count * hidden,
    )(
        facts,
        owned_rows,
        byte_ids.T,
        patch_order[None],
        byte_embed,
        norm_gain[None],
        up_held,
        down_held,
        *turned,
        vocab_head,
    )

    grad_rows = exchange(context_grad).reshape(rows, HEAD)
    side_scratch = kv_scratch + [pltpu.VMEM((rows, WIDE), BF16)]
    sums = [pltpu.VMEM((rows, HEAD), F32)] * 2
    pair_grad, turned_grad = kernel_call(
        functools.partial(backward_other, far_plan),
        "backward_other",
        (shape((heads, 2, count, HEAD)), shape((chunks, HEAD, WIDE), F32)),
        [vmem()] * 6,
        (vmem(), vmem()),
        sums + side_scratch,
        8,
        8 * far_rows * WIDE * HEAD,
    )(own, other, attended, far_inverse, far_kept, grad_rows)
    pair_sent = swap_cores(pair_grad)
    query_grad, key_grad, value_grad = kernel_call(
        functools.partial(backward_own, near_plan),
        "backward_own",
        (shape((rows, HEAD)), shape((rows, HEAD), F32), shape((rows, HEAD), F32)),
        [vmem()] * 6,
        (vmem(), vmem(), vmem()),
        side_scratch,
        8,
        8 * near_rows * WIDE * HEAD,
    )(own, attended, near_inverse, near_kept, grad_rows, turned_grad)
    joined = kernel_call(
        join_kernel,
        "join",
        shape((heads, 3, count, HEAD)),
        [vmem()] * 4,
        vmem(),
        [],
        4,
        0,
    )(query_grad, key_grad, value_grad, pair_sent)
    joined, losses = lax.optimization_barrier((joined, losses))
    all_losses = pltpu.with_memory_space_constraint(lax.all_gather(losses, "grp"), pltpu.HBM)
    back = exchange(joined)
    query_out, key_out, value_out, byte_loss = kernel_call(
        unpack_kernel,
        "unpack",
        (shape((count, columns)),) * 3 + (shape((PATCH, count // PATCH), F32),),
        [smem(), anywhere(), anywhere()],
        (anywhere(),) * 4,
        [
            pltpu.VMEM((PATCH, 8, 2 * HEAD), F32),
            pltpu.VMEM((2 * HEAD, PATCH), F32),
            pltpu.VMEM((PATCH, count // PATCH), F32),
            pltpu.SemaphoreType.DMA((3 * heads + 2,)),
        ],
        2,
        0,
    )(facts, back, all_losses)
    return byte_loss.T, query_out, key_out, value_out


def solution(mesh):
    torus = Mesh(
        mesh.devices.reshape(4, 2, 2, mesh.shape["grp"]), ("seq_0", "seq_1", "seq_2", "grp")
    )
    placed = (
        P(SEQ, None),
        P(SEQ),
        P(SEQ, "grp"),
        P(SEQ, "grp"),
        P(SEQ, "grp"),
        P(),
        P(),
        P(),
        P(),
        P(),
    )
    return jax.shard_map(
        shards,
        mesh=torus,
        in_specs=placed,
        out_specs=(P(SEQ_GRP, None), P(SEQ, "grp"), P(SEQ, "grp"), P(SEQ, "grp")),
        check_vma=False,
    )
```

```python
import functools

import jax
import jax.numpy as jnp
from jax import lax
from jax.experimental import pallas as pl
from jax.experimental.pallas import tpu as pltpu
from jax.sharding import Mesh
from jax.sharding import PartitionSpec as P

HEAD = 128
PATCH = 8
SEQ = ("seq_0", "seq_1", "seq_2")
SEQ_GRP = ("seq_0", "seq_1", "seq_2", "grp")
CHIPS = ("seq_0", "seq_1")

EPSILON = 1e-05
FLOOR = -1e30
SCALE = HEAD ** (-0.5)
LOG2E = 1.4426950408889634
MIB = 2**20

BF16 = jnp.bfloat16
F32 = jnp.float32

NT = (((1,), (1,)), ((), ()))
NN = (((1,), (0,)), ((), ()))


def dot(a, b, dims=NN):
    return lax.dot_general(a, b, dims, preferred_element_type=F32)


WIDE = 256


def own_plan(rows):
    plan = []
    base = 0
    for first in range(0, rows, WIDE):
        pieces = [(at, WIDE, "causal" if at == first else "all") for at in range(0, first + WIDE, WIDE)]
        plan.append((first, base, first + WIDE, pieces))
        base += first + WIDE
    return plan, base


def other_plan(rows, block):
    plan = []
    base = 0
    for first in range(0, rows, WIDE):
        lowest, highest = first // block, (first + WIDE - 1) // block
        keys = min(rows, 2 * block * ((highest + 2) // 2))
        pieces = []
        for at in range(0, keys, block):
            part = at // block
            kind = "all" if part < lowest else "block" if part <= highest else "none"
            pieces.append((at, block, kind))
        plan.append((first, base, keys, pieces))
        base += keys
    return plan, base


def flat_rows(ref, at, target):
    block = ref.shape[2]
    for j in range(ref.shape[0]):
        target[pl.ds(j * block, block)] = ref[j, at]


def turned_rows(ref, at, target):
    block = ref.shape[2]
    for j in range(0, ref.shape[0], 2):
        two = jnp.concatenate([ref[j, at], ref[j + 1, at]], 0)
        target[:, pl.ds(j * block, 2 * block)] = two.T


def query_chunk(ref, first):
    block = ref.shape[2]
    found = []
    at = first
    while at < first + WIDE:
        stop = min(first + WIDE, (at // block + 1) * block)
        found.append(ref[at // block, 0, pl.ds(at % block, stop - at)])
        at = stop
    return jnp.concatenate(found, 0)


def piece_scores(queries, first, pieces, key_s, score_s, core):
    top = None
    for at, size, kind in pieces:
        if kind == "none":
            continue
        score = dot(key_s[pl.ds(at, size)], queries, NT)
        if kind == "causal":
            key_at = lax.broadcasted_iota(jnp.int32, score.shape, 0)
            query_at = lax.broadcasted_iota(jnp.int32, score.shape, 1)
            score = jnp.where(key_at <= query_at, score, FLOOR)
        elif kind == "block":
            row = first + lax.broadcasted_iota(jnp.int32, (1, WIDE), 1)
            shown = row >= size * (at // size + 1 - core)
            score = jnp.where(shown, score, FLOOR)
        score_s[pl.ds(at, size)] = score
        piece_top = jnp.max(score, axis=0, keepdims=True)
        top = piece_top if top is None else jnp.maximum(top, piece_top)
    return top


def piece_chances(shift, base, pieces, score_s, kept_ref):
    total = jnp.zeros((1, WIDE), F32)
    for at, size, kind in pieces:
        kept = pl.ds(base + at, size)
        if kind == "none":
            kept_ref[kept] = jnp.zeros((size, WIDE), BF16)
            continue
        chance = jnp.exp2(score_s[pl.ds(at, size)] * (SCALE * LOG2E) - shift)
        total = total + jnp.sum(chance, axis=0, keepdims=True)
        kept_ref[kept] = chance.astype(BF16)
    return total


def forward_own(plan, own_ref, load_ref, kept_ref, mixed_ref, stats_ref, loaded_ref, key_s, turned_s, score_s, sem):
    load = pltpu.make_async_copy(load_ref, loaded_ref, sem)
    load.start()
    flat_rows(own_ref, 1, key_s)
    turned_rows(own_ref, 2, turned_s)
    for i, (first, base, keys, pieces) in enumerate(plan):
        top = piece_scores(query_chunk(own_ref, first), first, pieces, key_s, score_s, None)
        shift = top * (SCALE * LOG2E)
        total = piece_chances(shift, base, pieces, score_s, kept_ref)
        mixed_ref[i] = dot(turned_s[:, :keys], kept_ref[pl.ds(base, keys)])
        stats_ref[i, 0:1] = shift
        stats_ref[i, 1:2] = total
    load.wait()


def forward_other(
    plan,
    facts_ref,
    own_ref,
    other_ref,
    mixed_ref,
    stats_ref,
    load_ref,
    kept_ref,
    out_ref,
    own_inverse_ref,
    inverse_ref,
    loaded_ref,
    key_s,
    turned_s,
    score_s,
    sem,
):
    load = pltpu.make_async_copy(load_ref, loaded_ref, sem)
    load.start()
    flat_rows(other_ref, 0, key_s)
    turned_rows(other_ref, 1, turned_s)
    core = facts_ref[2]
    for i, (first, base, keys, pieces) in enumerate(plan):
        top = piece_scores(query_chunk(own_ref, first), first, pieces, key_s, score_s, core)
        own_shift = stats_ref[i, 0:1]
        shift = jnp.maximum(top * (SCALE * LOG2E), own_shift)
        total = piece_chances(shift, base, pieces, score_s, kept_ref)
        own_part = jnp.exp2(own_shift - shift)
        total = total + own_part * stats_ref[i, 1:2]
        mixed = mixed_ref[i] * own_part + dot(turned_s[:, :keys], kept_ref[pl.ds(base, keys)])
        inverse = 1.0 / total
        rows = pl.ds(first, WIDE)
        out_ref[rows] = (mixed * inverse).T.astype(BF16)
        inverse_ref[rows] = jnp.broadcast_to(inverse, (HEAD, WIDE)).T
        own_inverse_ref[rows] = jnp.broadcast_to(own_part * inverse, (HEAD, WIDE)).T
    load.wait()


def backward_side(
    plan, key_at, own_ref, side_ref, mixed_ref, inverse_ref, kept_ref, grad_ref, key_sum, value_sum, value_s, turned_s,
    slope_s,
):
    flat_rows(side_ref, key_at + 1, value_s)
    turned_rows(side_ref, key_at, turned_s)
    reached = 0
    for i, (first, base, keys, pieces) in enumerate(plan):
        queries = query_chunk(own_ref, first)
        rows = pl.ds(first, WIDE)
        grads = (grad_ref[rows].astype(F32) * inverse_ref[rows]).astype(BF16)
        product = grads.astype(F32) * mixed_ref[rows].astype(F32)
        row_dot = jnp.sum(product.T, axis=0, keepdims=True)
        for at, size, kind in pieces:
            spot = pl.ds(at, size)
            if kind == "none":
                slope_s[spot] = jnp.zeros((size, WIDE), BF16)
                continue
            kept = kept_ref[pl.ds(base + at, size)]
            chance_grad = dot(value_s[spot], grads, NT)
            slope = (kept.astype(F32) * (chance_grad - row_dot)).astype(BF16)
            slope_s[spot] = slope
            value_part = dot(kept, grads)
            key_part = dot(slope, queries)
            if at >= reached:
                reached = at + size
                value_sum[spot] = value_part
                key_sum[spot] = key_part
            else:
                value_sum[spot] += value_part
                key_sum[spot] += key_part
        yield i, dot(turned_s[:, :keys], slope_s[pl.ds(0, keys)])


def backward_other(
    plan, own_ref, other_ref, mixed_ref, inverse_ref, kept_ref, grad_ref, pair_ref, query_ref, key_sum, value_sum,
    value_s, turned_s, slope_s,
):
    for i, turned in backward_side(
        plan, 0, own_ref, other_ref, mixed_ref, inverse_ref, kept_ref, grad_ref, key_sum, value_sum, value_s, turned_s,
        slope_s,
    ):
        query_ref[i] = turned
    parts, _, block, _ = other_ref.shape
    for j in range(parts):
        rows = pl.ds(j * block, block)
        pair_ref[j, 0] = (key_sum[rows] * SCALE).astype(BF16)
        pair_ref[j, 1] = value_sum[rows].astype(BF16)


def backward_own(
    plan, own_ref, mixed_ref, inverse_ref, kept_ref, grad_ref, turned_ref, query_ref, key_ref, value_ref, value_s,
    turned_s, slope_s,
):
    for i, turned in backward_side(
        plan, 1, own_ref, own_ref, mixed_ref, inverse_ref, kept_ref, grad_ref, key_ref, value_ref, value_s, turned_s,
        slope_s,
    ):
        first = plan[i][0]
        query_ref[pl.ds(first, WIDE)] = ((turned + turned_ref[i]) * SCALE).T.astype(BF16)


def join_kernel(query_ref, key_ref, value_ref, pair_ref, out_ref):
    parts, _, block, _ = out_ref.shape
    for j in range(parts):
        rows = pl.ds(j * block, block)
        out_ref[j, 0] = query_ref[rows]
        out_ref[j, 1] = (key_ref[rows] * SCALE + pair_ref[j, 0].astype(F32)).astype(BF16)
        out_ref[j, 2] = (value_ref[rows] + pair_ref[j, 1].astype(F32)).astype(BF16)


def pack_kernel(*refs):
    arrays, out_ref, held_ref, in_sems, out_sems = refs[:-4], refs[-4], refs[-3], refs[-2], refs[-1]
    heads = out_ref.shape[0]
    loads = [pltpu.make_async_copy(ref, held_ref.at[t], in_sems.at[t]) for t, ref in enumerate(arrays)]
    for load in loads:
        load.start()
    stores = []
    for t, load in enumerate(loads):
        load.wait()
        for h in range(heads):
            source = held_ref.at[t, :, pl.ds(h * HEAD, HEAD)]
            stores.append(pltpu.make_async_copy(source, out_ref.at[h, t], out_sems.at[len(stores)]))
            stores[-1].start()
    for store in stores:
        store.wait()


def unpack_kernel(facts_ref, stack_ref, losses_ref, *refs):
    arrays, loss_ref, turned_s, loss_s, sems = refs[:-4], refs[-4], refs[-3], refs[-2], refs[-1]
    copies = []
    for t, ref in enumerate(arrays):
        for h in range(stack_ref.shape[0]):
            target = ref.at[:, pl.ds(h * HEAD, HEAD)]
            copies.append(pltpu.make_async_copy(stack_ref.at[h, t], target, sems.at[len(copies)]))
            copies[-1].start()
    slots = loss_s.shape[1]
    turned_s[...] = losses_ref[...].T
    loss_s[...] = turned_s[pl.ds(pl.multiple_of(facts_ref[0] * slots, 8), slots)].T
    copies.append(pltpu.make_async_copy(loss_s, loss_ref, sems.at[len(copies)]))
    copies[-1].start()
    for copy in copies:
        copy.wait()


def turn_kernel(up_ref, down_ref, up_out, down_out):
    up_out[...] = up_ref[...].T
    down_out[...] = down_ref[...].T


GELU_A = 0.7978845608028654
GELU_B = 0.044715


def byte_kernel(
    pieces,
    facts_ref,
    rows_ref,
    ids_ref,
    order_ref,
    embed_ref,
    gain_ref,
    up_ref,
    down_ref,
    up_turned_ref,
    down_turned_ref,
    vocab_ref,
    grad_ref,
    loss_ref,
    bend_s,
):
    heads, count, _ = rows_ref.shape
    size = up_ref.shape[1] // pieces
    place = facts_ref[0]
    ids = ids_ref[...].T
    lane = lax.broadcasted_iota(jnp.int32, ids.shape, 1)
    target = jnp.sum(jnp.where(lane == place, ids, 0), axis=1, keepdims=True)
    previous = jnp.sum(jnp.where(lane == place - 1, ids, 0), axis=1, keepdims=True)
    letters = lax.broadcasted_iota(jnp.int32, (count, vocab_ref.shape[1]), 1)
    live = jnp.where(place > 0, 1.0, 0.0)
    one_hot = jnp.where(previous == letters, live, 0.0).astype(BF16)
    hidden_in = jnp.concatenate([rows_ref[h].astype(F32) for h in range(heads)], 1)
    hidden_in = hidden_in + dot(one_hot, embed_ref[...])
    inverse_rms = lax.rsqrt(jnp.mean(hidden_in * hidden_in, axis=1, keepdims=True) + EPSILON)
    gain = gain_ref[...]
    normed = (hidden_in * inverse_rms * gain).astype(BF16)
    after = hidden_in
    for i in range(pieces):
        part = pl.ds(i * size, size)
        raised = dot(normed, up_ref[:, part])
        square = raised * raised
        half = 0.5 + 0.5 * jnp.tanh(raised * (GELU_A + (GELU_A * GELU_B) * square))
        active = (raised * half).astype(BF16)
        bend_s[:, part] = half + half * (1.0 - half) * raised * (
            2.0 * GELU_A + (6.0 * GELU_A * GELU_B) * square
        )
        after = after + dot(active, down_ref[part])
    final_scale = lax.rsqrt(jnp.mean(after * after, axis=1, keepdims=True) + EPSILON)
    final_rows = (after * final_scale).astype(BF16)
    logits = dot(final_rows, vocab_ref[...])
    row_top = jnp.max(logits, axis=1, keepdims=True)
    raised_mass = jnp.exp(logits - row_top)
    mass = jnp.sum(raised_mass, axis=1, keepdims=True)
    is_target = target == letters
    chosen = jnp.sum(jnp.where(is_target, logits, 0.0), axis=1, keepdims=True)
    loss = jnp.log(mass) + row_top - chosen
    row_at = lax.broadcasted_iota(jnp.int32, (count, count), 0)
    ordered = jnp.sum(jnp.where(row_at == order_ref[...] - facts_ref[1], loss, 0.0), axis=0, keepdims=True)
    slot = lax.broadcasted_iota(jnp.int32, loss_ref.shape, 0)
    loss_ref[...] = jnp.where(slot == place, ordered, 0.0)
    logit_grad = raised_mass / mass - jnp.where(is_target, 1.0, 0.0)
    final_grad = dot(logit_grad.astype(BF16), vocab_ref[...], NT).astype(BF16).astype(F32)
    mean_dot = jnp.mean(final_grad * after, axis=1, keepdims=True)
    after_grad = final_scale * final_grad - after * (final_scale * final_scale * final_scale * mean_dot)
    narrow = after_grad.astype(BF16)
    normed_grad = None
    for i in range(pieces):
        part = pl.ds(i * size, size)
        active_grad = dot(narrow, down_turned_ref[:, part]).astype(BF16).astype(F32)
        raised_grad = (active_grad * bend_s[:, part]).astype(BF16)
        term = dot(raised_grad, up_turned_ref[part])
        normed_grad = term if normed_grad is None else normed_grad + term
    scaled = normed_grad.astype(BF16).astype(F32) * gain
    mean_dot = jnp.mean(scaled * hidden_in, axis=1, keepdims=True)
    total = (
        after_grad
        + inverse_rms * scaled
        - hidden_in * (inverse_rms * inverse_rms * inverse_rms * mean_dot)
    ).astype(BF16)
    for h in range(heads):
        grad_ref[h] = total[:, h * HEAD : (h + 1) * HEAD]


def vmem():
    return pl.BlockSpec(memory_space=pltpu.VMEM)


def far():
    return pl.BlockSpec(memory_space=pltpu.HBM)


def smem():
    return pl.BlockSpec(memory_space=pltpu.SMEM)


def held(dims, kind=BF16):
    return pltpu.VMEM(dims, kind)


def shape(dims, kind=BF16):
    return jax.ShapeDtypeStruct(dims, kind)


def exchange(value):
    return lax.all_to_all(value, CHIPS, split_axis=0, concat_axis=0, tiled=True)


def gather_losses(value, steps):
    found = [lax.ppermute(value, "grp", [(i, (i + k) % PATCH) for i in range(PATCH)]) for k in steps]
    return functools.reduce(jnp.add, found, value)


def pair_losses(value):
    return value + lax.ppermute(value, "grp", [(i, i ^ 1) for i in range(PATCH)])


def swap_cores(value):
    return lax.ppermute(value, "seq_2", [(0, 1), (1, 0)])


def anywhere():
    return pl.BlockSpec(memory_space=pl.ANY)


def kernel_call(body, name, outs, ins, out_specs, scratch, grant, flops, transcendentals=0, moved=4 * MIB):
    return pl.pallas_call(
        body,
        out_shape=outs,
        in_specs=ins,
        out_specs=out_specs,
        scratch_shapes=scratch,
        compiler_params=pltpu.CompilerParams(vmem_limit_bytes=grant * MIB),
        cost_estimate=pl.CostEstimate(
            flops=flops, bytes_accessed=moved, transcendentals=transcendentals
        ),
        name=name,
    )


def shards(
    byte_ids,
    patch_order,
    query_rows,
    key_rows,
    value_rows,
    byte_embed,
    norm_gain,
    w_up,
    w_down,
    vocab_head,
):
    count, columns = query_rows.shape
    hidden = w_up.shape[1]
    heads = columns // HEAD
    rows = heads * count
    chunks = rows // WIDE
    seq_here = lax.axis_index(SEQ)
    place = lax.axis_index("grp").astype(jnp.int32)
    core = lax.axis_index("seq_2").astype(jnp.int32)
    facts = jnp.stack([place, seq_here * count, core])
    query_rows, facts = lax.optimization_barrier((query_rows, facts))
    near_plan, near_rows = own_plan(rows)
    far_plan, far_rows = other_plan(rows, count)

    query_rows, key_rows, value_rows = (
        pltpu.with_memory_space_constraint(a, pltpu.HBM) for a in (query_rows, key_rows, value_rows)
    )
    stacked = kernel_call(
        pack_kernel,
        "pack",
        shape((heads, 3, count, HEAD)),
        [far()] * 3,
        anywhere(),
        [
            pltpu.VMEM((3, count, columns), BF16),
            pltpu.SemaphoreType.DMA((3,)),
            pltpu.SemaphoreType.DMA((3 * heads,)),
        ],
        4,
        0,
    )(query_rows, key_rows, value_rows)
    own = exchange(stacked)

    size = 512
    w_up = pltpu.with_memory_space_constraint(w_up, pltpu.HBM)
    w_down = pltpu.with_memory_space_constraint(w_down, pltpu.HBM)
    wide_block = pl.BlockSpec((columns, size), lambda i: (0, i))
    tall_block = pl.BlockSpec((size, columns), lambda i: (i, 0))
    turned = pl.pallas_call(
        turn_kernel,
        out_shape=(pltpu.HBM((hidden, columns), BF16), pltpu.HBM((columns, hidden), BF16)),
        grid=(hidden // size,),
        in_specs=[wide_block, tall_block],
        out_specs=(tall_block, wide_block),
        compiler_params=pltpu.CompilerParams(vmem_limit_bytes=12 * MIB),
        cost_estimate=pl.CostEstimate(flops=0, bytes_accessed=32 * MIB, transcendentals=0),
        name="turn_weights",
    )(w_up, w_down)
    own, turned = lax.optimization_barrier((own, turned))
    other = swap_cores(own[:, 1:])

    kv_scratch = [pltpu.VMEM((rows, HEAD), BF16), pltpu.VMEM((HEAD, rows), BF16)]
    near_kept, near_mixed, stats, up_held = kernel_call(
        functools.partial(forward_own, near_plan),
        "forward_own",
        (
            held((near_rows, WIDE)),
            held((chunks, HEAD, WIDE), F32),
            held((chunks, 8, WIDE), F32),
            held(w_up.shape),
        ),
        [vmem(), far()],
        (vmem(),) * 4,
        kv_scratch + [pltpu.VMEM((rows, WIDE), F32), pltpu.SemaphoreType.DMA],
        8,
        4 * near_rows * WIDE * HEAD,
        near_rows * WIDE,
    )(own, w_up)
    far_kept, attended, near_inverse, far_inverse, down_held = kernel_call(
        functools.partial(forward_other, far_plan),
        "forward_other",
        (
            held((far_rows, WIDE)),
            held((rows, HEAD)),
            held((rows, HEAD), F32),
            held((rows, HEAD), F32),
            held(w_down.shape),
        ),
        [smem()] + [vmem()] * 4 + [far()],
        (vmem(),) * 5,
        kv_scratch + [pltpu.VMEM((rows, WIDE), F32), pltpu.SemaphoreType.DMA],
        8,
        4 * far_rows * WIDE * HEAD,
        far_rows * WIDE,
    )(facts, own, other, near_mixed, stats, w_down)

    byte_pieces = 4
    owned_rows = exchange(attended.reshape(heads, count, HEAD))
    context_grad, losses = kernel_call(
        functools.partial(byte_kernel, byte_pieces),
        "byte_layer",
        (shape((heads, count, HEAD)), shape((PATCH, count), F32)),
        [smem()] + [vmem()] * 10,
        (vmem(), vmem()),
        [pltpu.VMEM((count, hidden), F32)],
        14,
        8 * count * columns * hidden,
        count * hidden,
    )(
        facts,
        owned_rows,
        byte_ids.T,
        patch_order[None],
        byte_embed,
        norm_gain[None],
        up_held,
        down_held,
        *turned,
        vocab_head,
    )

    grad_rows, losses = lax.optimization_barrier((exchange(context_grad), losses))
    grad_rows = grad_rows.reshape(rows, HEAD)
    side_scratch = kv_scratch + [pltpu.VMEM((rows, WIDE), BF16)]
    sums = [pltpu.VMEM((rows, HEAD), F32)] * 2
    pair_grad, turned_grad = kernel_call(
        functools.partial(backward_other, far_plan),
        "backward_other",
        (shape((heads, 2, count, HEAD)), shape((chunks, HEAD, WIDE), F32)),
        [vmem()] * 6,
        (vmem(), vmem()),
        sums + side_scratch,
        8,
        8 * far_rows * WIDE * HEAD,
    )(own, other, attended, far_inverse, far_kept, grad_rows)
    pair_grad, turned_grad, losses = lax.optimization_barrier((pair_grad, turned_grad, gather_losses(losses, (2, 4, 6))))
    pair_sent = swap_cores(pair_grad)
    query_grad, key_grad, value_grad = kernel_call(
        functools.partial(backward_own, near_plan),
        "backward_own",
        (shape((rows, HEAD)), shape((rows, HEAD), F32), shape((rows, HEAD), F32)),
        [vmem()] * 6,
        (vmem(), vmem(), vmem()),
        side_scratch,
        8,
        8 * near_rows * WIDE * HEAD,
    )(own, attended, near_inverse, near_kept, grad_rows, turned_grad)
    query_grad, losses = lax.optimization_barrier((query_grad, pair_losses(losses)))
    joined = kernel_call(
        join_kernel,
        "join",
        shape((heads, 3, count, HEAD)),
        [vmem()] * 4,
        vmem(),
        [],
        4,
        0,
    )(query_grad, key_grad, value_grad, pair_sent)
    back = exchange(joined)
    query_out, key_out, value_out, byte_loss = kernel_call(
        unpack_kernel,
        "unpack",
        (shape((count, columns)),) * 3 + (shape((PATCH, count // PATCH), F32),),
        [smem(), anywhere(), vmem()],
        (anywhere(),) * 4,
        [
            pltpu.VMEM((count, PATCH), F32),
            pltpu.VMEM((PATCH, count // PATCH), F32),
            pltpu.SemaphoreType.DMA((3 * heads + 1,)),
        ],
        2,
        0,
    )(facts, back, losses)
    return byte_loss.T, query_out, key_out, value_out


def solution(mesh):
    torus = Mesh(
        mesh.devices.reshape(4, 2, 2, mesh.shape["grp"]), ("seq_0", "seq_1", "seq_2", "grp")
    )
    placed = (
        P(SEQ, None),
        P(SEQ),
        P(SEQ, "grp"),
        P(SEQ, "grp"),
        P(SEQ, "grp"),
        P(),
        P(),
        P(),
        P(),
        P(),
    )
    return jax.shard_map(
        shards,
        mesh=torus,
        in_specs=placed,
        out_specs=(P(SEQ_GRP, None), P(SEQ, "grp"), P(SEQ, "grp"), P(SEQ, "grp")),
        check_vma=False,
    )
```

```python
import functools

import jax
import jax.numpy as jnp
from jax import lax
from jax.experimental import pallas as pl
from jax.experimental.pallas import tpu as pltpu
from jax.sharding import Mesh
from jax.sharding import PartitionSpec as P

HEAD = 128
PATCH = 8
SEQ = ("seq_0", "seq_1", "seq_2")
SEQ_GRP = ("seq_0", "seq_1", "seq_2", "grp")
CHIPS = ("seq_0", "seq_1")

EPSILON = 1e-05
FLOOR = -1e30
SCALE = HEAD ** (-0.5)
LOG2E = 1.4426950408889634
MIB = 2**20

BF16 = jnp.bfloat16
F32 = jnp.float32

NT = (((1,), (1,)), ((), ()))
NN = (((1,), (0,)), ((), ()))


def dot(a, b, dims=NN):
    return lax.dot_general(a, b, dims, preferred_element_type=F32)


WIDE = 256


def own_plan(rows):
    plan = []
    base = 0
    for first in range(0, rows, WIDE):
        pieces = [(at, WIDE, "causal" if at == first else "all") for at in range(0, first + WIDE, WIDE)]
        plan.append((first, base, first + WIDE, pieces))
        base += first + WIDE
    return plan, base


def other_plan(rows, block):
    plan = []
    base = 0
    for first in range(0, rows, WIDE):
        lowest, highest = first // block, (first + WIDE - 1) // block
        keys = min(rows, 2 * block * ((highest + 2) // 2))
        pieces = []
        for at in range(0, keys, block):
            part = at // block
            kind = "all" if part < lowest else "block" if part <= highest else "none"
            pieces.append((at, block, kind))
        plan.append((first, base, keys, pieces))
        base += keys
    return plan, base


def flat_rows(ref, at, target):
    block = ref.shape[2]
    for j in range(ref.shape[0]):
        target[pl.ds(j * block, block)] = ref[j, at]


def turned_rows(ref, at, target):
    block = ref.shape[2]
    for j in range(0, ref.shape[0], 2):
        two = jnp.concatenate([ref[j, at], ref[j + 1, at]], 0)
        target[:, pl.ds(j * block, 2 * block)] = two.T


def query_chunk(ref, first):
    block = ref.shape[2]
    found = []
    at = first
    while at < first + WIDE:
        stop = min(first + WIDE, (at // block + 1) * block)
        found.append(ref[at // block, 0, pl.ds(at % block, stop - at)])
        at = stop
    return jnp.concatenate(found, 0)


def piece_scores(queries, first, pieces, key_s, score_s, core):
    top = None
    turned = queries.T
    for at, size, kind in pieces:
        if kind == "none":
            continue
        score = dot(key_s[pl.ds(at, size)], turned)
        if kind == "causal":
            key_at = lax.broadcasted_iota(jnp.int32, score.shape, 0)
            query_at = lax.broadcasted_iota(jnp.int32, score.shape, 1)
            score = jnp.where(key_at <= query_at, score, FLOOR)
        elif kind == "block":
            row = first + lax.broadcasted_iota(jnp.int32, (1, WIDE), 1)
            shown = row >= size * (at // size + 1 - core)
            score = jnp.where(shown, score, FLOOR)
        score_s[pl.ds(at, size)] = score
        piece_top = jnp.max(score, axis=0, keepdims=True)
        top = piece_top if top is None else jnp.maximum(top, piece_top)
    return top


def piece_chances(shift, base, pieces, score_s, kept_ref):
    total = jnp.zeros((1, WIDE), F32)
    for at, size, kind in pieces:
        kept = pl.ds(base + at, size)
        if kind == "none":
            kept_ref[kept] = jnp.zeros((size, WIDE), BF16)
            continue
        chance = jnp.exp2(score_s[pl.ds(at, size)] * (SCALE * LOG2E) - shift)
        total = total + jnp.sum(chance, axis=0, keepdims=True)
        kept_ref[kept] = chance.astype(BF16)
    return total


def staggered(count, start, middle, end):
    start(0)
    for i in range(count):
        if i + 1 < count:
            start(i + 1)
        if i > 0:
            end(i - 1)
        middle(i)
    end(count - 1)


def forward_own(plan, own_ref, load_ref, kept_ref, mixed_ref, stats_ref, loaded_ref, key_s, turned_s, score_s, sem):
    load = pltpu.make_async_copy(load_ref, loaded_ref, sem)
    load.start()
    flat_rows(own_ref, 1, key_s)
    turned_rows(own_ref, 2, turned_s)
    tops = {}

    def start(i):
        first, _, _, pieces = plan[i]
        tops[i] = piece_scores(query_chunk(own_ref, first), first, pieces, key_s, score_s.at[i % 2], None)

    def middle(i):
        _, base, _, pieces = plan[i]
        shift = tops[i] * (SCALE * LOG2E)
        stats_ref[i, 0:1] = shift
        stats_ref[i, 1:2] = piece_chances(shift, base, pieces, score_s.at[i % 2], kept_ref)

    def end(i):
        _, base, keys, _ = plan[i]
        mixed_ref[i] = dot(turned_s[:, :keys], kept_ref[pl.ds(base, keys)])

    staggered(len(plan), start, middle, end)
    load.wait()


def forward_other(
    plan,
    facts_ref,
    own_ref,
    other_ref,
    mixed_ref,
    stats_ref,
    load_ref,
    kept_ref,
    out_ref,
    own_inverse_ref,
    inverse_ref,
    loaded_ref,
    key_s,
    turned_s,
    score_s,
    sem,
):
    load = pltpu.make_async_copy(load_ref, loaded_ref, sem)
    load.start()
    flat_rows(other_ref, 0, key_s)
    turned_rows(other_ref, 1, turned_s)
    core = facts_ref[2]
    tops = {}
    parts = {}

    def start(i):
        first, _, _, pieces = plan[i]
        tops[i] = piece_scores(query_chunk(own_ref, first), first, pieces, key_s, score_s.at[i % 2], core)

    def middle(i):
        _, base, _, pieces = plan[i]
        own_shift = stats_ref[i, 0:1]
        shift = jnp.maximum(tops[i] * (SCALE * LOG2E), own_shift)
        total = piece_chances(shift, base, pieces, score_s.at[i % 2], kept_ref)
        own_part = jnp.exp2(own_shift - shift)
        parts[i] = own_part, 1.0 / (total + own_part * stats_ref[i, 1:2])

    def end(i):
        first, base, keys, _ = plan[i]
        own_part, inverse = parts[i]
        mixed = mixed_ref[i] * own_part + dot(turned_s[:, :keys], kept_ref[pl.ds(base, keys)])
        rows = pl.ds(first, WIDE)
        out_ref[rows] = (mixed * inverse).T.astype(BF16)
        inverse_ref[rows] = jnp.broadcast_to(inverse, (HEAD, WIDE)).T
        own_inverse_ref[rows] = jnp.broadcast_to(own_part * inverse, (HEAD, WIDE)).T

    staggered(len(plan), start, middle, end)
    load.wait()


def backward_side(
    plan, key_at, own_ref, side_ref, mixed_ref, inverse_ref, kept_ref, grad_ref, key_sum, value_sum, value_s, turned_s,
    slope_s,
):
    flat_rows(side_ref, key_at + 1, value_s)
    turned_rows(side_ref, key_at, turned_s)
    tasks = []
    for i, (first, base, keys, pieces) in enumerate(plan):
        rows = pl.ds(first, WIDE)
        grads = (grad_ref[rows].astype(F32) * inverse_ref[rows]).astype(BF16)
        product = grads.astype(F32) * mixed_ref[rows].astype(F32)
        row_dot = jnp.sum(product.T, axis=0, keepdims=True)
        queries = query_chunk(own_ref, first)
        live = [piece for piece in pieces if piece[2] != "none"]
        for at, size, _ in live:
            tasks.append((i, at, size, at == live[-1][0], queries, grads, row_dot))

    def chance_grad(task):
        _, at, size, _, _, grads, _ = task
        return dot(value_s[pl.ds(at, size)], grads, NT)

    reached = 0
    ahead = chance_grad(tasks[0])
    for k, (i, at, size, last, queries, grads, row_dot) in enumerate(tasks):
        here = ahead
        if k + 1 < len(tasks):
            ahead = chance_grad(tasks[k + 1])
        _, base, keys, _ = plan[i]
        spot = pl.ds(at, size)
        kept = kept_ref[pl.ds(base + at, size)]
        slope = (kept.astype(F32) * (here - row_dot)).astype(BF16)
        slope_s[i % 2, spot] = slope
        value_part = dot(kept, grads)
        key_part = dot(slope, queries)
        if at >= reached:
            reached = at + size
            value_sum[spot] = value_part
            key_sum[spot] = key_part
        else:
            value_sum[spot] += value_part
            key_sum[spot] += key_part
        if last:
            for unseen, size, kind in plan[i][3]:
                if kind == "none":
                    slope_s[i % 2, pl.ds(unseen, size)] = jnp.zeros((size, WIDE), BF16)
            yield i, dot(turned_s[:, :keys], slope_s[i % 2, pl.ds(0, keys)])


def backward_other(
    plan, own_ref, other_ref, mixed_ref, inverse_ref, kept_ref, grad_ref, pair_ref, query_ref, key_sum, value_sum,
    value_s, turned_s, slope_s,
):
    for i, turned in backward_side(
        plan, 0, own_ref, other_ref, mixed_ref, inverse_ref, kept_ref, grad_ref, key_sum, value_sum, value_s, turned_s,
        slope_s,
    ):
        query_ref[i] = turned
    parts, _, block, _ = other_ref.shape
    for j in range(parts):
        rows = pl.ds(j * block, block)
        pair_ref[j, 0] = (key_sum[rows] * SCALE).astype(BF16)
        pair_ref[j, 1] = value_sum[rows].astype(BF16)


def backward_own(
    plan, own_ref, mixed_ref, inverse_ref, kept_ref, grad_ref, turned_ref, query_ref, key_ref, value_ref, value_s,
    turned_s, slope_s,
):
    for i, turned in backward_side(
        plan, 1, own_ref, own_ref, mixed_ref, inverse_ref, kept_ref, grad_ref, key_ref, value_ref, value_s, turned_s,
        slope_s,
    ):
        first = plan[i][0]
        query_ref[pl.ds(first, WIDE)] = ((turned + turned_ref[i]) * SCALE).T.astype(BF16)


def join_kernel(query_ref, key_ref, value_ref, pair_ref, out_ref):
    parts, _, block, _ = out_ref.shape
    for j in range(parts):
        rows = pl.ds(j * block, block)
        out_ref[j, 0] = query_ref[rows]
        out_ref[j, 1] = (key_ref[rows] * SCALE + pair_ref[j, 0].astype(F32)).astype(BF16)
        out_ref[j, 2] = (value_ref[rows] + pair_ref[j, 1].astype(F32)).astype(BF16)


def pack_kernel(*refs):
    arrays, out_ref, held_ref, in_sems, out_sems = refs[:-4], refs[-4], refs[-3], refs[-2], refs[-1]
    heads = out_ref.shape[0]
    loads = [pltpu.make_async_copy(ref, held_ref.at[t], in_sems.at[t]) for t, ref in enumerate(arrays)]
    for load in loads:
        load.start()
    stores = []
    for t, load in enumerate(loads):
        load.wait()
        for h in range(heads):
            source = held_ref.at[t, :, pl.ds(h * HEAD, HEAD)]
            stores.append(pltpu.make_async_copy(source, out_ref.at[h, t], out_sems.at[len(stores)]))
            stores[-1].start()
    for store in stores:
        store.wait()


def unpack_kernel(facts_ref, stack_ref, losses_ref, *refs):
    arrays, loss_ref, turned_s, loss_s, sems = refs[:-4], refs[-4], refs[-3], refs[-2], refs[-1]
    copies = []
    for t, ref in enumerate(arrays):
        for h in range(stack_ref.shape[0]):
            target = ref.at[:, pl.ds(h * HEAD, HEAD)]
            copies.append(pltpu.make_async_copy(stack_ref.at[h, t], target, sems.at[len(copies)]))
            copies[-1].start()
    slots = loss_s.shape[1]
    turned_s[...] = losses_ref[...].T
    loss_s[...] = turned_s[pl.ds(pl.multiple_of(facts_ref[0] * slots, 8), slots)].T
    copies.append(pltpu.make_async_copy(loss_s, loss_ref, sems.at[len(copies)]))
    copies[-1].start()
    for copy in copies:
        copy.wait()


def turn_kernel(up_ref, down_ref, up_out, down_out):
    up_out[...] = up_ref[...].T
    down_out[...] = down_ref[...].T


GELU_A = 0.7978845608028654
GELU_B = 0.044715


def byte_kernel(
    pieces,
    facts_ref,
    rows_ref,
    ids_ref,
    order_ref,
    embed_ref,
    gain_ref,
    up_ref,
    down_ref,
    up_turned_ref,
    down_turned_ref,
    vocab_ref,
    grad_ref,
    loss_ref,
    bend_s,
):
    heads, count, _ = rows_ref.shape
    size = up_ref.shape[1] // pieces
    place = facts_ref[0]
    ids = ids_ref[...].T
    lane = lax.broadcasted_iota(jnp.int32, ids.shape, 1)
    target = jnp.sum(jnp.where(lane == place, ids, 0), axis=1, keepdims=True)
    previous = jnp.sum(jnp.where(lane == place - 1, ids, 0), axis=1, keepdims=True)
    letters = lax.broadcasted_iota(jnp.int32, (count, vocab_ref.shape[1]), 1)
    live = jnp.where(place > 0, 1.0, 0.0)
    one_hot = jnp.where(previous == letters, live, 0.0).astype(BF16)
    hidden_in = jnp.concatenate([rows_ref[h].astype(F32) for h in range(heads)], 1)
    hidden_in = hidden_in + dot(one_hot, embed_ref[...])
    inverse_rms = lax.rsqrt(jnp.mean(hidden_in * hidden_in, axis=1, keepdims=True) + EPSILON)
    gain = gain_ref[...]
    normed = (hidden_in * inverse_rms * gain).astype(BF16)
    after = hidden_in
    ahead = dot(normed, up_ref[:, :size])
    for i in range(pieces):
        part = pl.ds(i * size, size)
        raised = ahead
        if i + 1 < pieces:
            ahead = dot(normed, up_ref[:, pl.ds((i + 1) * size, size)])
        square = raised * raised
        half = 0.5 + 0.5 * jnp.tanh(raised * (GELU_A + (GELU_A * GELU_B) * square))
        active = (raised * half).astype(BF16)
        bend_s[:, part] = half + half * (1.0 - half) * raised * (
            2.0 * GELU_A + (6.0 * GELU_A * GELU_B) * square
        )
        after = after + dot(active, down_ref[part])
    final_scale = lax.rsqrt(jnp.mean(after * after, axis=1, keepdims=True) + EPSILON)
    final_rows = (after * final_scale).astype(BF16)
    logits = dot(final_rows, vocab_ref[...])
    row_top = jnp.max(logits, axis=1, keepdims=True)
    raised_mass = jnp.exp(logits - row_top)
    mass = jnp.sum(raised_mass, axis=1, keepdims=True)
    is_target = target == letters
    chosen = jnp.sum(jnp.where(is_target, logits, 0.0), axis=1, keepdims=True)
    loss = jnp.log(mass) + row_top - chosen
    row_at = lax.broadcasted_iota(jnp.int32, (count, count), 0)
    ordered = jnp.sum(jnp.where(row_at == order_ref[...] - facts_ref[1], loss, 0.0), axis=0, keepdims=True)
    slot = lax.broadcasted_iota(jnp.int32, loss_ref.shape, 0)
    loss_ref[...] = jnp.where(slot == place, ordered, 0.0)
    logit_grad = raised_mass / mass - jnp.where(is_target, 1.0, 0.0)
    final_grad = dot(logit_grad.astype(BF16), vocab_ref[...], NT).astype(BF16).astype(F32)
    mean_dot = jnp.mean(final_grad * after, axis=1, keepdims=True)
    after_grad = final_scale * final_grad - after * (final_scale * final_scale * final_scale * mean_dot)
    narrow = after_grad.astype(BF16)
    normed_grad = None
    ahead = dot(narrow, down_turned_ref[:, :size])
    for i in range(pieces):
        part = pl.ds(i * size, size)
        active_grad = ahead.astype(BF16).astype(F32)
        if i + 1 < pieces:
            ahead = dot(narrow, down_turned_ref[:, pl.ds((i + 1) * size, size)])
        raised_grad = (active_grad * bend_s[:, part]).astype(BF16)
        term = dot(raised_grad, up_turned_ref[part])
        normed_grad = term if normed_grad is None else normed_grad + term
    scaled = normed_grad.astype(BF16).astype(F32) * gain
    mean_dot = jnp.mean(scaled * hidden_in, axis=1, keepdims=True)
    total = (
        after_grad
        + inverse_rms * scaled
        - hidden_in * (inverse_rms * inverse_rms * inverse_rms * mean_dot)
    ).astype(BF16)
    for h in range(heads):
        grad_ref[h] = total[:, h * HEAD : (h + 1) * HEAD]


def vmem():
    return pl.BlockSpec(memory_space=pltpu.VMEM)


def far():
    return pl.BlockSpec(memory_space=pltpu.HBM)


def smem():
    return pl.BlockSpec(memory_space=pltpu.SMEM)


def held(dims, kind=BF16):
    return pltpu.VMEM(dims, kind)


def shape(dims, kind=BF16):
    return jax.ShapeDtypeStruct(dims, kind)


def exchange(value):
    return lax.all_to_all(value, CHIPS, split_axis=0, concat_axis=0, tiled=True)


def gather_losses(value, bit):
    return value + lax.ppermute(value, "grp", [(i, i ^ (1 << bit)) for i in range(PATCH)])


def swap_cores(value):
    return lax.ppermute(value, "seq_2", [(0, 1), (1, 0)])


def anywhere():
    return pl.BlockSpec(memory_space=pl.ANY)


def kernel_call(body, name, outs, ins, out_specs, scratch, grant, flops, transcendentals=0, moved=4 * MIB):
    return pl.pallas_call(
        body,
        out_shape=outs,
        in_specs=ins,
        out_specs=out_specs,
        scratch_shapes=scratch,
        compiler_params=pltpu.CompilerParams(vmem_limit_bytes=grant * MIB),
        cost_estimate=pl.CostEstimate(
            flops=flops, bytes_accessed=moved, transcendentals=transcendentals
        ),
        name=name,
    )


def shards(
    byte_ids,
    patch_order,
    query_rows,
    key_rows,
    value_rows,
    byte_embed,
    norm_gain,
    w_up,
    w_down,
    vocab_head,
):
    count, columns = query_rows.shape
    hidden = w_up.shape[1]
    heads = columns // HEAD
    rows = heads * count
    chunks = rows // WIDE
    seq_here = lax.axis_index(SEQ)
    place = lax.axis_index("grp").astype(jnp.int32)
    core = lax.axis_index("seq_2").astype(jnp.int32)
    facts = jnp.stack([place, seq_here * count, core])
    query_rows, facts = lax.optimization_barrier((query_rows, facts))
    near_plan, near_rows = own_plan(rows)
    far_plan, far_rows = other_plan(rows, count)

    query_rows, key_rows, value_rows = (
        pltpu.with_memory_space_constraint(a, pltpu.HBM) for a in (query_rows, key_rows, value_rows)
    )
    stacked = kernel_call(
        pack_kernel,
        "pack",
        shape((heads, 3, count, HEAD)),
        [far()] * 3,
        anywhere(),
        [
            pltpu.VMEM((3, count, columns), BF16),
            pltpu.SemaphoreType.DMA((3,)),
            pltpu.SemaphoreType.DMA((3 * heads,)),
        ],
        4,
        0,
    )(query_rows, key_rows, value_rows)
    own = exchange(stacked)

    size = 512
    w_up = pltpu.with_memory_space_constraint(w_up, pltpu.HBM)
    w_down = pltpu.with_memory_space_constraint(w_down, pltpu.HBM)
    wide_block = pl.BlockSpec((columns, size), lambda i: (0, i))
    tall_block = pl.BlockSpec((size, columns), lambda i: (i, 0))
    turned = pl.pallas_call(
        turn_kernel,
        out_shape=(pltpu.HBM((hidden, columns), BF16), pltpu.HBM((columns, hidden), BF16)),
        grid=(hidden // size,),
        in_specs=[wide_block, tall_block],
        out_specs=(tall_block, wide_block),
        compiler_params=pltpu.CompilerParams(vmem_limit_bytes=12 * MIB),
        cost_estimate=pl.CostEstimate(flops=0, bytes_accessed=32 * MIB, transcendentals=0),
        name="turn_weights",
    )(w_up, w_down)
    own, turned = lax.optimization_barrier((own, turned))
    other = swap_cores(own[:, 1:])

    kv_scratch = [pltpu.VMEM((rows, HEAD), BF16), pltpu.VMEM((HEAD, rows), BF16)]
    near_kept, near_mixed, stats, up_held = kernel_call(
        functools.partial(forward_own, near_plan),
        "forward_own",
        (
            held((near_rows, WIDE)),
            held((chunks, HEAD, WIDE), F32),
            held((chunks, 8, WIDE), F32),
            held(w_up.shape),
        ),
        [vmem(), far()],
        (vmem(),) * 4,
        kv_scratch + [pltpu.VMEM((2, rows, WIDE), F32), pltpu.SemaphoreType.DMA],
        8,
        4 * near_rows * WIDE * HEAD,
        near_rows * WIDE,
    )(own, w_up)
    far_kept, attended, near_inverse, far_inverse, down_held = kernel_call(
        functools.partial(forward_other, far_plan),
        "forward_other",
        (
            held((far_rows, WIDE)),
            held((rows, HEAD)),
            held((rows, HEAD), F32),
            held((rows, HEAD), F32),
            held(w_down.shape),
        ),
        [smem()] + [vmem()] * 4 + [far()],
        (vmem(),) * 5,
        kv_scratch + [pltpu.VMEM((2, rows, WIDE), F32), pltpu.SemaphoreType.DMA],
        8,
        4 * far_rows * WIDE * HEAD,
        far_rows * WIDE,
    )(facts, own, other, near_mixed, stats, w_down)

    byte_pieces = 4
    owned_rows = exchange(attended.reshape(heads, count, HEAD))
    context_grad, losses = kernel_call(
        functools.partial(byte_kernel, byte_pieces),
        "byte_layer",
        (shape((heads, count, HEAD)), shape((PATCH, count), F32)),
        [smem()] + [vmem()] * 10,
        (vmem(), vmem()),
        [pltpu.VMEM((count, hidden), F32)],
        14,
        8 * count * columns * hidden,
        count * hidden,
    )(
        facts,
        owned_rows,
        byte_ids.T,
        patch_order[None],
        byte_embed,
        norm_gain[None],
        up_held,
        down_held,
        *turned,
        vocab_head,
    )

    grad_rows = exchange(context_grad).reshape(rows, HEAD)
    side_scratch = kv_scratch + [pltpu.VMEM((2, rows, WIDE), BF16)]
    sums = [pltpu.VMEM((rows, HEAD), F32)] * 2
    pair_grad, turned_grad = kernel_call(
        functools.partial(backward_other, far_plan),
        "backward_other",
        (shape((heads, 2, count, HEAD)), shape((chunks, HEAD, WIDE), F32)),
        [vmem()] * 6,
        (vmem(), vmem()),
        sums + side_scratch,
        8,
        8 * far_rows * WIDE * HEAD,
    )(own, other, attended, far_inverse, far_kept, grad_rows)
    pair_sent = swap_cores(pair_grad)
    query_grad, key_grad, value_grad = kernel_call(
        functools.partial(backward_own, near_plan),
        "backward_own",
        (shape((rows, HEAD)), shape((rows, HEAD), F32), shape((rows, HEAD), F32)),
        [vmem()] * 6,
        (vmem(), vmem(), vmem()),
        side_scratch,
        8,
        8 * near_rows * WIDE * HEAD,
    )(own, attended, near_inverse, near_kept, grad_rows, turned_grad)
    joined = kernel_call(
        join_kernel,
        "join",
        shape((heads, 3, count, HEAD)),
        [vmem()] * 4,
        vmem(),
        [],
        4,
        0,
    )(query_grad, key_grad, value_grad, pair_sent)
    joined, losses = lax.optimization_barrier((joined, losses))
    back = exchange(joined)
    for bit in (1, 2, 0):
        losses = gather_losses(losses, bit)
    query_out, key_out, value_out, byte_loss = kernel_call(
        unpack_kernel,
        "unpack",
        (shape((count, columns)),) * 3 + (shape((PATCH, count // PATCH), F32),),
        [smem(), anywhere(), vmem()],
        (anywhere(),) * 4,
        [
            pltpu.VMEM((count, PATCH), F32),
            pltpu.VMEM((PATCH, count // PATCH), F32),
            pltpu.SemaphoreType.DMA((3 * heads + 1,)),
        ],
        2,
        0,
    )(facts, back, losses)
    return byte_loss.T, query_out, key_out, value_out


def solution(mesh):
    torus = Mesh(
        mesh.devices.reshape(4, 2, 2, mesh.shape["grp"]), ("seq_0", "seq_1", "seq_2", "grp")
    )
    placed = (
        P(SEQ, None),
        P(SEQ),
        P(SEQ, "grp"),
        P(SEQ, "grp"),
        P(SEQ, "grp"),
        P(),
        P(),
        P(),
        P(),
        P(),
    )
    return jax.shard_map(
        shards,
        mesh=torus,
        in_specs=placed,
        out_specs=(P(SEQ_GRP, None), P(SEQ, "grp"), P(SEQ, "grp"), P(SEQ, "grp")),
        check_vma=False,
    )
```

```python
import functools

import jax
import jax.numpy as jnp
from jax import lax
from jax.experimental import pallas as pl
from jax.experimental.pallas import tpu as pltpu
from jax.sharding import Mesh
from jax.sharding import PartitionSpec as P

HEAD = 128
PATCH = 8
SEQ = ("seq_0", "seq_1", "seq_2")
SEQ_GRP = ("seq_0", "seq_1", "seq_2", "grp")
CHIPS = ("seq_0", "seq_1")

EPSILON = 1e-05
FLOOR = -1e30
SCALE = HEAD ** (-0.5)
LOG2E = 1.4426950408889634
MIB = 2**20

BF16 = jnp.bfloat16
F32 = jnp.float32

NT = (((1,), (1,)), ((), ()))
NN = (((1,), (0,)), ((), ()))


def dot(a, b, dims=NN):
    return lax.dot_general(a, b, dims, preferred_element_type=F32)


WIDE = 256
COVER = 32


def own_plan(rows):
    plan = []
    base = 0
    for first in range(0, rows, WIDE):
        pieces = [(at, WIDE, "causal" if at == first else "all") for at in range(0, first + WIDE, WIDE)]
        plan.append((first, base, first + WIDE, pieces))
        base += first + WIDE
    return plan, base


def other_plan(rows, block):
    plan = []
    base = 0
    for first in range(0, rows, WIDE):
        lowest, highest = first // block, (first + WIDE - 1) // block
        keys = min(rows, 2 * block * ((highest + 2) // 2))
        pieces = []
        for at in range(0, keys, block):
            part = at // block
            kind = "all" if part < lowest else "block" if part <= highest else "none"
            pieces.append((at, block, kind))
        plan.append((first, base, keys, pieces))
        base += keys
    return plan, base


def flat_rows(ref, at, target):
    block = ref.shape[2]
    for j in range(ref.shape[0]):
        target[pl.ds(j * block, block)] = ref[j, at]


def turned_rows(ref, at, target):
    block = ref.shape[2]
    for j in range(0, ref.shape[0], 2):
        two = jnp.concatenate([ref[j, at], ref[j + 1, at]], 0)
        target[:, pl.ds(j * block, 2 * block)] = two.T


def query_chunk(ref, first):
    block = ref.shape[2]
    found = []
    at = first
    while at < first + WIDE:
        stop = min(first + WIDE, (at // block + 1) * block)
        found.append(ref[at // block, 0, pl.ds(at % block, stop - at)])
        at = stop
    return jnp.concatenate(found, 0)


def piece_scores(queries, first, pieces, key_s, score_s, core):
    top = None
    turned = queries.T
    for at, size, kind in pieces:
        if kind == "none":
            continue
        score = dot(key_s[pl.ds(at, size)], turned)
        if kind == "causal":
            key_at = lax.broadcasted_iota(jnp.int32, score.shape, 0)
            query_at = lax.broadcasted_iota(jnp.int32, score.shape, 1)
            score = jnp.where(key_at <= query_at, score, FLOOR)
        elif kind == "block":
            row = first + lax.broadcasted_iota(jnp.int32, (1, WIDE), 1)
            shown = row >= size * (at // size + 1 - core)
            score = jnp.where(shown, score, FLOOR)
        score_s[pl.ds(at, size)] = score
        piece_top = jnp.max(score, axis=0, keepdims=True)
        top = piece_top if top is None else jnp.maximum(top, piece_top)
    return top


def piece_chances(shift, base, pieces, score_s, kept_ref):
    total = jnp.zeros((1, WIDE), F32)
    for at, size, kind in pieces:
        kept = pl.ds(base + at, size)
        if kind == "none":
            kept_ref[kept] = jnp.zeros((size, WIDE), BF16)
            continue
        chance = jnp.exp2(score_s[pl.ds(at, size)] * (SCALE * LOG2E) - shift)
        total = total + jnp.sum(chance, axis=0, keepdims=True)
        kept_ref[kept] = chance.astype(BF16)
    return total


def staggered(count, start, middle, end):
    start(0)
    for i in range(count):
        if i + 1 < count:
            start(i + 1)
        if i > 0:
            end(i - 1)
        middle(i)
    end(count - 1)


def forward_own(plan, own_ref, kept_ref, mixed_ref, stats_ref, key_s, turned_s, score_s):
    flat_rows(own_ref, 1, key_s)
    turned_rows(own_ref, 2, turned_s)
    tops = {}

    def start(i):
        first, _, _, pieces = plan[i]
        tops[i] = piece_scores(query_chunk(own_ref, first), first, pieces, key_s, score_s.at[i % 2], None)

    def middle(i):
        _, base, _, pieces = plan[i]
        shift = tops[i] * (SCALE * LOG2E)
        stats_ref[i, 0:1] = shift
        stats_ref[i, 1:2] = piece_chances(shift, base, pieces, score_s.at[i % 2], kept_ref)

    def end(i):
        _, base, keys, _ = plan[i]
        mixed_ref[i] = dot(turned_s[:, :keys], kept_ref[pl.ds(base, keys)])

    staggered(len(plan), start, middle, end)


def forward_other(
    plan,
    facts_ref,
    own_ref,
    other_ref,
    mixed_ref,
    stats_ref,
    kept_ref,
    out_ref,
    own_inverse_ref,
    inverse_ref,
    key_s,
    turned_s,
    score_s,
):
    flat_rows(other_ref, 0, key_s)
    turned_rows(other_ref, 1, turned_s)
    core = facts_ref[2]
    tops = {}
    parts = {}

    def start(i):
        first, _, _, pieces = plan[i]
        tops[i] = piece_scores(query_chunk(own_ref, first), first, pieces, key_s, score_s.at[i % 2], core)

    def middle(i):
        _, base, _, pieces = plan[i]
        own_shift = stats_ref[i, 0:1]
        shift = jnp.maximum(tops[i] * (SCALE * LOG2E), own_shift)
        total = piece_chances(shift, base, pieces, score_s.at[i % 2], kept_ref)
        own_part = jnp.exp2(own_shift - shift)
        parts[i] = own_part, 1.0 / (total + own_part * stats_ref[i, 1:2])

    def end(i):
        first, base, keys, _ = plan[i]
        own_part, inverse = parts[i]
        mixed = mixed_ref[i] * own_part + dot(turned_s[:, :keys], kept_ref[pl.ds(base, keys)])
        rows = pl.ds(first, WIDE)
        out_ref[rows] = (mixed * inverse).T.astype(BF16)
        inverse_ref[rows] = jnp.broadcast_to(inverse, (HEAD, WIDE)).T
        own_inverse_ref[rows] = jnp.broadcast_to(own_part * inverse, (HEAD, WIDE)).T

    staggered(len(plan), start, middle, end)


def backward_side(
    plan, key_at, own_ref, side_ref, mixed_ref, inverse_ref, kept_ref, grad_ref, key_sum, value_sum, value_s, turned_s,
    slope_s,
):
    flat_rows(side_ref, key_at + 1, value_s)
    turned_rows(side_ref, key_at, turned_s)
    tasks = []
    for i, (first, base, keys, pieces) in enumerate(plan):
        rows = pl.ds(first, WIDE)
        grads = (grad_ref[rows].astype(F32) * inverse_ref[rows]).astype(BF16)
        product = grads.astype(F32) * mixed_ref[rows].astype(F32)
        row_dot = jnp.sum(product.T, axis=0, keepdims=True)
        queries = query_chunk(own_ref, first)
        live = [piece for piece in pieces if piece[2] != "none"]
        for at, size, _ in live:
            tasks.append((i, at, size, at == live[-1][0], queries, grads, row_dot))

    def chance_grad(task):
        _, at, size, _, _, grads, _ = task
        return dot(value_s[pl.ds(at, size)], grads, NT)

    reached = 0
    ahead = chance_grad(tasks[0])
    for k, (i, at, size, last, queries, grads, row_dot) in enumerate(tasks):
        here = ahead
        if k + 1 < len(tasks):
            ahead = chance_grad(tasks[k + 1])
        _, base, keys, _ = plan[i]
        spot = pl.ds(at, size)
        kept = kept_ref[pl.ds(base + at, size)]
        slope = (kept.astype(F32) * (here - row_dot)).astype(BF16)
        slope_s[i % 2, spot] = slope
        value_part = dot(kept, grads)
        key_part = dot(slope, queries)
        if at >= reached:
            reached = at + size
            value_sum[spot] = value_part
            key_sum[spot] = key_part
        else:
            value_sum[spot] += value_part
            key_sum[spot] += key_part
        if last:
            for unseen, size, kind in plan[i][3]:
                if kind == "none":
                    slope_s[i % 2, pl.ds(unseen, size)] = jnp.zeros((size, WIDE), BF16)
            yield i, dot(turned_s[:, :keys], slope_s[i % 2, pl.ds(0, keys)])


def backward_other(
    plan, own_ref, other_ref, mixed_ref, inverse_ref, kept_ref, grad_ref, pair_ref, query_ref, key_sum, value_sum,
    value_s, turned_s, slope_s,
):
    for i, turned in backward_side(
        plan, 0, own_ref, other_ref, mixed_ref, inverse_ref, kept_ref, grad_ref, key_sum, value_sum, value_s, turned_s,
        slope_s,
    ):
        query_ref[i] = turned
    parts, _, block, _ = other_ref.shape
    for j in range(parts):
        rows = pl.ds(j * block, block)
        pair_ref[j, 0] = (key_sum[rows] * SCALE).astype(BF16)
        pair_ref[j, 1] = value_sum[rows].astype(BF16)


def backward_own(
    plan, own_ref, mixed_ref, inverse_ref, kept_ref, grad_ref, turned_ref, query_ref, key_ref, value_ref, value_s,
    turned_s, slope_s,
):
    for i, turned in backward_side(
        plan, 1, own_ref, own_ref, mixed_ref, inverse_ref, kept_ref, grad_ref, key_ref, value_ref, value_s, turned_s,
        slope_s,
    ):
        first = plan[i][0]
        query_ref[pl.ds(first, WIDE)] = ((turned + turned_ref[i]) * SCALE).T.astype(BF16)


def join_kernel(query_ref, key_ref, value_ref, pair_ref, out_ref, pair_s, sems):
    parts, _, block, _ = out_ref.shape
    copies = []
    for j in range(parts):
        source = query_ref.at[pl.ds(j * block, block)]
        copies.append(pltpu.make_async_copy(source, out_ref.at[j, 0], sems.at[len(copies)]))
        copies[-1].start()
    for j in range(parts):
        rows = pl.ds(j * block, block)
        pair_s[j, 0] = (key_ref[rows] * SCALE + pair_ref[j, 0].astype(F32)).astype(BF16)
        pair_s[j, 1] = (value_ref[rows] + pair_ref[j, 1].astype(F32)).astype(BF16)
        target = out_ref.at[j, pl.ds(1, 2)]
        copies.append(pltpu.make_async_copy(pair_s.at[j], target, sems.at[len(copies)]))
        copies[-1].start()
    for copy in copies:
        copy.wait()


def pack_kernel(*refs):
    arrays, out_ref, held_ref, in_sems, out_sems = refs[:-4], refs[-4], refs[-3], refs[-2], refs[-1]
    heads = out_ref.shape[0]
    loads = [pltpu.make_async_copy(ref, held_ref.at[t], in_sems.at[t]) for t, ref in enumerate(arrays)]
    for load in loads:
        load.start()
    stores = []
    for t, load in enumerate(loads):
        load.wait()
        for h in range(heads):
            source = held_ref.at[t, :, pl.ds(h * HEAD, HEAD)]
            stores.append(pltpu.make_async_copy(source, out_ref.at[h, t], out_sems.at[len(stores)]))
            stores[-1].start()
    for store in stores:
        store.wait()


def unpack_kernel(facts_ref, stack_ref, losses_ref, *refs):
    arrays, loss_ref, turned_s, loss_s, sems = refs[:-4], refs[-4], refs[-3], refs[-2], refs[-1]
    slots = loss_s.shape[1]
    turned_s[...] = losses_ref[...].T
    loss_s[...] = turned_s[pl.ds(pl.multiple_of(facts_ref[0] * slots, 8), slots)].T
    copies = [pltpu.make_async_copy(loss_s, loss_ref, sems.at[0])]
    for t, ref in enumerate(arrays):
        for h in range(stack_ref.shape[0]):
            target = ref.at[:, pl.ds(h * HEAD, HEAD)]
            copies.append(pltpu.make_async_copy(stack_ref.at[h, t], target, sems.at[len(copies)]))
    for copy in copies:
        copy.start()
    for copy in copies:
        copy.wait()


def turn_kernel(up_ref, down_ref, up_out, down_out):
    up_out[...] = up_ref[...].T
    down_out[...] = down_ref[...].T


GELU_A = 0.7978845608028654
GELU_B = 0.044715


def byte_kernel(
    pieces,
    facts_ref,
    rows_ref,
    ids_ref,
    order_ref,
    embed_ref,
    gain_ref,
    up_ref,
    down_ref,
    up_turned_ref,
    down_turned_ref,
    vocab_ref,
    grad_ref,
    loss_ref,
    bend_s,
):
    heads, count, _ = rows_ref.shape
    size = up_ref.shape[1] // pieces
    place = facts_ref[0]
    ids = ids_ref[...].T
    lane = lax.broadcasted_iota(jnp.int32, ids.shape, 1)
    target = jnp.sum(jnp.where(lane == place, ids, 0), axis=1, keepdims=True)
    previous = jnp.sum(jnp.where(lane == place - 1, ids, 0), axis=1, keepdims=True)
    letters = lax.broadcasted_iota(jnp.int32, (count, vocab_ref.shape[1]), 1)
    live = jnp.where(place > 0, 1.0, 0.0)
    one_hot = jnp.where(previous == letters, live, 0.0).astype(BF16)
    hidden_in = jnp.concatenate([rows_ref[h].astype(F32) for h in range(heads)], 1)
    hidden_in = hidden_in + dot(one_hot, embed_ref[...])
    inverse_rms = lax.rsqrt(jnp.mean(hidden_in * hidden_in, axis=1, keepdims=True) + EPSILON)
    gain = gain_ref[...]
    normed = (hidden_in * inverse_rms * gain).astype(BF16)
    after = hidden_in
    ahead = dot(normed, up_ref[:, :size])
    for i in range(pieces):
        part = pl.ds(i * size, size)
        raised = ahead
        if i + 1 < pieces:
            ahead = dot(normed, up_ref[:, pl.ds((i + 1) * size, size)])
        square = raised * raised
        half = 0.5 + 0.5 * jnp.tanh(raised * (GELU_A + (GELU_A * GELU_B) * square))
        active = (raised * half).astype(BF16)
        bend_s[:, part] = half + half * (1.0 - half) * raised * (
            2.0 * GELU_A + (6.0 * GELU_A * GELU_B) * square
        )
        after = after + dot(active, down_ref[part])
    final_scale = lax.rsqrt(jnp.mean(after * after, axis=1, keepdims=True) + EPSILON)
    final_rows = (after * final_scale).astype(BF16)
    logits = dot(final_rows, vocab_ref[...])
    row_top = jnp.max(logits, axis=1, keepdims=True)
    raised_mass = jnp.exp(logits - row_top)
    mass = jnp.sum(raised_mass, axis=1, keepdims=True)
    is_target = target == letters
    chosen = jnp.sum(jnp.where(is_target, logits, 0.0), axis=1, keepdims=True)
    loss = jnp.log(mass) + row_top - chosen
    row_at = lax.broadcasted_iota(jnp.int32, (count, count), 0)
    ordered = jnp.sum(jnp.where(row_at == order_ref[...] - facts_ref[1], loss, 0.0), axis=0, keepdims=True)
    slot = lax.broadcasted_iota(jnp.int32, loss_ref.shape, 0)
    loss_ref[...] = jnp.where(slot == place, ordered, 0.0)
    logit_grad = raised_mass / mass - jnp.where(is_target, 1.0, 0.0)
    final_grad = dot(logit_grad.astype(BF16), vocab_ref[...], NT).astype(BF16).astype(F32)
    mean_dot = jnp.mean(final_grad * after, axis=1, keepdims=True)
    after_grad = final_scale * final_grad - after * (final_scale * final_scale * final_scale * mean_dot)
    narrow = after_grad.astype(BF16)
    normed_grad = None
    ahead = dot(narrow, down_turned_ref[:, :size])
    for i in range(pieces):
        part = pl.ds(i * size, size)
        active_grad = ahead.astype(BF16).astype(F32)
        if i + 1 < pieces:
            ahead = dot(narrow, down_turned_ref[:, pl.ds((i + 1) * size, size)])
        raised_grad = (active_grad * bend_s[:, part]).astype(BF16)
        term = dot(raised_grad, up_turned_ref[part])
        normed_grad = term if normed_grad is None else normed_grad + term
    scaled = normed_grad.astype(BF16).astype(F32) * gain
    mean_dot = jnp.mean(scaled * hidden_in, axis=1, keepdims=True)
    total = (
        after_grad
        + inverse_rms * scaled
        - hidden_in * (inverse_rms * inverse_rms * inverse_rms * mean_dot)
    ).astype(BF16)
    for h in range(heads):
        grad_ref[h] = total[:, h * HEAD : (h + 1) * HEAD]


def vmem():
    return pl.BlockSpec(memory_space=pltpu.VMEM)


def far():
    return pl.BlockSpec(memory_space=pltpu.HBM)


def smem():
    return pl.BlockSpec(memory_space=pltpu.SMEM)


def held(dims, kind=BF16):
    return pltpu.VMEM(dims, kind)


def shape(dims, kind=BF16):
    return jax.ShapeDtypeStruct(dims, kind)


def exchange(value):
    return lax.all_to_all(value, CHIPS, split_axis=0, concat_axis=0, tiled=True)


def gather_losses(value, bit):
    return value + lax.ppermute(value, "grp", [(i, i ^ (1 << bit)) for i in range(PATCH)])


def swap_cores(value):
    return lax.ppermute(value, "seq_2", [(0, 1), (1, 0)])


def anywhere():
    return pl.BlockSpec(memory_space=pl.ANY)


def kernel_call(body, name, outs, ins, out_specs, scratch, grant, flops, transcendentals=0, moved=4 * MIB):
    return pl.pallas_call(
        body,
        out_shape=outs,
        in_specs=ins,
        out_specs=out_specs,
        scratch_shapes=scratch,
        compiler_params=pltpu.CompilerParams(vmem_limit_bytes=grant * MIB),
        cost_estimate=pl.CostEstimate(
            flops=flops, bytes_accessed=moved, transcendentals=transcendentals
        ),
        name=name,
    )


def shards(
    byte_ids,
    patch_order,
    query_rows,
    key_rows,
    value_rows,
    byte_embed,
    norm_gain,
    w_up,
    w_down,
    vocab_head,
):
    count, columns = query_rows.shape
    hidden = w_up.shape[1]
    heads = columns // HEAD
    rows = heads * count
    chunks = rows // WIDE
    seq_here = lax.axis_index(SEQ)
    place = lax.axis_index("grp").astype(jnp.int32)
    core = lax.axis_index("seq_2").astype(jnp.int32)
    facts = jnp.stack([place, seq_here * count, core])
    query_rows, facts = lax.optimization_barrier((query_rows, facts))
    near_plan, near_rows = own_plan(rows)
    far_plan, far_rows = other_plan(rows, count)

    query_rows, key_rows, value_rows = (
        pltpu.with_memory_space_constraint(a, pltpu.HBM) for a in (query_rows, key_rows, value_rows)
    )
    stacked = kernel_call(
        pack_kernel,
        "pack",
        shape((heads, 3, count, HEAD)),
        [far()] * 3,
        anywhere(),
        [
            pltpu.VMEM((3, count, columns), BF16),
            pltpu.SemaphoreType.DMA((3,)),
            pltpu.SemaphoreType.DMA((3 * heads,)),
        ],
        4,
        0,
    )(query_rows, key_rows, value_rows)
    own = exchange(stacked)

    size = 512
    w_up_free, w_down_free = w_up, w_down
    w_up = pltpu.with_memory_space_constraint(w_up, pltpu.HBM)
    w_down = pltpu.with_memory_space_constraint(w_down, pltpu.HBM)
    wide_block = pl.BlockSpec((columns, size), lambda i: (0, i))
    tall_block = pl.BlockSpec((size, columns), lambda i: (i, 0))
    turned = pl.pallas_call(
        turn_kernel,
        out_shape=(pltpu.HBM((hidden, columns), BF16), pltpu.HBM((columns, hidden), BF16)),
        grid=(hidden // size,),
        in_specs=[wide_block, tall_block],
        out_specs=(tall_block, wide_block),
        compiler_params=pltpu.CompilerParams(vmem_limit_bytes=12 * MIB),
        cost_estimate=pl.CostEstimate(flops=0, bytes_accessed=32 * MIB, transcendentals=0),
        name="turn_weights",
    )(w_up, w_down)
    own, turned = lax.optimization_barrier((own, turned))
    other = swap_cores(own[:, 1:])

    kv_scratch = [pltpu.VMEM((rows, HEAD), BF16), pltpu.VMEM((HEAD, rows), BF16)]
    near_kept, near_mixed, stats = kernel_call(
        functools.partial(forward_own, near_plan),
        "forward_own",
        (
            held((near_rows, WIDE)),
            held((chunks, HEAD, WIDE), F32),
            held((chunks, 8, WIDE), F32),
        ),
        [vmem()],
        (vmem(),) * 3,
        kv_scratch + [pltpu.VMEM((2, rows, WIDE), F32)],
        8,
        COVER * 4 * near_rows * WIDE * HEAD,
        near_rows * WIDE,
    )(own)
    far_kept, attended, near_inverse, far_inverse = kernel_call(
        functools.partial(forward_other, far_plan),
        "forward_other",
        (
            held((far_rows, WIDE)),
            held((rows, HEAD)),
            held((rows, HEAD), F32),
            held((rows, HEAD), F32),
        ),
        [smem()] + [vmem()] * 4,
        (vmem(),) * 4,
        kv_scratch + [pltpu.VMEM((2, rows, WIDE), F32)],
        8,
        COVER * 4 * far_rows * WIDE * HEAD,
        far_rows * WIDE,
    )(facts, own, other, near_mixed, stats)

    byte_pieces = 2
    owned_rows = exchange(attended.reshape(heads, count, HEAD))
    context_grad, losses = kernel_call(
        functools.partial(byte_kernel, byte_pieces),
        "byte_layer",
        (shape((heads, count, HEAD)), shape((PATCH, count), F32)),
        [smem()] + [vmem()] * 10,
        (vmem(), vmem()),
        [pltpu.VMEM((count, hidden), F32)],
        14,
        8 * count * columns * hidden,
        count * hidden,
    )(
        facts,
        owned_rows,
        byte_ids.T,
        patch_order[None],
        byte_embed,
        norm_gain[None],
        w_up_free,
        w_down_free,
        *turned,
        vocab_head,
    )

    grad_rows = exchange(context_grad).reshape(rows, HEAD)
    side_scratch = kv_scratch + [pltpu.VMEM((2, rows, WIDE), BF16)]
    sums = [pltpu.VMEM((rows, HEAD), F32)] * 2
    pair_grad, turned_grad = kernel_call(
        functools.partial(backward_other, far_plan),
        "backward_other",
        (shape((heads, 2, count, HEAD)), shape((chunks, HEAD, WIDE), F32)),
        [vmem()] * 6,
        (vmem(), vmem()),
        sums + side_scratch,
        8,
        8 * far_rows * WIDE * HEAD,
    )(own, other, attended, far_inverse, far_kept, grad_rows)
    pair_sent = swap_cores(pair_grad)
    query_grad, key_grad, value_grad = kernel_call(
        functools.partial(backward_own, near_plan),
        "backward_own",
        (shape((rows, HEAD)), shape((rows, HEAD), F32), shape((rows, HEAD), F32)),
        [vmem()] * 6,
        (vmem(), vmem(), vmem()),
        side_scratch,
        8,
        8 * near_rows * WIDE * HEAD,
    )(own, attended, near_inverse, near_kept, grad_rows, turned_grad)
    joined = kernel_call(
        join_kernel,
        "join",
        shape((heads, 3, count, HEAD)),
        [vmem()] * 4,
        anywhere(),
        [pltpu.VMEM((heads, 2, count, HEAD), BF16), pltpu.SemaphoreType.DMA((2 * heads,))],
        4,
        0,
    )(query_grad, key_grad, value_grad, pair_sent)
    joined, losses = lax.optimization_barrier((joined, losses))
    back = exchange(joined)
    for bit in (1, 2, 0):
        losses = gather_losses(losses, bit)
    query_out, key_out, value_out, byte_loss = kernel_call(
        unpack_kernel,
        "unpack",
        (shape((count, columns)),) * 3 + (shape((PATCH, count // PATCH), F32),),
        [smem(), anywhere(), vmem()],
        (anywhere(),) * 4,
        [
            pltpu.VMEM((count, PATCH), F32),
            pltpu.VMEM((PATCH, count // PATCH), F32),
            pltpu.SemaphoreType.DMA((3 * heads + 1,)),
        ],
        2,
        0,
    )(facts, back, losses)
    return byte_loss.T, query_out, key_out, value_out


def solution(mesh):
    torus = Mesh(
        mesh.devices.reshape(4, 2, 2, mesh.shape["grp"]), ("seq_0", "seq_1", "seq_2", "grp")
    )
    placed = (
        P(SEQ, None),
        P(SEQ),
        P(SEQ, "grp"),
        P(SEQ, "grp"),
        P(SEQ, "grp"),
        P(),
        P(),
        P(),
        P(),
        P(),
    )
    return jax.shard_map(
        shards,
        mesh=torus,
        in_specs=placed,
        out_specs=(P(SEQ_GRP, None), P(SEQ, "grp"), P(SEQ, "grp"), P(SEQ, "grp")),
        check_vma=False,
    )
```

```python
import functools

import jax
import jax.numpy as jnp
from jax import lax
from jax.experimental import pallas as pl
from jax.experimental.pallas import tpu as pltpu
from jax.sharding import Mesh
from jax.sharding import PartitionSpec as P

HEAD = 128
PATCH = 8
SEQ = ("seq_0", "seq_1", "seq_2")
SEQ_GRP = ("seq_0", "seq_1", "seq_2", "grp")
CHIPS = ("seq_0", "seq_1")

EPSILON = 1e-05
FLOOR = -1e30
SCALE = HEAD ** (-0.5)
LOG2E = 1.4426950408889634
MIB = 2**20

BF16 = jnp.bfloat16
F32 = jnp.float32

NT = (((1,), (1,)), ((), ()))
NN = (((1,), (0,)), ((), ()))


def dot(a, b, dims=NN):
    return lax.dot_general(a, b, dims, preferred_element_type=F32)


WIDE = 256
COVER = 32


def own_plan(rows):
    plan = []
    base = 0
    for first in range(0, rows, WIDE):
        pieces = [(at, WIDE, "causal" if at == first else "all") for at in range(0, first + WIDE, WIDE)]
        plan.append((first, base, first + WIDE, pieces))
        base += first + WIDE
    return plan, base


def other_plan(rows, block):
    plan = []
    base = 0
    for first in range(0, rows, WIDE):
        lowest, highest = first // block, (first + WIDE - 1) // block
        keys = min(rows, 2 * block * ((highest + 2) // 2))
        pieces = []
        for at in range(0, keys, block):
            part = at // block
            kind = "all" if part < lowest else "block" if part <= highest else "none"
            if kind == "all" and part % 2 and pieces[-1][2] == "all":
                pieces[-1] = (at - block, 2 * block, kind)
            else:
                pieces.append((at, block, kind))
        plan.append((first, base, keys, pieces))
        base += keys
    return plan, base


def flat_rows(ref, at, target):
    block = ref.shape[2]
    for j in range(ref.shape[0]):
        target[pl.ds(j * block, block)] = ref[j, at]


def turned_rows(ref, at, target):
    block = ref.shape[2]
    for j in range(0, ref.shape[0], 2):
        two = jnp.concatenate([ref[j, at], ref[j + 1, at]], 0)
        target[:, pl.ds(j * block, 2 * block)] = two.T


def query_chunk(ref, first):
    block = ref.shape[2]
    found = []
    at = first
    while at < first + WIDE:
        stop = min(first + WIDE, (at // block + 1) * block)
        found.append(ref[at // block, 0, pl.ds(at % block, stop - at)])
        at = stop
    return jnp.concatenate(found, 0)


def piece_scores(queries, first, pieces, key_s, score_s, core):
    top = None
    turned = queries.T
    for at, size, kind in pieces:
        if kind == "none":
            continue
        score = dot(key_s[pl.ds(at, size)], turned)
        if kind == "causal":
            key_at = lax.broadcasted_iota(jnp.int32, score.shape, 0)
            query_at = lax.broadcasted_iota(jnp.int32, score.shape, 1)
            score = jnp.where(key_at <= query_at, score, FLOOR)
        elif kind == "block":
            row = first + lax.broadcasted_iota(jnp.int32, (1, WIDE), 1)
            shown = row >= size * (at // size + 1 - core)
            score = jnp.where(shown, score, FLOOR)
        score_s[pl.ds(at, size)] = score
        piece_top = jnp.max(score, axis=0, keepdims=True)
        top = piece_top if top is None else jnp.maximum(top, piece_top)
    return top


def piece_chances(shift, base, pieces, score_s, kept_ref):
    total = jnp.zeros((1, WIDE), F32)
    for at, size, kind in pieces:
        kept = pl.ds(base + at, size)
        if kind == "none":
            kept_ref[kept] = jnp.zeros((size, WIDE), BF16)
            continue
        chance = jnp.exp2(score_s[pl.ds(at, size)] * (SCALE * LOG2E) - shift)
        total = total + jnp.sum(chance, axis=0, keepdims=True)
        kept_ref[kept] = chance.astype(BF16)
    return total


def staggered(count, start, middle, end):
    start(0)
    for i in range(count):
        if i + 1 < count:
            start(i + 1)
        if i > 0:
            end(i - 1)
        middle(i)
    end(count - 1)


def forward_own(plan, own_ref, kept_ref, mixed_ref, stats_ref, key_s, turned_s, score_s):
    flat_rows(own_ref, 1, key_s)
    turned_rows(own_ref, 2, turned_s)
    tops = {}

    def start(i):
        first, _, _, pieces = plan[i]
        tops[i] = piece_scores(query_chunk(own_ref, first), first, pieces, key_s, score_s.at[i % 2], None)

    def middle(i):
        _, base, _, pieces = plan[i]
        shift = tops[i] * (SCALE * LOG2E)
        stats_ref[i, 0:1] = shift
        stats_ref[i, 1:2] = piece_chances(shift, base, pieces, score_s.at[i % 2], kept_ref)

    def end(i):
        _, base, keys, _ = plan[i]
        mixed_ref[i] = dot(turned_s[:, :keys], kept_ref[pl.ds(base, keys)])

    staggered(len(plan), start, middle, end)


def forward_other(
    plan,
    facts_ref,
    own_ref,
    other_ref,
    mixed_ref,
    stats_ref,
    kept_ref,
    out_ref,
    own_inverse_ref,
    inverse_ref,
    key_s,
    turned_s,
    score_s,
):
    flat_rows(other_ref, 0, key_s)
    turned_rows(other_ref, 1, turned_s)
    core = facts_ref[2]
    tops = {}
    parts = {}

    def start(i):
        first, _, _, pieces = plan[i]
        tops[i] = piece_scores(query_chunk(own_ref, first), first, pieces, key_s, score_s.at[i % 2], core)

    def middle(i):
        _, base, _, pieces = plan[i]
        own_shift = stats_ref[i, 0:1]
        shift = jnp.maximum(tops[i] * (SCALE * LOG2E), own_shift)
        total = piece_chances(shift, base, pieces, score_s.at[i % 2], kept_ref)
        own_part = jnp.exp2(own_shift - shift)
        parts[i] = own_part, 1.0 / (total + own_part * stats_ref[i, 1:2])

    def end(i):
        first, base, keys, _ = plan[i]
        own_part, inverse = parts[i]
        mixed = mixed_ref[i] * own_part + dot(turned_s[:, :keys], kept_ref[pl.ds(base, keys)])
        rows = pl.ds(first, WIDE)
        out_ref[rows] = (mixed * inverse).T.astype(BF16)
        inverse_ref[rows] = jnp.broadcast_to(inverse, (HEAD, WIDE)).T
        own_inverse_ref[rows] = jnp.broadcast_to(own_part * inverse, (HEAD, WIDE)).T

    staggered(len(plan), start, middle, end)


def backward_side(
    plan, key_at, own_ref, side_ref, mixed_ref, inverse_ref, kept_ref, grad_ref, key_sum, value_sum, value_s, turned_s,
    slope_s,
):
    flat_rows(side_ref, key_at + 1, value_s)
    turned_rows(side_ref, key_at, turned_s)
    tasks = []
    for i, (first, base, keys, pieces) in enumerate(plan):
        rows = pl.ds(first, WIDE)
        grads = (grad_ref[rows].astype(F32) * inverse_ref[rows]).astype(BF16)
        product = grads.astype(F32) * mixed_ref[rows].astype(F32)
        row_dot = jnp.sum(product.T, axis=0, keepdims=True)
        queries = query_chunk(own_ref, first)
        live = [piece for piece in pieces if piece[2] != "none"]
        for at, size, _ in live:
            tasks.append((i, at, size, at == live[-1][0], queries, grads, row_dot))

    def chance_grad(task):
        _, at, size, _, _, grads, _ = task
        return dot(value_s[pl.ds(at, size)], grads, NT)

    reached = 0
    ahead = chance_grad(tasks[0])
    for k, (i, at, size, last, queries, grads, row_dot) in enumerate(tasks):
        here = ahead
        if k + 1 < len(tasks):
            ahead = chance_grad(tasks[k + 1])
        _, base, keys, _ = plan[i]
        spot = pl.ds(at, size)
        kept = kept_ref[pl.ds(base + at, size)]
        slope = (kept.astype(F32) * (here - row_dot)).astype(BF16)
        slope_s[i % 2, spot] = slope
        value_part = dot(kept, grads)
        key_part = dot(slope, queries)
        if at >= reached:
            reached = at + size
            value_sum[spot] = value_part
            key_sum[spot] = key_part
        else:
            value_sum[spot] += value_part
            key_sum[spot] += key_part
        if last:
            for unseen, size, kind in plan[i][3]:
                if kind == "none":
                    slope_s[i % 2, pl.ds(unseen, size)] = jnp.zeros((size, WIDE), BF16)
            yield i, dot(turned_s[:, :keys], slope_s[i % 2, pl.ds(0, keys)])


def backward_other(
    plan, own_ref, other_ref, mixed_ref, inverse_ref, kept_ref, grad_ref, pair_ref, query_ref, key_sum, value_sum,
    value_s, turned_s, slope_s,
):
    for i, turned in backward_side(
        plan, 0, own_ref, other_ref, mixed_ref, inverse_ref, kept_ref, grad_ref, key_sum, value_sum, value_s, turned_s,
        slope_s,
    ):
        query_ref[i] = turned
    parts, _, block, _ = other_ref.shape
    for j in range(parts):
        rows = pl.ds(j * block, block)
        pair_ref[j, 0] = (key_sum[rows] * SCALE).astype(BF16)
        pair_ref[j, 1] = value_sum[rows].astype(BF16)


def backward_own(
    plan, own_ref, mixed_ref, inverse_ref, kept_ref, grad_ref, turned_ref, query_ref, key_ref, value_ref, value_s,
    turned_s, slope_s,
):
    for i, turned in backward_side(
        plan, 1, own_ref, own_ref, mixed_ref, inverse_ref, kept_ref, grad_ref, key_ref, value_ref, value_s, turned_s,
        slope_s,
    ):
        first = plan[i][0]
        query_ref[pl.ds(first, WIDE)] = ((turned + turned_ref[i]) * SCALE).T.astype(BF16)


def join_kernel(query_ref, key_ref, value_ref, pair_ref, out_ref):
    parts, _, block, _ = out_ref.shape
    for j in range(parts):
        rows = pl.ds(j * block, block)
        out_ref[j, 0] = query_ref[rows]
        out_ref[j, 1] = (key_ref[rows] * SCALE + pair_ref[j, 0].astype(F32)).astype(BF16)
        out_ref[j, 2] = (value_ref[rows] + pair_ref[j, 1].astype(F32)).astype(BF16)


def pack_kernel(*refs):
    arrays, out_ref, held_ref, in_sems, out_sems = refs[:-4], refs[-4], refs[-3], refs[-2], refs[-1]
    heads = out_ref.shape[0]
    loads = [pltpu.make_async_copy(ref, held_ref.at[t], in_sems.at[t]) for t, ref in enumerate(arrays)]
    for load in loads:
        load.start()
    stores = []
    for t, load in enumerate(loads):
        load.wait()
        for h in range(heads):
            source = held_ref.at[t, :, pl.ds(h * HEAD, HEAD)]
            stores.append(pltpu.make_async_copy(source, out_ref.at[h, t], out_sems.at[len(stores)]))
            stores[-1].start()
    for store in stores:
        store.wait()


def unpack_kernel(facts_ref, stack_ref, losses_ref, *refs):
    arrays, loss_ref, turned_s, loss_s, sems = refs[:-4], refs[-4], refs[-3], refs[-2], refs[-1]
    copies = []
    for t, ref in enumerate(arrays):
        for h in range(stack_ref.shape[0]):
            target = ref.at[:, pl.ds(h * HEAD, HEAD)]
            copies.append(pltpu.make_async_copy(stack_ref.at[h, t], target, sems.at[len(copies)]))
            copies[-1].start()
    slots = loss_s.shape[1]
    turned_s[...] = losses_ref[...].T
    loss_s[...] = turned_s[pl.ds(pl.multiple_of(facts_ref[0] * slots, 8), slots)].T
    copies.append(pltpu.make_async_copy(loss_s, loss_ref, sems.at[len(copies)]))
    copies[-1].start()
    for copy in copies:
        copy.wait()


def turn_kernel(up_ref, down_ref, up_out, down_out):
    up_out[...] = up_ref[...].T
    down_out[...] = down_ref[...].T


GELU_A = 0.7978845608028654
GELU_B = 0.044715


def byte_kernel(
    pieces,
    facts_ref,
    rows_ref,
    ids_ref,
    order_ref,
    embed_ref,
    gain_ref,
    up_ref,
    down_ref,
    up_turned_ref,
    down_turned_ref,
    vocab_ref,
    grad_ref,
    loss_ref,
    bend_s,
):
    heads, count, _ = rows_ref.shape
    size = up_ref.shape[1] // pieces
    place = facts_ref[0]
    ids = ids_ref[...].T
    lane = lax.broadcasted_iota(jnp.int32, ids.shape, 1)
    target = jnp.sum(jnp.where(lane == place, ids, 0), axis=1, keepdims=True)
    previous = jnp.sum(jnp.where(lane == place - 1, ids, 0), axis=1, keepdims=True)
    letters = lax.broadcasted_iota(jnp.int32, (count, vocab_ref.shape[1]), 1)
    live = jnp.where(place > 0, 1.0, 0.0)
    one_hot = jnp.where(previous == letters, live, 0.0).astype(BF16)
    hidden_in = jnp.concatenate([rows_ref[h].astype(F32) for h in range(heads)], 1)
    hidden_in = hidden_in + dot(one_hot, embed_ref[...])
    inverse_rms = lax.rsqrt(jnp.mean(hidden_in * hidden_in, axis=1, keepdims=True) + EPSILON)
    gain = gain_ref[...]
    normed = (hidden_in * inverse_rms * gain).astype(BF16)
    after = hidden_in
    ahead = dot(normed, up_ref[:, :size])
    for i in range(pieces):
        part = pl.ds(i * size, size)
        raised = ahead
        if i + 1 < pieces:
            ahead = dot(normed, up_ref[:, pl.ds((i + 1) * size, size)])
        square = raised * raised
        half = 0.5 + 0.5 * jnp.tanh(raised * (GELU_A + (GELU_A * GELU_B) * square))
        active = (raised * half).astype(BF16)
        bend_s[:, part] = half + half * (1.0 - half) * raised * (
            2.0 * GELU_A + (6.0 * GELU_A * GELU_B) * square
        )
        after = after + dot(active, down_ref[part])
    final_scale = lax.rsqrt(jnp.mean(after * after, axis=1, keepdims=True) + EPSILON)
    final_rows = (after * final_scale).astype(BF16)
    logits = dot(final_rows, vocab_ref[...])
    row_top = jnp.max(logits, axis=1, keepdims=True)
    raised_mass = jnp.exp(logits - row_top)
    mass = jnp.sum(raised_mass, axis=1, keepdims=True)
    is_target = target == letters
    chosen = jnp.sum(jnp.where(is_target, logits, 0.0), axis=1, keepdims=True)
    loss = jnp.log(mass) + row_top - chosen
    row_at = lax.broadcasted_iota(jnp.int32, (count, count), 0)
    ordered = jnp.sum(jnp.where(row_at == order_ref[...] - facts_ref[1], loss, 0.0), axis=0, keepdims=True)
    slot = lax.broadcasted_iota(jnp.int32, loss_ref.shape, 0)
    loss_ref[...] = jnp.where(slot == place, ordered, 0.0)
    logit_grad = raised_mass / mass - jnp.where(is_target, 1.0, 0.0)
    final_grad = dot(logit_grad.astype(BF16), vocab_ref[...], NT).astype(BF16).astype(F32)
    mean_dot = jnp.mean(final_grad * after, axis=1, keepdims=True)
    after_grad = final_scale * final_grad - after * (final_scale * final_scale * final_scale * mean_dot)
    narrow = after_grad.astype(BF16)
    normed_grad = None
    ahead = dot(narrow, down_turned_ref[:, :size])
    for i in range(pieces):
        part = pl.ds(i * size, size)
        active_grad = ahead.astype(BF16).astype(F32)
        if i + 1 < pieces:
            ahead = dot(narrow, down_turned_ref[:, pl.ds((i + 1) * size, size)])
        raised_grad = (active_grad * bend_s[:, part]).astype(BF16)
        term = dot(raised_grad, up_turned_ref[part])
        normed_grad = term if normed_grad is None else normed_grad + term
    scaled = normed_grad.astype(BF16).astype(F32) * gain
    mean_dot = jnp.mean(scaled * hidden_in, axis=1, keepdims=True)
    total = (
        after_grad
        + inverse_rms * scaled
        - hidden_in * (inverse_rms * inverse_rms * inverse_rms * mean_dot)
    ).astype(BF16)
    for h in range(heads):
        grad_ref[h] = total[:, h * HEAD : (h + 1) * HEAD]


def vmem():
    return pl.BlockSpec(memory_space=pltpu.VMEM)


def far():
    return pl.BlockSpec(memory_space=pltpu.HBM)


def smem():
    return pl.BlockSpec(memory_space=pltpu.SMEM)


def held(dims, kind=BF16):
    return pltpu.VMEM(dims, kind)


def shape(dims, kind=BF16):
    return jax.ShapeDtypeStruct(dims, kind)


def exchange(value):
    return lax.all_to_all(value, CHIPS, split_axis=0, concat_axis=0, tiled=True)


def gather_losses(value, bit):
    return value + lax.ppermute(value, "grp", [(i, i ^ (1 << bit)) for i in range(PATCH)])


def swap_cores(value):
    return lax.ppermute(value, "seq_2", [(0, 1), (1, 0)])


def anywhere():
    return pl.BlockSpec(memory_space=pl.ANY)


def kernel_call(body, name, outs, ins, out_specs, scratch, grant, flops, transcendentals=0, moved=4 * MIB):
    return pl.pallas_call(
        body,
        out_shape=outs,
        in_specs=ins,
        out_specs=out_specs,
        scratch_shapes=scratch,
        compiler_params=pltpu.CompilerParams(vmem_limit_bytes=grant * MIB),
        cost_estimate=pl.CostEstimate(
            flops=flops, bytes_accessed=moved, transcendentals=transcendentals
        ),
        name=name,
    )


def shards(
    byte_ids,
    patch_order,
    query_rows,
    key_rows,
    value_rows,
    byte_embed,
    norm_gain,
    w_up,
    w_down,
    vocab_head,
):
    count, columns = query_rows.shape
    hidden = w_up.shape[1]
    heads = columns // HEAD
    rows = heads * count
    chunks = rows // WIDE
    seq_here = lax.axis_index(SEQ)
    place = lax.axis_index("grp").astype(jnp.int32)
    core = lax.axis_index("seq_2").astype(jnp.int32)
    facts = jnp.stack([place, seq_here * count, core])
    query_rows, facts = lax.optimization_barrier((query_rows, facts))
    near_plan, near_rows = own_plan(rows)
    far_plan, far_rows = other_plan(rows, count)

    query_rows, key_rows, value_rows = (
        pltpu.with_memory_space_constraint(a, pltpu.HBM) for a in (query_rows, key_rows, value_rows)
    )
    stacked = kernel_call(
        pack_kernel,
        "pack",
        shape((heads, 3, count, HEAD)),
        [far()] * 3,
        anywhere(),
        [
            pltpu.VMEM((3, count, columns), BF16),
            pltpu.SemaphoreType.DMA((3,)),
            pltpu.SemaphoreType.DMA((3 * heads,)),
        ],
        4,
        0,
    )(query_rows, key_rows, value_rows)
    own = exchange(stacked)

    size = 512
    w_up_free, w_down_free = w_up, w_down
    w_up = pltpu.with_memory_space_constraint(w_up, pltpu.HBM)
    w_down = pltpu.with_memory_space_constraint(w_down, pltpu.HBM)
    wide_block = pl.BlockSpec((columns, size), lambda i: (0, i))
    tall_block = pl.BlockSpec((size, columns), lambda i: (i, 0))
    turned = pl.pallas_call(
        turn_kernel,
        out_shape=(pltpu.HBM((hidden, columns), BF16), pltpu.HBM((columns, hidden), BF16)),
        grid=(hidden // size,),
        in_specs=[wide_block, tall_block],
        out_specs=(tall_block, wide_block),
        compiler_params=pltpu.CompilerParams(vmem_limit_bytes=12 * MIB),
        cost_estimate=pl.CostEstimate(flops=0, bytes_accessed=32 * MIB, transcendentals=0),
        name="turn_weights",
    )(w_up, w_down)
    own, turned = lax.optimization_barrier((own, turned))
    other = swap_cores(own[:, 1:])

    kv_scratch = [pltpu.VMEM((rows, HEAD), BF16), pltpu.VMEM((HEAD, rows), BF16)]
    near_kept, near_mixed, stats = kernel_call(
        functools.partial(forward_own, near_plan),
        "forward_own",
        (
            held((near_rows, WIDE)),
            held((chunks, HEAD, WIDE), F32),
            held((chunks, 8, WIDE), F32),
        ),
        [vmem()],
        (vmem(),) * 3,
        kv_scratch + [pltpu.VMEM((2, rows, WIDE), F32)],
        8,
        COVER * 4 * near_rows * WIDE * HEAD,
        near_rows * WIDE,
    )(own)
    far_kept, attended, near_inverse, far_inverse = kernel_call(
        functools.partial(forward_other, far_plan),
        "forward_other",
        (
            held((far_rows, WIDE)),
            held((rows, HEAD)),
            held((rows, HEAD), F32),
            held((rows, HEAD), F32),
        ),
        [smem()] + [vmem()] * 4,
        (vmem(),) * 4,
        kv_scratch + [pltpu.VMEM((2, rows, WIDE), F32)],
        8,
        COVER * 4 * far_rows * WIDE * HEAD,
        far_rows * WIDE,
    )(facts, own, other, near_mixed, stats)

    byte_pieces = 4
    owned_rows = exchange(attended.reshape(heads, count, HEAD))
    context_grad, losses = kernel_call(
        functools.partial(byte_kernel, byte_pieces),
        "byte_layer",
        (shape((heads, count, HEAD)), shape((PATCH, count), F32)),
        [smem()] + [vmem()] * 10,
        (vmem(), vmem()),
        [pltpu.VMEM((count, hidden), F32)],
        14,
        8 * count * columns * hidden,
        count * hidden,
    )(
        facts,
        owned_rows,
        byte_ids.T,
        patch_order[None],
        byte_embed,
        norm_gain[None],
        w_up_free,
        w_down_free,
        *turned,
        vocab_head,
    )

    grad_rows = exchange(context_grad).reshape(rows, HEAD)
    side_scratch = kv_scratch + [pltpu.VMEM((2, rows, WIDE), BF16)]
    sums = [pltpu.VMEM((rows, HEAD), F32)] * 2
    pair_grad, turned_grad = kernel_call(
        functools.partial(backward_other, far_plan),
        "backward_other",
        (shape((heads, 2, count, HEAD)), shape((chunks, HEAD, WIDE), F32)),
        [vmem()] * 6,
        (vmem(), vmem()),
        sums + side_scratch,
        8,
        8 * far_rows * WIDE * HEAD,
    )(own, other, attended, far_inverse, far_kept, grad_rows)
    pair_sent = swap_cores(pair_grad)
    query_grad, key_grad, value_grad = kernel_call(
        functools.partial(backward_own, near_plan),
        "backward_own",
        (shape((rows, HEAD)), shape((rows, HEAD), F32), shape((rows, HEAD), F32)),
        [vmem()] * 6,
        (vmem(), vmem(), vmem()),
        side_scratch,
        8,
        8 * near_rows * WIDE * HEAD,
    )(own, attended, near_inverse, near_kept, grad_rows, turned_grad)
    joined = kernel_call(
        join_kernel,
        "join",
        shape((heads, 3, count, HEAD)),
        [vmem()] * 4,
        vmem(),
        [],
        4,
        0,
    )(query_grad, key_grad, value_grad, pair_sent)
    joined, losses = lax.optimization_barrier((joined, losses))
    back = exchange(joined)
    for bit in (1, 2, 0):
        losses = gather_losses(losses, bit)
    query_out, key_out, value_out, byte_loss = kernel_call(
        unpack_kernel,
        "unpack",
        (shape((count, columns)),) * 3 + (shape((PATCH, count // PATCH), F32),),
        [smem(), anywhere(), vmem()],
        (anywhere(),) * 4,
        [
            pltpu.VMEM((count, PATCH), F32),
            pltpu.VMEM((PATCH, count // PATCH), F32),
            pltpu.SemaphoreType.DMA((3 * heads + 1,)),
        ],
        2,
        0,
    )(facts, back, losses)
    return byte_loss.T, query_out, key_out, value_out


def solution(mesh):
    torus = Mesh(
        mesh.devices.reshape(4, 2, 2, mesh.shape["grp"]), ("seq_0", "seq_1", "seq_2", "grp")
    )
    placed = (
        P(SEQ, None),
        P(SEQ),
        P(SEQ, "grp"),
        P(SEQ, "grp"),
        P(SEQ, "grp"),
        P(),
        P(),
        P(),
        P(),
        P(),
    )
    return jax.shard_map(
        shards,
        mesh=torus,
        in_specs=placed,
        out_specs=(P(SEQ_GRP, None), P(SEQ, "grp"), P(SEQ, "grp"), P(SEQ, "grp")),
        check_vma=False,
    )
```
